32 devices in a mesh: ctx: 4 (over y, x), fsdp: 8 (over z, core).
Axes of the slice: x: 2, y: 2, z: 4, core: 2. Of those that a mesh axis runs over, the one named last changes fastest.
Arguments:
- tokens: bfloat16 [8, 1024, 2048], P('fsdp', 'ctx'), may hold values from -6 to 6
- dealing: int32 [8, 8], P('fsdp'), may hold values from 0 to 7, as said below
- first_gain: bfloat16 [2048], P('fsdp'), may hold values from 0.5 to 1.5
- query_weight: bfloat16 [2048, 2048], P('fsdp'), may hold values from -0.1875 to 0.1875
- key_weight: bfloat16 [2048, 256], P('fsdp'), may hold values from -0.1875 to 0.1875
- value_weight: bfloat16 [2048, 256], P('fsdp'), may hold values from -0.125 to 0.125
- output_weight: bfloat16 [2048, 2048], P('fsdp'), may hold values from -0.5 to 0.5
- second_gain: bfloat16 [2048], P('fsdp'), may hold values from 0.5 to 1.5
- gate_weight: bfloat16 [2048, 5632], P('fsdp'), may hold values from -0.125 to 0.125
- up_weight: bfloat16 [2048, 5632], P('fsdp'), may hold values from -0.125 to 0.125
- down_weight: bfloat16 [5632, 2048], P('fsdp'), may hold values from -0.15625 to 0.15625
- cotangent: bfloat16 [8, 1024, 2048], P('fsdp', 'ctx'), may hold values from -6 to 6
Outputs:
- block_output: bfloat16 [8, 1024, 2048], P('fsdp', 'ctx')
- input_grad: bfloat16 [8, 1024, 2048], P('fsdp', 'ctx')
- first_gain_grad: float32 [2048], P('fsdp')
- query_grad: float32 [2048, 2048], P('fsdp')
- key_grad: float32 [2048, 256], P('fsdp')
- value_grad: float32 [2048, 256], P('fsdp')
- output_grad: float32 [2048, 2048], P('fsdp')
- second_gain_grad: float32 [2048], P('fsdp')
- gate_grad: float32 [2048, 5632], P('fsdp')
- up_grad: float32 [2048, 5632], P('fsdp')
- down_grad: float32 [5632, 2048], P('fsdp')
The draws below stay inside these ranges and needn't reach their ends.
Inputs may be any that keep to these rules, and one draw needn't show every extreme that they name: In each row of dealing every block number 0 to 7 appears once, and the two slots 2 c and 2 c + 1 of one device c of ctx hold two blocks whose numbers add up to 7.
All inputs are finite; a program needn't handle non-finite values.
Results may differ from the reference program's by a relative error of at most 0.024.
Values may be sent and summed in bfloat16 or wider, within the bound.
A program may use at most 576 MiB of HBM per device.

```python
import math
import jax
import jax.numpy as jnp
from jax import lax

D = 2048
FF = 5632
HEADS = 32
KV_HEADS = 4
HEAD_DIM = 64
TOK_DEV = 256
KV_WIDTH = 256
LEN = 1024
SEQS = 8
N_CTX = 4


def draw_dealing(key, part):
    pair_key, flip_key = jax.random.split(key)
    orders = jax.vmap(lambda one_key: jax.random.permutation(one_key, N_CTX))(jax.random.split(pair_key, SEQS))
    flips = jax.random.randint(flip_key, (SEQS, N_CTX), 0, 2)
    first_block = jnp.where(flips == 1, 2 * N_CTX - 1 - orders, orders)
    second_block = 2 * N_CTX - 1 - first_block
    return jnp.stack([first_block, second_block], axis=-1).reshape(SEQS, 2 * N_CTX).astype(jnp.int32)


def block_levels(own_key, shape, cuts, least, high):
    def one(dim, shards_of):
        draws = jax.random.uniform(jax.random.fold_in(jax.random.fold_in(own_key, 6), dim), (shards_of,), jnp.float32, least / len(cuts), high / len(cuts))
        return jnp.repeat(jnp.exp(draws), shape[dim] // shards_of).reshape((-1,) + (1,) * (len(shape) - dim - 1))

    factor_of = one(*cuts[0])
    for cut in cuts[1:]:
        factor_of = factor_of * one(*cut)
    return factor_of


def noise(own_key, dims, width, limit, shards=(), kind=jnp.bfloat16):
    loudness = block_levels(own_key, dims, shards, -0.22, 0.18) if shards else 1.0
    values = jax.random.normal(own_key, dims, jnp.float32) * width * loudness
    return jnp.minimum(jnp.maximum(values, -limit), limit).astype(kind)


def setup_inputs(seed: int = 0) -> dict:
    keys = jax.random.split(jax.random.key(seed), 13)
    tokens = noise(keys[0], (SEQS, LEN, D), 1.0, 6.0, ((0, 8), (1, 4)))
    dealing = draw_dealing(jax.random.fold_in(keys[12], 71), 0)
    first_gain = jnp.clip(1.0 + 0.1 * jax.random.normal(keys[2], (D,), jnp.float32), 0.5, 1.5).astype(jnp.bfloat16)
    query_weight = noise(keys[3], (D, D), (D // 2) ** -0.5, 0.1875, ((0, 8),))
    key_weight = noise(keys[4], (D, KV_WIDTH), (D // 2) ** -0.5, 0.1875, ((0, 8),))
    value_weight = noise(keys[5], (D, KV_WIDTH), D ** -0.5, 0.125, ((0, 8),))
    output_weight = noise(keys[6], (D, D), (D // 16) ** -0.5, 0.5, ((0, 8),))
    second_gain = jnp.clip(1.0 + 0.1 * jax.random.normal(keys[7], (D,), jnp.float32), 0.5, 1.5).astype(jnp.bfloat16)
    gate_weight = noise(keys[8], (D, FF), D ** -0.5, 0.125, ((0, 8),))
    up_weight = noise(keys[9], (D, FF), D ** -0.5, 0.125, ((0, 8),))
    down_weight = noise(keys[10], (FF, D), (FF // 4) ** -0.5, 0.15625, ((0, 8),))
    cotangent = noise(keys[11], (SEQS, LEN, D), 1.0, 6.0, ((0, 8), (1, 4)))
    return dict(tokens=tokens, dealing=dealing, first_gain=first_gain, query_weight=query_weight, key_weight=key_weight, value_weight=value_weight, output_weight=output_weight, second_gain=second_gain, gate_weight=gate_weight, up_weight=up_weight, down_weight=down_weight, cotangent=cotangent)


highest = lax.Precision.HIGHEST
epsilon = 1e-05

@jax.custom_vjp
def low(v):
    return lax.optimization_barrier(v.astype(jnp.bfloat16)).astype(jnp.float32)

@jax.custom_vjp
def low_back(v):
    return v

def low_keep(v):
    return (low(v), None)

def low_pass(kept, grad):
    return (grad,)

def back_keep(v):
    return (v, None)

def back_low(kept, grad):
    return (low(grad),)
low.defvjp(low_keep, low_pass)
low_back.defvjp(back_keep, back_low)

def rotary_tables(positions):
    frequency = jnp.exp(-math.log(10000.0) * jnp.arange(HEAD_DIM // 2).astype(jnp.float32) * (2.0 / HEAD_DIM))
    angles = positions.astype(jnp.float32)[:, None] * frequency[None, :]
    return (jnp.cos(angles), jnp.sin(angles))

def rotate(matrix, cosine_table, sine_table):
    half_dim = HEAD_DIM // 2
    first_half = matrix[..., :half_dim]
    second_half = matrix[..., half_dim:]
    cosine_wide = cosine_table[:, None, :]
    sine_wide = sine_table[:, None, :]
    return jnp.concatenate([first_half * cosine_wide - second_half * sine_wide, second_half * cosine_wide + first_half * sine_wide], axis=-1)

def rms_norm(values, gain_vector):
    inverse = lax.rsqrt(lax.optimization_barrier(jnp.mean(values * values, axis=-1, keepdims=True)) + epsilon)
    return values * inverse * gain_vector

def sequence_forward(params, inputs, positions):
    first_gain, query_weight, key_weight, value_weight, output_weight, second_gain, gate_weight, up_weight, down_weight = params
    length = inputs.shape[0]
    group_size = HEADS // KV_HEADS
    first_input = low(rms_norm(inputs, first_gain))
    query_rows = low_back(jnp.dot(first_input, query_weight, precision=highest))
    key_rows = low_back(jnp.dot(first_input, key_weight, precision=highest))
    value_rows = low(low_back(jnp.dot(first_input, value_weight, precision=highest)))
    cosine_table, sine_table = rotary_tables(positions)
    query_rows = low(rotate(query_rows.reshape(length, HEADS, HEAD_DIM), cosine_table, sine_table))
    key_rows = low(rotate(key_rows.reshape(length, KV_HEADS, HEAD_DIM), cosine_table, sine_table))
    value_rows = value_rows.reshape(length, KV_HEADS, HEAD_DIM)
    allowed = positions[None, :] <= positions[:, None]

    def attend_group(operands):
        head_queries, head_keys, head_values = operands
        scores = low_back(jnp.einsum('qhd,kd->hqk', head_queries, head_keys, precision=highest)) * (1.0 / math.sqrt(HEAD_DIM))
        scores = jnp.where(allowed[None], scores, -1e+30)
        weights = low(jax.nn.softmax(scores, axis=-1))
        return jnp.einsum('hqk,kd->qhd', weights, head_values, precision=highest)
    grouped = (query_rows.reshape(length, KV_HEADS, group_size, HEAD_DIM).transpose(1, 0, 2, 3), key_rows.transpose(1, 0, 2), value_rows.transpose(1, 0, 2))
    attended = lax.map(jax.checkpoint(attend_group), grouped)
    attended = low(low_back(attended.transpose(1, 0, 2, 3).reshape(length, HEADS * HEAD_DIM)))
    residual_mid = inputs + low_back(jnp.dot(attended, output_weight, precision=highest))
    second_input = low(rms_norm(residual_mid, second_gain))
    gate_act = low_back(jnp.dot(second_input, gate_weight, precision=highest))
    upward = low_back(jnp.dot(second_input, up_weight, precision=highest))
    hidden = low(jax.nn.silu(gate_act) * upward)
    return residual_mid + low_back(jnp.dot(hidden, down_weight, precision=highest))

def forward(inputs_all, params, positions_all):
    checked = jax.checkpoint(sequence_forward)

    def one_sequence(operands):
        return checked(params, operands[0], operands[1])
    return lax.map(one_sequence, (inputs_all, positions_all))

def reference(tokens, dealing, first_gain, query_weight, key_weight, value_weight, output_weight, second_gain, gate_weight, up_weight, down_weight, cotangent):
    block_rows = TOK_DEV // 2
    positions_all = (dealing[:, :, None] * block_rows + jnp.arange(block_rows, dtype=jnp.int32)[None, None, :]).reshape(SEQS, LEN)
    params = (first_gain.astype(jnp.float32), query_weight.astype(jnp.float32), key_weight.astype(jnp.float32), value_weight.astype(jnp.float32), output_weight.astype(jnp.float32), second_gain.astype(jnp.float32), gate_weight.astype(jnp.float32), up_weight.astype(jnp.float32), down_weight.astype(jnp.float32))

    def closed(inputs_all, weights_all):
        return forward(inputs_all, weights_all, positions_all)
    result, pullback = jax.vjp(closed, tokens.astype(jnp.float32), params)
    input_grad, weight_grads = pullback(cotangent.astype(jnp.float32))
    return (result.astype(jnp.bfloat16), input_grad.astype(jnp.bfloat16), weight_grads[0], weight_grads[1], weight_grads[2], weight_grads[3], weight_grads[4], weight_grads[5], weight_grads[6], weight_grads[7], weight_grads[8])
```

```python
import math

import jax
import jax.numpy as jnp
from jax import lax
from jax.sharding import PartitionSpec as P

D = 2048
FF = 5632
HEADS = 32
KV_HEADS = 4
HEAD_DIM = 64
KV_WIDTH = 256


epsilon = 1e-05


def rotary_tables(positions):
    frequency = jnp.exp(
        -math.log(10000.0) * jnp.arange(HEAD_DIM // 2).astype(jnp.float32) * (2.0 / HEAD_DIM)
    )
    angles = positions.astype(jnp.float32)[:, None] * frequency[None, :]
    return (jnp.cos(angles), jnp.sin(angles))


def rotate(matrix, cosine_table, sine_table):
    half_dim = HEAD_DIM // 2
    first_half = matrix[..., :half_dim]
    second_half = matrix[..., half_dim:]
    cosine_wide = cosine_table[:, None, :]
    sine_wide = sine_table[:, None, :]
    return jnp.concatenate(
        [
            first_half * cosine_wide - second_half * sine_wide,
            second_half * cosine_wide + first_half * sine_wide,
        ],
        axis=-1,
    )


def unrotate(matrix, cosine_table, sine_table):
    half_dim = HEAD_DIM // 2
    first_half = matrix[..., :half_dim]
    second_half = matrix[..., half_dim:]
    cosine_wide = cosine_table[:, None, :]
    sine_wide = sine_table[:, None, :]
    return jnp.concatenate(
        [
            first_half * cosine_wide + second_half * sine_wide,
            second_half * cosine_wide - first_half * sine_wide,
        ],
        axis=-1,
    )


def norm_parts(values):
    inverse = lax.rsqrt(jnp.mean(values * values, axis=-1, keepdims=True) + epsilon)
    return (values * inverse, inverse)


def norm_back(gradient, normed, inverse):
    return inverse * (gradient - normed * jnp.mean(gradient * normed, axis=-1, keepdims=True))


def times_transposed(left_side, right_side):
    return lax.dot_general(
        left_side, right_side, (((1,), (1,)), ((), ())), preferred_element_type=jnp.float32
    )


def take_columns(matrix, outer, parts, index):
    rows, columns = matrix.shape
    pieces = matrix.reshape(rows, outer, parts, columns // (outer * parts))
    return lax.dynamic_index_in_dim(pieces, index, axis=2, keepdims=False).reshape(rows, -1)


def take_rows(matrix, parts, index):
    count = matrix.shape[0] // parts
    return lax.dynamic_slice_in_dim(matrix, index * count, count, axis=0)


def put_columns(gathered, outer):
    parts, rows, columns = gathered.shape
    return (
        gathered.reshape(parts, rows, outer, columns // outer)
        .transpose(1, 2, 0, 3)
        .reshape(rows, parts * columns)
    )


def masked_scores(head_queries, head_keys, allowed):
    scores = jnp.einsum(
        "qhd,kd->hqk", head_queries, head_keys, preferred_element_type=jnp.float32
    ) * (1.0 / math.sqrt(HEAD_DIM))
    return jnp.where(allowed[None], scores, -1e30)


def attend_forward(queries, keys, values, allowed):
    outputs = []
    log_totals = []
    group_size = queries.shape[1] // keys.shape[1]
    for group_index in range(keys.shape[1]):
        head_queries = queries[:, group_index * group_size : (group_index + 1) * group_size]
        scores = masked_scores(head_queries, keys[:, group_index], allowed)
        largest = jnp.max(scores, axis=-1, keepdims=True)
        exponent = jnp.exp(scores - largest)
        totals = jnp.sum(exponent, axis=-1, keepdims=True)
        weights = (exponent / totals).astype(jnp.bfloat16)
        outputs.append(
            jnp.einsum(
                "hqk,kd->qhd", weights, values[:, group_index], preferred_element_type=jnp.float32
            )
        )
        log_totals.append(largest + jnp.log(totals))
    return (jnp.concatenate(outputs, axis=1), log_totals)


def attend_backward(queries, keys, values, allowed, log_totals, grad_attended):
    query_parts = []
    key_parts = []
    value_parts = []
    group_size = queries.shape[1] // keys.shape[1]
    for group_index in range(keys.shape[1]):
        head_queries = queries[:, group_index * group_size : (group_index + 1) * group_size]
        head_grads = grad_attended[:, group_index * group_size : (group_index + 1) * group_size]
        head_keys = keys[:, group_index]
        head_values = values[:, group_index]
        scores = masked_scores(head_queries, head_keys, allowed)
        weights = jnp.exp(scores - log_totals[group_index])
        grad_probs = jnp.einsum(
            "qhd,kd->hqk", head_grads, head_values, preferred_element_type=jnp.float32
        )
        row_dots = jnp.sum(weights * grad_probs, axis=-1, keepdims=True)
        grad_scores = (weights * (grad_probs - row_dots) * (1.0 / math.sqrt(HEAD_DIM))).astype(
            jnp.bfloat16
        )
        value_parts.append(
            jnp.einsum(
                "hqk,qhd->kd",
                weights.astype(jnp.bfloat16),
                head_grads,
                preferred_element_type=jnp.float32,
            )
        )
        query_parts.append(
            jnp.einsum("hqk,kd->qhd", grad_scores, head_keys, preferred_element_type=jnp.float32)
        )
        key_parts.append(
            jnp.einsum("hqk,qhd->kd", grad_scores, head_queries, preferred_element_type=jnp.float32)
        )
    return (
        jnp.concatenate(query_parts, axis=1),
        jnp.stack(key_parts, axis=1),
        jnp.stack(value_parts, axis=1),
    )


def column_term(source, gradient):
    return lax.dot_general(
        source, gradient, (((0,), (0,)), ((), ())), preferred_element_type=jnp.float32
    )


def product(left_side, right_side):
    return jnp.dot(left_side, right_side, preferred_element_type=jnp.float32)


def gather_shards(array):
    return lax.all_gather(array, "fsdp", axis=0, tiled=True)


def gather_rows(array):
    return lax.all_gather(array, "ctx", axis=0, tiled=True)


def scatter_rows(array):
    return lax.psum_scatter(
        array.astype(jnp.bfloat16), "ctx", scatter_dimension=0, tiled=True
    ).astype(jnp.float32)


def scatter_shards(array):
    return lax.psum_scatter(
        array.astype(jnp.bfloat16), "fsdp", scatter_dimension=0, tiled=True
    )


def per_device(
    tokens,
    dealing,
    first_gain,
    query_weight,
    key_weight,
    value_weight,
    output_weight,
    second_gain,
    gate_weight,
    up_weight,
    down_weight,
    cotangent,
):
    shard_count = lax.axis_size("fsdp")
    part_count = lax.axis_size("ctx")
    ctx_index = lax.axis_index("ctx")
    shard_index = lax.axis_index("fsdp")
    row_count = tokens.shape[1]
    block_rows = row_count // 2
    seq_rows = row_count * part_count
    own_heads = HEADS // part_count
    dealt_heads = (D // shard_count // part_count) % HEAD_DIM == 0
    offsets = jnp.arange(block_rows, dtype=jnp.int32)
    positions = (dealing[0][:, None] * block_rows + offsets[None, :]).reshape(-1)
    allowed = positions[None, :] <= positions[:, None]
    cosine_table, sine_table = rotary_tables(positions)
    inputs = tokens[0].astype(jnp.float32)

    gain_first = gather_shards(first_gain).astype(jnp.float32)
    gain_second = gather_shards(second_gain).astype(jnp.float32)
    key_value = gather_shards(jnp.concatenate([key_weight, value_weight], axis=1))
    if dealt_heads:
        query_part = gather_shards(take_columns(query_weight, shard_count, part_count, ctx_index))
        output_part = gather_shards(take_rows(output_weight, part_count, ctx_index))
    else:
        query_part = gather_shards(take_columns(query_weight, 1, part_count, ctx_index))
        output_part = take_rows(gather_shards(output_weight), part_count, ctx_index)
    gate_part = gather_shards(take_columns(gate_weight, shard_count, part_count, ctx_index))
    up_part = gather_shards(take_columns(up_weight, shard_count, part_count, ctx_index))
    down_part = gather_shards(take_rows(down_weight, part_count, ctx_index))

    normed_first, inverse_first = norm_parts(inputs)
    first_input = (normed_first * gain_first).astype(jnp.bfloat16)
    first_all = gather_rows(first_input)
    grad_out_all = gather_rows(cotangent[0])
    query_rot = rotate(
        product(first_all, query_part).reshape(seq_rows, own_heads, HEAD_DIM),
        cosine_table,
        sine_table,
    ).astype(jnp.bfloat16)
    key_value_rows = product(first_all, key_value)
    key_rot = rotate(
        key_value_rows[:, :KV_WIDTH].reshape(seq_rows, KV_HEADS, HEAD_DIM), cosine_table, sine_table
    ).astype(jnp.bfloat16)
    value_rows = (
        key_value_rows[:, KV_WIDTH:].astype(jnp.bfloat16).reshape(seq_rows, KV_HEADS, HEAD_DIM)
    )
    if not dealt_heads:
        kv_heads = max(1, KV_HEADS // part_count)
        kv_first = ctx_index * KV_HEADS // part_count
        key_rot = lax.dynamic_slice_in_dim(key_rot, kv_first, kv_heads, 1)
        value_rows = lax.dynamic_slice_in_dim(value_rows, kv_first, kv_heads, 1)
    attended, log_totals = attend_forward(query_rot, key_rot, value_rows, allowed)
    attended = attended.reshape(seq_rows, own_heads * HEAD_DIM).astype(jnp.bfloat16)
    residual_mid = inputs + scatter_rows(product(attended, output_part))

    normed_second, inverse_second = norm_parts(residual_mid)
    second_input = (normed_second * gain_second).astype(jnp.bfloat16)
    second_all = gather_rows(second_input)
    gate_act = product(second_all, gate_part)
    upward = product(second_all, up_part)
    sigmoid_gate = jax.nn.sigmoid(gate_act)
    silu_gate = gate_act * sigmoid_gate
    hidden = (silu_gate * upward).astype(jnp.bfloat16)
    block_output = (residual_mid + scatter_rows(product(hidden, down_part))).astype(jnp.bfloat16)

    grad_hidden = times_transposed(grad_out_all, down_part)
    down_piece = scatter_shards(column_term(hidden, grad_out_all))
    grad_gate = (
        grad_hidden * upward * sigmoid_gate * (1.0 + gate_act * (1.0 - sigmoid_gate))
    ).astype(jnp.bfloat16)
    grad_up = (grad_hidden * silu_gate).astype(jnp.bfloat16)
    grad_second = scatter_rows(
        times_transposed(grad_gate, gate_part) + times_transposed(grad_up, up_part)
    )
    gate_piece = scatter_shards(column_term(second_all, grad_gate))
    up_piece = scatter_shards(column_term(second_all, grad_up))
    second_gain_part = jnp.sum(grad_second * normed_second, axis=0)
    grad_mid = cotangent[0].astype(jnp.float32) + norm_back(
        grad_second * gain_second, normed_second, inverse_second
    )

    branch_all = gather_rows(grad_mid.astype(jnp.bfloat16))
    grad_attended = times_transposed(branch_all, output_part).astype(jnp.bfloat16)
    grad_query_rot, key_terms, value_terms = attend_backward(
        query_rot,
        key_rot,
        value_rows,
        allowed,
        log_totals,
        grad_attended.reshape(seq_rows, own_heads, HEAD_DIM),
    )
    grad_query = (
        unrotate(grad_query_rot, cosine_table, sine_table)
        .reshape(seq_rows, own_heads * HEAD_DIM)
        .astype(jnp.bfloat16)
    )
    grad_key = unrotate(key_terms, cosine_table, sine_table).astype(jnp.bfloat16)
    grad_value = value_terms.astype(jnp.bfloat16)
    if not dealt_heads:
        empty = jnp.zeros((seq_rows, KV_HEADS, HEAD_DIM), jnp.bfloat16)
        grad_key = lax.dynamic_update_slice_in_dim(empty, grad_key, kv_first, 1)
        grad_value = lax.dynamic_update_slice_in_dim(empty, grad_value, kv_first, 1)
    grad_key_value = jnp.concatenate(
        [grad_key.reshape(seq_rows, KV_WIDTH), grad_value.reshape(seq_rows, KV_WIDTH)], axis=1
    )
    grad_first = scatter_rows(
        times_transposed(grad_query, query_part) + times_transposed(grad_key_value, key_value)
    )
    first_gain_part = jnp.sum(grad_first * normed_first, axis=0)
    grad_input = grad_mid + norm_back(grad_first * gain_first, normed_first, inverse_first)

    query_piece = scatter_shards(column_term(first_all, grad_query))
    key_value_piece = scatter_shards(column_term(first_all, grad_key_value))
    output_term = column_term(attended, branch_all)
    if dealt_heads:
        output_shard = gather_rows(scatter_shards(output_term))
    else:
        spread = jnp.zeros((D, D), jnp.float32)
        spread = lax.dynamic_update_slice_in_dim(
            spread, output_term, ctx_index * output_term.shape[0], 0
        )
        output_shard = lax.psum(scatter_shards(spread), "ctx")

    def gather_columns(piece, outer):
        return put_columns(lax.all_gather(piece, "ctx", axis=0), outer).astype(jnp.float32)

    key_value_shard = lax.psum(key_value_piece, "ctx").astype(jnp.float32)
    gain_totals = lax.psum(jnp.stack([first_gain_part, second_gain_part]), ("ctx", "fsdp"))
    gain_rows = D // shard_count
    gain_shard = lax.dynamic_slice_in_dim(gain_totals, shard_index * gain_rows, gain_rows, 1)
    return (
        block_output[None],
        grad_input.astype(jnp.bfloat16)[None],
        gain_shard[0],
        gather_columns(query_piece, shard_count if dealt_heads else 1),
        key_value_shard[:, :KV_WIDTH],
        key_value_shard[:, KV_WIDTH:],
        output_shard.astype(jnp.float32),
        gain_shard[1],
        gather_columns(gate_piece, shard_count),
        gather_columns(up_piece, shard_count),
        gather_rows(down_piece).astype(jnp.float32),
    )


def solution(mesh):
    in_specs = (
        P("fsdp", "ctx", None),
        P("fsdp", None),
        P("fsdp"),
        P("fsdp", None),
        P("fsdp", None),
        P("fsdp", None),
        P("fsdp", None),
        P("fsdp"),
        P("fsdp", None),
        P("fsdp", None),
        P("fsdp", None),
        P("fsdp", "ctx", None),
    )
    out_specs = (
        P("fsdp", "ctx", None),
        P("fsdp", "ctx", None),
        P("fsdp"),
        P("fsdp", None),
        P("fsdp", None),
        P("fsdp", None),
        P("fsdp", None),
        P("fsdp"),
        P("fsdp", None),
        P("fsdp", None),
        P("fsdp", None),
    )
    return jax.shard_map(
        per_device, mesh=mesh, in_specs=in_specs, out_specs=out_specs, check_vma=False
    )
```

```python
import functools
import math

import jax
import jax.numpy as jnp
from jax import lax
from jax.experimental import pallas as pl
from jax.experimental.pallas import tpu as pltpu
from jax.sharding import PartitionSpec as P

D = 2048
FF = 5632
HEADS = 32
KV_HEADS = 4
HEAD_DIM = 64
KV_WIDTH = 256


epsilon = 1e-05


MESH = pl.DeviceIdType.MESH
VMEM = pl.BlockSpec(memory_space=pltpu.VMEM)
SMEM = pl.BlockSpec(memory_space=pltpu.SMEM)
HBM = pl.BlockSpec(memory_space=pl.ANY)
LANES = 128
PAIR = LANES // HEAD_DIM
QUERY_ROWS = 256


def shape(dims, kind=jnp.bfloat16):
    return jax.ShapeDtypeStruct(dims, kind)


def norm_parts(values):
    inverse = lax.rsqrt(jnp.mean(values * values, axis=-1, keepdims=True) + epsilon)
    return (values * inverse, inverse)


def norm_back(gradient, normed, inverse):
    return inverse * (gradient - normed * jnp.mean(gradient * normed, axis=-1, keepdims=True))


def product(left_side, right_side):
    return jnp.dot(left_side, right_side, preferred_element_type=jnp.float32)


def times_transposed(left_side, right_side):
    return lax.dot_general(
        left_side, right_side, (((1,), (1,)), ((), ())), preferred_element_type=jnp.float32
    )


def column_term(source, gradient):
    return lax.dot_general(
        source, gradient, (((0,), (0,)), ((), ())), preferred_element_type=jnp.float32
    )


def meet(count):
    me = lax.axis_index("ctx")
    barrier = pltpu.get_barrier_semaphore()
    for step in range(1, count):
        pl.semaphore_signal(
            barrier, inc=1, device_id={"ctx": lax.rem(me + step, count)}, device_id_type=MESH
        )
    pl.semaphore_wait(barrier, count - 1)


def send_rows(count, piece, source, target, sems):
    local_sem, send_sem, recv_sem = sems
    me = lax.axis_index("ctx")
    copies = []
    for step in range(1, count):
        copies.append(
            pltpu.make_async_remote_copy(
                src_ref=source,
                dst_ref=target,
                send_sem=send_sem.at[step - 1, piece],
                recv_sem=recv_sem.at[step - 1, piece],
                device_id={"ctx": lax.rem(me + step, count)},
                device_id_type=MESH,
            )
        )
    copies.append(pltpu.make_async_copy(source, target, local_sem.at[piece]))
    for copy in copies:
        copy.start()
    return copies


def send_sems(count, pieces):
    return [
        pltpu.SemaphoreType.DMA((pieces,)),
        pltpu.SemaphoreType.DMA((count - 1, pieces)),
        pltpu.SemaphoreType.DMA((count - 1, pieces)),
    ]


def scatter_products(count, pairs, send_buf, recv_buf, total, send_sem, recv_sem):
    me = lax.axis_index("ctx")
    rows, width = total.shape
    tile = 512

    def block(owner, store):
        start = pl.multiple_of(owner * rows, rows)

        def column(index, carry):
            columns = pl.ds(pl.multiple_of(index * tile, tile), tile)
            value = None
            for left, right, transposed in pairs:
                piece = left[pl.ds(start, rows), :]
                if transposed:
                    term = times_transposed(piece, right[columns, :])
                else:
                    term = product(piece, right[:, columns])
                value = term if value is None else value + term
            store(columns, value)
            return carry

        lax.fori_loop(0, width // tile, column, 0)

    copies = []
    for step in range(1, count):
        owner = lax.rem(me + step, count)

        def store_sent(columns, value, step=step):
            send_buf[step - 1, :, columns] = value.astype(send_buf.dtype)

        block(owner, store_sent)
        copy = pltpu.make_async_remote_copy(
            src_ref=send_buf.at[step - 1],
            dst_ref=recv_buf.at[step - 1],
            send_sem=send_sem.at[step - 1],
            recv_sem=recv_sem.at[step - 1],
            device_id={"ctx": owner},
            device_id_type=MESH,
        )
        copy.start()
        copies.append(copy)

    def store_own(columns, value):
        total[:, columns] = value

    block(me, store_own)
    return copies


def scatter_scratch(count, rows, width):
    return [
        pltpu.VMEM((count - 1, rows, width), jnp.bfloat16),
        pltpu.VMEM((count - 1, rows, width), jnp.bfloat16),
        pltpu.VMEM((rows, width), jnp.float32),
        pltpu.SemaphoreType.DMA((count - 1,)),
        pltpu.SemaphoreType.DMA((count - 1,)),
    ]


def received(count, recv_buf, total, rows):
    value = total[rows, :]
    for step in range(count - 1):
        value = value + recv_buf[step, rows, :].astype(jnp.float32)
    return value


STRIP = 32
PIECES = 2


def for_strips(first, rows, body):
    def strip(index, carry):
        body(pl.ds(pl.multiple_of(first + index * STRIP, STRIP), STRIP))
        return carry

    lax.fori_loop(0, rows // STRIP, strip, 0)


def call_plane(body, count, ident, outs, out_specs, in_specs, scratch, cost, megabytes, args):
    return pl.pallas_call(
        functools.partial(body, count),
        out_shape=outs,
        in_specs=in_specs,
        out_specs=out_specs,
        scratch_shapes=scratch,
        compiler_params=pltpu.CompilerParams(
            collective_id=ident, has_side_effects=True, vmem_limit_bytes=megabytes << 20
        ),
        cost_estimate=pl.CostEstimate(flops=cost, bytes_accessed=cost // 300, transcendentals=0),
    )(*args)


def start_body(
    count, tokens, gain, grad_out, first_all, grad_out_all, own, *sems
):
    me = lax.axis_index("ctx")
    rows = tokens.shape[0]
    size = rows // PIECES
    meet(count)
    copies = []
    for piece in range(PIECES):

        def strip(where):
            values = tokens[where, :].astype(jnp.float32)
            normed, _ = norm_parts(values)
            own[where, :] = (normed * gain[...]).astype(jnp.bfloat16)

        for_strips(piece * size, size, strip)
        place = pl.ds(pl.multiple_of(me * rows + piece * size, size), size)
        part = pl.ds(piece * size, size)
        copies += send_rows(count, piece, own.at[part], first_all.at[place], sems)
    for piece in range(PIECES):
        place = pl.ds(pl.multiple_of(me * rows + piece * size, size), size)
        part = pl.ds(piece * size, size)
        copies += send_rows(
            count, PIECES + piece, grad_out.at[part], grad_out_all.at[place], sems
        )
    for copy in copies:
        copy.wait()


def start_gather(count, ident, tokens, gain, grad_out):
    rows, width = tokens.shape
    gathered = shape((count * rows, width))
    return call_plane(
        start_body,
        count,
        ident,
        (gathered, gathered),
        (HBM, HBM),
        [VMEM] * 3,
        [pltpu.VMEM((rows, width), jnp.bfloat16)] + send_sems(count, 2 * PIECES),
        10**11 * 5,
        32,
        (tokens, gain, grad_out),
    )


def middle_body(
    count,
    attended,
    weight,
    tokens,
    gain,
    residual,
    second_all,
    own,
    send_buf,
    recv_buf,
    total,
    send_sem,
    recv_sem,
    *sems,
):
    me = lax.axis_index("ctx")
    rows = tokens.shape[0]
    size = rows // PIECES
    meet(count)
    copies = scatter_products(
        count, [(attended, weight, False)], send_buf, recv_buf, total, send_sem, recv_sem
    )
    for copy in copies:
        copy.wait()
    copies = []
    for piece in range(PIECES):

        def strip(where):
            values = tokens[where, :].astype(jnp.float32) + received(count, recv_buf, total, where)
            residual[where, :] = values
            normed, _ = norm_parts(values)
            own[where, :] = (normed * gain[...]).astype(jnp.bfloat16)

        for_strips(piece * size, size, strip)
        place = pl.ds(pl.multiple_of(me * rows + piece * size, size), size)
        copies += send_rows(
            count, piece, own.at[pl.ds(piece * size, size)], second_all.at[place], sems
        )
    for copy in copies:
        copy.wait()


def middle_gather(count, ident, attended, weight, tokens, gain):
    rows, width = tokens.shape
    return call_plane(
        middle_body,
        count,
        ident,
        (shape((rows, width), jnp.float32), shape((count * rows, width))),
        (VMEM, HBM),
        [VMEM] * 4,
        [pltpu.VMEM((rows, width), jnp.bfloat16)]
        + scatter_scratch(count, rows, width)
        + send_sems(count, PIECES),
        10**11,
        48,
        (attended, weight, tokens, gain),
    )


def output_body(
    count, hidden, weight, residual, output, send_buf, recv_buf, total, send_sem, recv_sem
):
    meet(count)
    copies = scatter_products(
        count, [(hidden, weight, False)], send_buf, recv_buf, total, send_sem, recv_sem
    )
    for copy in copies:
        copy.wait()

    def strip(where):
        values = residual[where, :] + received(count, recv_buf, total, where)
        output[where, :] = values.astype(jnp.bfloat16)

    for_strips(0, output.shape[0], strip)


def output_scatter(count, ident, hidden, weight, residual):
    rows, width = residual.shape
    return call_plane(
        output_body,
        count,
        ident,
        shape((rows, width)),
        VMEM,
        [VMEM] * 3,
        scatter_scratch(count, rows, width),
        10**11,
        48,
        (hidden, weight, residual),
    )


def middle_back_body(
    count,
    grad_gate,
    gate_weight,
    grad_up,
    up_weight,
    residual,
    gain,
    grad_out,
    grad_mid,
    gain_part,
    branch_all,
    own,
    send_buf,
    recv_buf,
    total,
    send_sem,
    recv_sem,
    *sems,
):
    me = lax.axis_index("ctx")
    rows = residual.shape[0]
    size = rows // PIECES
    meet(count)
    copies = scatter_products(
        count,
        [(grad_gate, gate_weight, True), (grad_up, up_weight, True)],
        send_buf,
        recv_buf,
        total,
        send_sem,
        recv_sem,
    )
    gain_part[...] = jnp.zeros_like(gain_part)
    for copy in copies:
        copy.wait()
    copies = []
    for piece in range(PIECES):

        def strip(where):
            gradient = received(count, recv_buf, total, where)
            normed, inverse = norm_parts(residual[where, :])
            gain_part[...] += jnp.sum(gradient * normed, axis=0, keepdims=True)
            values = grad_out[where, :].astype(jnp.float32) + norm_back(
                gradient * gain[...], normed, inverse
            )
            grad_mid[where, :] = values
            own[where, :] = values.astype(jnp.bfloat16)

        for_strips(piece * size, size, strip)
        place = pl.ds(pl.multiple_of(me * rows + piece * size, size), size)
        copies += send_rows(
            count, piece, own.at[pl.ds(piece * size, size)], branch_all.at[place], sems
        )
    for copy in copies:
        copy.wait()


def middle_back(
    count, ident, grad_gate, gate_weight, grad_up, up_weight, residual, gain, grad_out
):
    rows, width = residual.shape
    return call_plane(
        middle_back_body,
        count,
        ident,
        (
            shape((rows, width), jnp.float32),
            shape((1, width), jnp.float32),
            shape((count * rows, width)),
        ),
        (VMEM, VMEM, HBM),
        [VMEM] * 7,
        [pltpu.VMEM((rows, width), jnp.bfloat16)]
        + scatter_scratch(count, rows, width)
        + send_sems(count, PIECES),
        10**11,
        56,
        (grad_gate, gate_weight, grad_up, up_weight, residual, gain, grad_out),
    )


def input_back_body(
    count,
    grad_query,
    query_weight,
    grad_key_value,
    key_value_weight,
    tokens,
    gain,
    grad_mid,
    grad_input,
    gain_part,
    send_buf,
    recv_buf,
    total,
    send_sem,
    recv_sem,
):
    meet(count)
    copies = scatter_products(
        count,
        [(grad_query, query_weight, True), (grad_key_value, key_value_weight, True)],
        send_buf,
        recv_buf,
        total,
        send_sem,
        recv_sem,
    )
    gain_part[...] = jnp.zeros_like(gain_part)
    for copy in copies:
        copy.wait()

    def strip(where):
        gradient = received(count, recv_buf, total, where)
        normed, inverse = norm_parts(tokens[where, :].astype(jnp.float32))
        gain_part[...] += jnp.sum(gradient * normed, axis=0, keepdims=True)
        values = grad_mid[where, :] + norm_back(gradient * gain[...], normed, inverse)
        grad_input[where, :] = values.astype(jnp.bfloat16)

    for_strips(0, grad_input.shape[0], strip)


def input_back(
    count, ident, grad_query, query_weight, grad_key_value, key_value_weight, tokens, gain, grad_mid
):
    rows, width = tokens.shape
    return call_plane(
        input_back_body,
        count,
        ident,
        (shape((rows, width)), shape((1, width), jnp.float32)),
        (VMEM, VMEM),
        [VMEM] * 7,
        scatter_scratch(count, rows, width),
        10**11,
        48,
        (grad_query, query_weight, grad_key_value, key_value_weight, tokens, gain, grad_mid),
    )


def rotary_tables(length):
    frequency = jnp.exp(
        -math.log(10000.0) * jnp.arange(HEAD_DIM // 2).astype(jnp.float32) * (2.0 / HEAD_DIM)
    )
    angles = jnp.arange(length).astype(jnp.float32)[:, None] * frequency[None, :]
    cosine, sine = (jnp.cos(angles), jnp.sin(angles))
    return (
        jnp.concatenate([cosine] * (2 * PAIR), axis=1),
        jnp.concatenate([-sine, sine] * PAIR, axis=1),
    )


def low_lanes(dims, size):
    return lax.rem(lax.broadcasted_iota(jnp.int32, dims, len(dims) - 1), 2 * size) < size


def turn(values, cosine, sine):
    half = HEAD_DIM // 2
    swapped = jnp.where(
        low_lanes(values.shape, half),
        pltpu.roll(values, LANES - half, 1),
        pltpu.roll(values, half, 1),
    )
    return values * cosine + swapped * sine


def two_heads(values):
    low = low_lanes(values.shape, HEAD_DIM)
    zero = jnp.zeros_like(values)
    return jnp.concatenate([jnp.where(low, values, zero), jnp.where(low, zero, values)], axis=0)


def pick_heads(values):
    rows = values.shape[1] // PAIR
    return jnp.concatenate(
        [values[:HEAD_DIM, :rows], values[HEAD_DIM:, rows:]], axis=0
    )


def later_key(dims):
    key = lax.broadcasted_iota(jnp.int32, dims, 0)
    query = lax.rem(lax.broadcasted_iota(jnp.int32, dims, 1), QUERY_ROWS)
    return key > query


def block_rows_at(order, block, rows):
    return pl.ds(pl.multiple_of(order[block] * rows, rows), rows)


def rows_in_order(order, source, index, rows):
    per = QUERY_ROWS // rows
    return jnp.concatenate(
        [source[block_rows_at(order, index * per + i, rows), :] for i in range(per)], axis=0
    )


def attend_body(
    block_rows,
    order,
    first_all,
    query_weight,
    key_value_weight,
    cosine,
    sine,
    attended,
    queries,
    keys,
    values,
    log_totals,
    values_across,
):
    length, width = queries.shape
    kv_heads = keys.shape[0]
    pairs = width // LANES
    blocks = length // QUERY_ROWS

    def project(index, carry):
        place = pl.ds(pl.multiple_of(index * QUERY_ROWS, QUERY_ROWS), QUERY_ROWS)
        rows = rows_in_order(order, first_all, index, block_rows)
        cos_rows, sin_rows = (cosine[place, :], sine[place, :])
        projected = product(rows, query_weight[...])
        for pair in range(pairs):
            lanes = slice(pair * LANES, (pair + 1) * LANES)
            turned = turn(projected[:, lanes], cos_rows, sin_rows).astype(jnp.bfloat16)
            queries[place, lanes] = turned * jnp.asarray(1.0 / math.sqrt(HEAD_DIM), jnp.bfloat16)
        projected = product(rows, key_value_weight[...])
        for head in range(2 * kv_heads):
            tile = projected[:, head // PAIR * LANES : (head // PAIR + 1) * LANES]
            if head < kv_heads:
                tile = turn(tile, cos_rows, sin_rows)
            low = low_lanes(tile.shape, HEAD_DIM)
            moved = pltpu.roll(tile, HEAD_DIM, 1)
            both = jnp.where(low, tile, moved) if head % PAIR == 0 else jnp.where(low, moved, tile)
            if head < kv_heads:
                keys[head, place, :] = both.astype(jnp.bfloat16)
            else:
                values[head - kv_heads, place, :] = both.astype(jnp.bfloat16)
                values_across[head - kv_heads, :, place] = both.T.astype(jnp.bfloat16)
        return carry

    lax.fori_loop(0, blocks, project, 0)

    def attend(pair, carry):
        kv_head = pair // (pairs // kv_heads)
        lanes = pl.ds(pl.multiple_of(pair * LANES, LANES), LANES)
        for index in range(blocks):
            seen = (index + 1) * QUERY_ROWS
            rows = two_heads(queries[index * QUERY_ROWS : seen, lanes])
            scores = times_transposed(keys[kv_head, :seen, :], rows)
            own = scores[seen - QUERY_ROWS :]
            own = jnp.where(later_key(own.shape), -1e30, own)
            if index:
                scores = jnp.concatenate([scores[: seen - QUERY_ROWS], own], axis=0)
            else:
                scores = own
            largest = jnp.max(scores, axis=0, keepdims=True)
            exponent = jnp.exp(scores - largest)
            totals = jnp.sum(exponent, axis=0, keepdims=True)
            mixed = product(values_across[kv_head, :, :seen], exponent.astype(jnp.bfloat16))
            log_totals[pl.ds(pair * blocks + index, 1), :] = largest + jnp.log(totals)
            mixed = pick_heads(mixed / totals).T.astype(jnp.bfloat16)
            per = QUERY_ROWS // block_rows
            for i in range(per):
                attended[block_rows_at(order, index * per + i, block_rows), lanes] = mixed[
                    i * block_rows : (i + 1) * block_rows
                ]
        return carry

    lax.fori_loop(0, pairs, attend, 0)


def attend_forward(block_rows, kv_heads, order, first_all, query_weight, key_value_weight, tables):
    length, _ = first_all.shape
    width = query_weight.shape[1]
    blocks = length // QUERY_ROWS
    wide = shape((kv_heads, length, LANES))
    return pl.pallas_call(
        functools.partial(attend_body, block_rows),
        out_shape=(
            shape((length, width)),
            shape((length, width)),
            wide,
            wide,
            shape((width // LANES * blocks, PAIR * QUERY_ROWS), jnp.float32),
        ),
        in_specs=[SMEM] + [VMEM] * 5,
        out_specs=(VMEM,) * 5,
        scratch_shapes=[pltpu.VMEM((kv_heads, LANES, length), jnp.bfloat16)],
        compiler_params=pltpu.CompilerParams(vmem_limit_bytes=48 << 20),
        cost_estimate=pl.CostEstimate(
            flops=3 * 10**10, bytes_accessed=10**7, transcendentals=10**7
        ),
    )(order, first_all, query_weight, key_value_weight, *tables)


def attend_back_body(
    block_rows,
    order,
    branch_all,
    output_weight,
    queries,
    keys,
    values,
    attended,
    log_totals,
    cosine,
    sine,
    grad_query,
    grad_key_value,
    grads,
    row_dots,
    keys_across,
    key_sums,
    value_sums,
):
    length, width = queries.shape
    kv_heads = keys.shape[0]
    pairs = width // LANES
    blocks = length // QUERY_ROWS
    per = QUERY_ROWS // block_rows

    def project(index, carry):
        place = pl.ds(pl.multiple_of(index * QUERY_ROWS, QUERY_ROWS), QUERY_ROWS)
        rows = rows_in_order(order, branch_all, index, block_rows)
        low = times_transposed(rows, output_weight[...]).astype(jnp.bfloat16)
        grads[place, :] = low
        dots = low.astype(jnp.float32) * rows_in_order(order, attended, index, block_rows).astype(
            jnp.float32
        )
        for pair in range(pairs):
            across = dots[:, pair * LANES : (pair + 1) * LANES].T
            sums = [
                jnp.sum(across[i * HEAD_DIM : (i + 1) * HEAD_DIM], axis=0, keepdims=True)
                for i in range(PAIR)
            ]
            row_dots[pl.ds(pair * blocks + index, 1), :] = jnp.concatenate(sums, axis=1)
        for head in range(kv_heads):
            keys_across[head, :, place] = keys[head, place, :].T
        return carry

    lax.fori_loop(0, blocks, project, 0)

    group = pairs // kv_heads

    def attend(kv_head, carry):
        key_sums[kv_head] = jnp.zeros(key_sums.shape[1:], jnp.float32)
        value_sums[kv_head] = jnp.zeros(value_sums.shape[1:], jnp.float32)
        for member in range(group):
            pair = kv_head * group + member
            lanes = pl.ds(pl.multiple_of(pair * LANES, LANES), LANES)
            for index in range(blocks):
                seen = (index + 1) * QUERY_ROWS
                place = slice(index * QUERY_ROWS, seen)
                rows = two_heads(queries[place, lanes])
                grad_rows = two_heads(grads[place, lanes])
                row = pl.ds(pair * blocks + index, 1)
                scores = times_transposed(keys[kv_head, :seen, :], rows)
                weights = jnp.exp(scores - log_totals[row, :])
                own = weights[seen - QUERY_ROWS :]
                own = jnp.where(later_key(own.shape), 0.0, own)
                if index:
                    weights = jnp.concatenate([weights[: seen - QUERY_ROWS], own], axis=0)
                else:
                    weights = own
                grad_probs = times_transposed(values[kv_head, :seen, :], grad_rows)
                grad_scores = (weights * (grad_probs - row_dots[row, :])).astype(jnp.bfloat16)
                value_sums[kv_head, :seen, :] += product(weights.astype(jnp.bfloat16), grad_rows)
                key_sums[kv_head, :seen, :] += product(grad_scores, rows)
                turned = product(keys_across[kv_head, :, :seen], grad_scores)
                turned = pick_heads(turned).T * (1.0 / math.sqrt(HEAD_DIM))
                turned = turn(turned, cosine[place, :], -sine[place, :]).astype(jnp.bfloat16)
                for i in range(per):
                    grad_query[block_rows_at(order, index * per + i, block_rows), lanes] = turned[
                        i * block_rows : (i + 1) * block_rows
                    ]
        return carry

    lax.fori_loop(0, kv_heads, attend, 0)

    def finish(block, carry):
        place = pl.ds(pl.multiple_of(block * block_rows, block_rows), block_rows)
        target = block_rows_at(order, block, block_rows)

        def head_sum(head):
            if head < kv_heads:
                tile = key_sums[head, place, :]
            else:
                tile = value_sums[head - kv_heads, place, :]
            tile = tile + pltpu.roll(tile, HEAD_DIM, 1)
            if head < kv_heads:
                tile = turn(tile, cosine[place, :], -sine[place, :])
            return tile

        for tile in range(2 * kv_heads // PAIR):
            first, second = (head_sum(tile * PAIR), head_sum(tile * PAIR + 1))
            joined = jnp.where(low_lanes(first.shape, HEAD_DIM), first, second)
            grad_key_value[target, tile * LANES : (tile + 1) * LANES] = joined.astype(jnp.bfloat16)
        return carry

    lax.fori_loop(0, length // block_rows, finish, 0)


def attend_backward(
    block_rows, order, branch_all, output_weight, queries, keys, values, attended, log_totals, tables
):
    length, width = queries.shape
    kv_heads = keys.shape[0]
    return pl.pallas_call(
        functools.partial(attend_back_body, block_rows),
        out_shape=(shape((length, width)), shape((length, 2 * kv_heads * HEAD_DIM))),
        in_specs=[SMEM] + [VMEM] * 9,
        out_specs=(VMEM, VMEM),
        scratch_shapes=[
            pltpu.VMEM((length, width), jnp.bfloat16),
            pltpu.VMEM(log_totals.shape, jnp.float32),
            pltpu.VMEM((kv_heads, LANES, length), jnp.bfloat16),
            pltpu.VMEM((kv_heads, length, LANES), jnp.float32),
            pltpu.VMEM((kv_heads, length, LANES), jnp.float32),
        ],
        compiler_params=pltpu.CompilerParams(vmem_limit_bytes=56 << 20),
        cost_estimate=pl.CostEstimate(
            flops=6 * 10**10, bytes_accessed=10**7, transcendentals=10**7
        ),
    )(
        order,
        branch_all,
        output_weight,
        queries,
        keys,
        values,
        attended,
        log_totals,
        *tables,
    )


def take_columns(matrix, outer, parts, index):
    rows, columns = matrix.shape
    pieces = matrix.reshape(rows, outer, parts, columns // (outer * parts))
    return lax.dynamic_index_in_dim(pieces, index, axis=2, keepdims=False).reshape(rows, -1)


def take_rows(matrix, parts, index):
    count = matrix.shape[0] // parts
    return lax.dynamic_slice_in_dim(matrix, index * count, count, axis=0)


def put_columns(gathered, outer):
    parts, rows, columns = gathered.shape
    return (
        gathered.reshape(parts, rows, outer, columns // outer)
        .transpose(1, 2, 0, 3)
        .reshape(rows, parts * columns)
    )


def gather_shards(array):
    return lax.all_gather(array, "fsdp", axis=0, tiled=True)


def scatter_shards(array):
    return lax.psum_scatter(
        array.astype(jnp.bfloat16), "fsdp", scatter_dimension=0, tiled=True
    )


def per_device(
    tokens,
    dealing,
    first_gain,
    query_weight,
    key_weight,
    value_weight,
    output_weight,
    second_gain,
    gate_weight,
    up_weight,
    down_weight,
    cotangent,
):
    shard_count = lax.axis_size("fsdp")
    part_count = lax.axis_size("ctx")
    ctx_index = lax.axis_index("ctx")
    shard_index = lax.axis_index("fsdp")
    row_count = tokens.shape[1]
    block_rows = row_count // 2
    seq_rows = row_count * part_count
    own_heads = HEADS // part_count
    dealt_heads = (D // shard_count // part_count) % HEAD_DIM == 0
    kv_heads = KV_HEADS if dealt_heads else max(1, KV_HEADS // part_count)
    kv_first = 0 if dealt_heads else ctx_index * KV_HEADS // part_count
    blocks = jnp.arange(2 * part_count, dtype=jnp.int32)
    order = jnp.sum(
        jnp.where(dealing[0][None, :] == blocks[:, None], blocks[None, :], 0), axis=1
    ).astype(jnp.int32)
    tables = rotary_tables(seq_rows)

    gains = gather_shards(jnp.stack([first_gain, second_gain], axis=1)).astype(jnp.float32)
    gain_first, gain_second = (gains[:, 0][None], gains[:, 1][None])
    key_value = jnp.concatenate([key_weight, value_weight], axis=1)
    if dealt_heads:
        query_part = gather_shards(
            jnp.concatenate(
                [take_columns(query_weight, shard_count, part_count, ctx_index), key_value], axis=1
            )
        )
        query_part, key_value = (query_part[:, : D // part_count], query_part[:, D // part_count :])
        output_part = gather_shards(take_rows(output_weight, part_count, ctx_index))
    else:
        query_part = gather_shards(take_columns(query_weight, 1, part_count, ctx_index))
        output_part = take_rows(gather_shards(output_weight), part_count, ctx_index)
        key_value = gather_shards(key_value).reshape(D, 2, KV_HEADS, HEAD_DIM)
        key_value = lax.dynamic_slice_in_dim(key_value, kv_first, kv_heads, 2).reshape(D, -1)
    gate_part = gather_shards(take_columns(gate_weight, shard_count, part_count, ctx_index))
    up_part = gather_shards(take_columns(up_weight, shard_count, part_count, ctx_index))
    down_part = gather_shards(take_rows(down_weight, part_count, ctx_index))

    first_all, grad_out_all = start_gather(part_count, 1, tokens[0], gain_first, cotangent[0])
    attended, query_rot, key_rot, value_rows, log_totals = attend_forward(
        block_rows, kv_heads, order, first_all, query_part, key_value, tables
    )
    residual_mid, second_all = middle_gather(
        part_count, 2, attended, output_part, tokens[0], gain_second
    )

    gate_act = product(second_all, gate_part)
    upward = product(second_all, up_part)
    sigmoid_gate = jax.nn.sigmoid(gate_act)
    silu_gate = gate_act * sigmoid_gate
    hidden = (silu_gate * upward).astype(jnp.bfloat16)
    grad_hidden = times_transposed(grad_out_all, down_part)
    down_piece = scatter_shards(column_term(hidden, grad_out_all))
    grad_gate = (
        grad_hidden * upward * sigmoid_gate * (1.0 + gate_act * (1.0 - sigmoid_gate))
    ).astype(jnp.bfloat16)
    grad_up = (grad_hidden * silu_gate).astype(jnp.bfloat16)
    grad_mid, second_gain_part, branch_all = middle_back(
        part_count, 3, grad_gate, gate_part, grad_up, up_part, residual_mid, gain_second, cotangent[0]
    )
    gate_piece = scatter_shards(column_term(second_all, grad_gate))
    up_piece = scatter_shards(column_term(second_all, grad_up))
    block_output = output_scatter(part_count, 4, hidden, down_part, residual_mid)

    grad_query, grad_key_value = attend_backward(
        block_rows,
        order,
        branch_all,
        output_part,
        query_rot,
        key_rot,
        value_rows,
        attended,
        log_totals,
        tables,
    )
    grad_input, first_gain_part = input_back(
        part_count,
        5,
        grad_query,
        query_part,
        grad_key_value,
        key_value,
        tokens[0],
        gain_first,
        grad_mid,
    )

    query_piece = scatter_shards(column_term(first_all, grad_query))
    key_value_piece = scatter_shards(column_term(first_all, grad_key_value))
    output_term = column_term(attended, branch_all)

    def gather_columns(piece, outer):
        return put_columns(lax.all_gather(piece, "ctx", axis=0), outer).astype(jnp.float32)

    if dealt_heads:
        output_shard = lax.all_gather(scatter_shards(output_term), "ctx", axis=0, tiled=True)
        key_value_shard = lax.psum(key_value_piece, "ctx").astype(jnp.float32)
    else:
        spread = jnp.zeros((D, D), jnp.float32)
        spread = lax.dynamic_update_slice_in_dim(
            spread, output_term, ctx_index * output_term.shape[0], 0
        )
        output_shard = lax.psum(scatter_shards(spread), "ctx")
        wide = jnp.zeros((D // shard_count, 2, KV_HEADS, HEAD_DIM), jnp.bfloat16)
        wide = lax.dynamic_update_slice_in_dim(
            wide, key_value_piece.reshape(-1, 2, kv_heads, HEAD_DIM), kv_first, 2
        )
        key_value_shard = lax.psum(wide.reshape(-1, 2 * KV_WIDTH), "ctx").astype(jnp.float32)
    gain_totals = lax.psum(
        jnp.concatenate([first_gain_part, second_gain_part], axis=0), ("ctx", "fsdp")
    )
    gain_rows = D // shard_count
    gain_shard = lax.dynamic_slice_in_dim(gain_totals, shard_index * gain_rows, gain_rows, 1)
    return (
        block_output[None],
        grad_input[None],
        gain_shard[0],
        gather_columns(query_piece, shard_count if dealt_heads else 1),
        key_value_shard[:, :KV_WIDTH],
        key_value_shard[:, KV_WIDTH:],
        output_shard.astype(jnp.float32),
        gain_shard[1],
        gather_columns(gate_piece, shard_count),
        gather_columns(up_piece, shard_count),
        lax.all_gather(down_piece, "ctx", axis=0, tiled=True).astype(jnp.float32),
    )


def solution(mesh):
    in_specs = (
        P("fsdp", "ctx", None),
        P("fsdp", None),
        P("fsdp"),
        P("fsdp", None),
        P("fsdp", None),
        P("fsdp", None),
        P("fsdp", None),
        P("fsdp"),
        P("fsdp", None),
        P("fsdp", None),
        P("fsdp", None),
        P("fsdp", "ctx", None),
    )
    out_specs = (
        P("fsdp", "ctx", None),
        P("fsdp", "ctx", None),
        P("fsdp"),
        P("fsdp", None),
        P("fsdp", None),
        P("fsdp", None),
        P("fsdp", None),
        P("fsdp"),
        P("fsdp", None),
        P("fsdp", None),
        P("fsdp", None),
    )
    return jax.shard_map(
        per_device, mesh=mesh, in_specs=in_specs, out_specs=out_specs, check_vma=False
    )
```

```python
import functools
import math

import jax
import jax.numpy as jnp
from jax import lax
from jax.experimental import pallas as pl
from jax.experimental.pallas import tpu as pltpu
from jax.sharding import PartitionSpec as P

D = 2048
FF = 5632
HEADS = 32
KV_HEADS = 4
HEAD_DIM = 64
KV_WIDTH = 256


epsilon = 1e-05


MESH = pl.DeviceIdType.MESH
VMEM = pl.BlockSpec(memory_space=pltpu.VMEM)
SMEM = pl.BlockSpec(memory_space=pltpu.SMEM)
HBM = pl.BlockSpec(memory_space=pl.ANY)
LANES = 128
PAIR = LANES // HEAD_DIM
QUERY_ROWS = 256


def shape(dims, kind=jnp.bfloat16):
    return jax.ShapeDtypeStruct(dims, kind)


def norm_parts(values):
    inverse = lax.rsqrt(jnp.mean(values * values, axis=-1, keepdims=True) + epsilon)
    return (values * inverse, inverse)


def norm_back(gradient, normed, inverse):
    return inverse * (gradient - normed * jnp.mean(gradient * normed, axis=-1, keepdims=True))


def product(left_side, right_side):
    return jnp.dot(left_side, right_side, preferred_element_type=jnp.float32)


def times_transposed(left_side, right_side):
    return lax.dot_general(
        left_side, right_side, (((1,), (1,)), ((), ())), preferred_element_type=jnp.float32
    )


def column_term(source, gradient):
    return lax.dot_general(
        source, gradient, (((0,), (0,)), ((), ())), preferred_element_type=jnp.float32
    )


STRIP = 32
PIECES = 4


def plane_places():
    me = lax.axis_index("ctx")
    return (me, me + 1 - 2 * lax.rem(me, 2), lax.rem(me + 2, 4), 3 - me)


def signal(barrier, **place):
    pl.semaphore_signal(barrier, inc=1, device_id=place, device_id_type=MESH)


def meet(count, shards=1):
    me = lax.axis_index("ctx")
    barrier = pltpu.get_barrier_semaphore()
    for step in range(1, count):
        signal(barrier, ctx=lax.rem(me + step, count))
    for step in range(1, shards):
        signal(barrier, fsdp=lax.rem(lax.axis_index("fsdp") + step, shards))
    pl.semaphore_wait(barrier, count - 1 + shards - 1)


def remote(source, target, send_sem, recv_sem, **place):
    copy = pltpu.make_async_remote_copy(
        src_ref=source,
        dst_ref=target,
        send_sem=send_sem,
        recv_sem=recv_sem,
        device_id=place,
        device_id_type=MESH,
    )
    copy.start()
    return copy


def gather_sems(count):
    sends = 3 if count == 4 else count - 1
    return [
        pltpu.SemaphoreType.DMA((PIECES,)),
        pltpu.SemaphoreType.DMA((sends, PIECES)),
        pltpu.SemaphoreType.DMA((sends, PIECES)),
    ]


class RowGather:
    def __init__(self, count, own, out, sems):
        self.count, self.own, self.out = (count, own, out)
        self.local_sem, self.send_sem, self.recv_sem = sems
        self.size = own.shape[0] // PIECES
        self.copies = [[] for _ in range(PIECES)]

    def place(self, owner, piece):
        start = owner * self.own.shape[0] + piece * self.size
        return self.out.at[pl.ds(pl.multiple_of(start, self.size), self.size)]

    def send(self, piece):
        me = lax.axis_index("ctx")
        source = self.own.at[pl.ds(piece * self.size, self.size)]
        target = self.place(me, piece)
        if self.count == 4:
            _, across, along, _ = plane_places()
            peers = (across, along)
        else:
            peers = [lax.rem(me + step, self.count) for step in range(1, self.count)]
        for index, peer in enumerate(peers):
            self.copies[piece].append(
                remote(
                    source,
                    target,
                    self.send_sem.at[index, piece],
                    self.recv_sem.at[index, piece],
                    ctx=peer,
                )
            )
        local = pltpu.make_async_copy(source, target, self.local_sem.at[piece])
        local.start()
        self.copies[piece].append(local)

    def finish(self):
        if self.count != 4:
            for copies in self.copies:
                for copy in copies:
                    copy.wait()
            return
        _, across, along, _ = plane_places()
        relays = []
        for piece in (0, PIECES // 2, 1, PIECES // 2 + 1):
            first = piece < PIECES // 2
            came, left = (0, 1) if first else (1, 0)
            owner, peer = (across, along) if first else (along, across)
            self.copies[piece][came].wait_recv()
            block = self.place(owner, piece)
            relays.append(
                remote(
                    block, block, self.send_sem.at[2, piece], self.recv_sem.at[2, piece], ctx=peer
                )
            )
        for piece in range(PIECES):
            to_across, to_along, local = self.copies[piece]
            (to_along if piece < PIECES // 2 else to_across).wait_recv()
            to_across.wait_send()
            to_along.wait_send()
            local.wait()
        for relay in relays:
            relay.wait()


def product_blocks(count, pairs, rows, width):
    tile = 512

    def block(owner, store):
        start = pl.multiple_of(owner * rows, rows)

        def column(index, carry):
            columns = pl.ds(pl.multiple_of(index * tile, tile), tile)
            value = None
            for left, right, transposed in pairs:
                piece = left[pl.ds(start, rows), :]
                if transposed:
                    term = times_transposed(piece, right[columns, : piece.shape[1]])
                else:
                    term = product(piece, right[:, columns])
                value = term if value is None else value + term
            store(columns, value)
            return carry

        lax.fori_loop(0, width // tile, column, 0)

    return block


def scatter_products(count, pairs, send_buf, recv_buf, kept, total, send_sem, recv_sem):
    rows, width = total.shape
    half = rows // 2
    block = product_blocks(count, pairs, rows, width)
    me = lax.axis_index("ctx")

    def store_own(columns, value):
        total[:, columns] = value

    def send(slot, part, sem, peer):
        return remote(
            send_buf.at[slot, part],
            recv_buf.at[slot, part],
            send_sem.at[sem],
            recv_sem.at[sem],
            ctx=peer,
        )

    if count != 4:
        copies = []
        for step in range(1, count):
            owner = lax.rem(me + step, count)

            def store_sent(columns, value, step=step):
                send_buf[step - 1, :, columns] = value.astype(send_buf.dtype)

            block(owner, store_sent)
            copies.append(send(step - 1, pl.ds(0, rows), step - 1, owner))
        block(me, store_own)
        for copy in copies:
            copy.wait()
        return
    _, across, along, corner = plane_places()
    low, high = (pl.ds(0, half), pl.ds(half, half))

    def store_corner(columns, value):
        send_buf[0, :, columns] = value.astype(send_buf.dtype)

    def store_across(columns, value):
        send_buf[1, low, columns] = value[:half].astype(send_buf.dtype)
        kept[high, columns] = value[half:]

    def store_along(columns, value):
        send_buf[1, high, columns] = value[half:].astype(send_buf.dtype)
        kept[low, columns] = value[:half]

    block(corner, store_corner)
    relay_low = send(0, low, 0, across)
    relay_high = send(0, high, 1, along)
    block(across, store_across)
    direct_low = send(1, low, 2, across)
    block(along, store_along)
    direct_high = send(1, high, 3, along)
    block(me, store_own)

    def add(where):
        value = kept[where, :] + recv_buf[0, where, :].astype(jnp.float32)
        send_buf[2, where, :] = value.astype(send_buf.dtype)

    relay_low.wait_recv()
    for_strips(0, half, add)
    final_low = send(2, low, 4, along)
    relay_high.wait_recv()
    for_strips(half, half, add)
    final_high = send(2, high, 5, across)
    relay_low.wait_send()
    relay_high.wait_send()
    direct_low.wait()
    direct_high.wait()
    final_low.wait()
    final_high.wait()


def scatter_scratch(count, rows, width):
    slots = 3 if count == 4 else count - 1
    sems = 6 if count == 4 else count - 1
    return [
        pltpu.VMEM((slots, rows, width), jnp.bfloat16),
        pltpu.VMEM((slots, rows, width), jnp.bfloat16),
        pltpu.VMEM((rows, width) if count == 4 else (8, LANES), jnp.float32),
        pltpu.VMEM((rows, width), jnp.float32),
        pltpu.SemaphoreType.DMA((sems,)),
        pltpu.SemaphoreType.DMA((sems,)),
    ]


def received(count, recv_buf, total, rows):
    value = total[rows, :]
    for slot in (1, 2) if count == 4 else range(count - 1):
        value = value + recv_buf[slot, rows, :].astype(jnp.float32)
    return value


def for_strips(first, rows, body):
    def strip(index, carry):
        body(pl.ds(pl.multiple_of(first + index * STRIP, STRIP), STRIP))
        return carry

    lax.fori_loop(0, rows // STRIP, strip, 0)


def call_plane(body, ident, outs, out_specs, in_specs, scratch, flops, megabytes, args):
    return pl.pallas_call(
        body,
        out_shape=outs,
        in_specs=in_specs,
        out_specs=out_specs,
        scratch_shapes=scratch,
        compiler_params=pltpu.CompilerParams(
            collective_id=ident, has_side_effects=True, vmem_limit_bytes=megabytes << 20
        ),
        cost_estimate=pl.CostEstimate(
            flops=flops, bytes_accessed=flops // 300, transcendentals=0
        ),
    )(*args)


def start_body(count, shards, tokens, gains, tokens_all, gains_all, *sems):
    meet(count, shards)
    gain_local, gain_send, gain_recv = sems[:3]
    me = lax.axis_index("fsdp")
    copies = []
    for step in range(1, shards):
        copies.append(
            remote(
                gains,
                gains_all.at[me],
                gain_send.at[step - 1],
                gain_recv.at[step - 1],
                fsdp=lax.rem(me + step, shards),
            )
        )
    local = pltpu.make_async_copy(gains, gains_all.at[me], gain_local)
    local.start()
    first = RowGather(count, tokens, tokens_all, sems[3:6])
    order = (0, PIECES // 2, 1, PIECES // 2 + 1)
    for piece in order:
        first.send(piece)
    first.finish()
    local.wait()
    for copy in copies:
        copy.wait()


def start_gather(count, shards, ident, tokens, gains):
    rows, width = tokens.shape
    gathered = shape((count * rows, width))
    return call_plane(
        functools.partial(start_body, count, shards),
        ident,
        (gathered, shape((shards,) + gains.shape)),
        (HBM, HBM),
        [HBM] * 2,
        [
            pltpu.SemaphoreType.DMA,
            pltpu.SemaphoreType.DMA((shards - 1,)),
            pltpu.SemaphoreType.DMA((shards - 1,)),
        ]
        + gather_sems(count),
        4 * 10**10,
        4,
        (tokens, gains),
    )


def strips_and_send(gather, strip):
    size = gather.size
    for piece in range(PIECES):
        for_strips(piece * size, size, strip)
        gather.send(piece)
    gather.finish()


def middle_body(
    count, attended, weight, tokens, gain, residual, second_all, own, send_buf, recv_buf, kept, total,
    send_sem, recv_sem, *sems
):
    meet(count)
    scatter_products(
        count, [(attended, weight, False)], send_buf, recv_buf, kept, total, send_sem, recv_sem
    )

    def strip(where):
        values = tokens[where, :].astype(jnp.float32) + received(count, recv_buf, total, where)
        residual[where, :] = values
        normed, _ = norm_parts(values)
        own[where, :] = (normed * gain[...]).astype(jnp.bfloat16)

    strips_and_send(RowGather(count, own, second_all, sems), strip)


def middle_gather(count, ident, attended, weight, tokens, gain):
    rows, width = tokens.shape
    return call_plane(
        functools.partial(middle_body, count),
        ident,
        (shape((rows, width), jnp.float32), shape((count * rows, width))),
        (VMEM, HBM),
        [VMEM] * 4,
        [pltpu.VMEM((rows, width), jnp.bfloat16)]
        + scatter_scratch(count, rows, width)
        + gather_sems(count),
        6 * 10**10,
        40,
        (attended, weight, tokens, gain),
    )


def middle_back_body(
    count, grad_gate_up, gate_up_weight, residual, gain, grad_out, grad_mid, gain_part,
    branch_all, own, send_buf, recv_buf, kept, total, send_sem, recv_sem, *sems
):
    meet(count)
    scatter_products(
        count,
        [(grad_gate_up, gate_up_weight, True)],
        send_buf,
        recv_buf,
        kept,
        total,
        send_sem,
        recv_sem,
    )
    gain_part[...] = jnp.zeros_like(gain_part)

    def strip(where):
        gradient = received(count, recv_buf, total, where)
        normed, inverse = norm_parts(residual[where, :])
        gain_part[...] += jnp.sum(gradient * normed, axis=0, keepdims=True)
        values = grad_out[where, :].astype(jnp.float32) + norm_back(
            gradient * gain[...], normed, inverse
        )
        grad_mid[where, :] = values
        own[where, :] = values.astype(jnp.bfloat16)

    strips_and_send(RowGather(count, own, branch_all, sems), strip)


def column_halves(array):
    rows, width = array.shape
    if width // 2 % LANES:
        return ((array[:, : width // 2], array[:, width // 2 :]), (VMEM, VMEM))
    specs = [pl.BlockSpec((rows, width // 2), lambda *index, side=side: (0, side)) for side in (0, 1)]
    return ((array, array), specs)


def middle_back(count, ident, grad_gate_up, gate_up_weight, residual, gain, grad_out):
    rows, width = residual.shape
    return call_plane(
        functools.partial(middle_back_body, count),
        ident,
        (
            shape((rows, width), jnp.float32),
            shape((1, width), jnp.float32),
            shape((count * rows, width)),
        ),
        (VMEM, VMEM, HBM),
        [VMEM] * 5,
        [pltpu.VMEM((rows, width), jnp.bfloat16)]
        + scatter_scratch(count, rows, width)
        + gather_sems(count),
        6 * 10**10,
        52,
        (grad_gate_up, gate_up_weight, residual, gain, grad_out),
    )


def input_back_body(
    count, shards, grad_packed, weight, tokens, gain, grad_mid, second_part, grad_input, gain_sums, gain_part, parts, part_recv, sums, sums_recv, send_buf,
    recv_buf, kept, total, send_sem, recv_sem, part_send_sem, part_recv_sem, sums_send_sem,
    sums_recv_sem
):
    meet(count, shards)
    scatter_products(
        count,
        [(grad_packed, weight, True)],
        send_buf,
        recv_buf,
        kept,
        total,
        send_sem,
        recv_sem,
    )
    gain_part[...] = jnp.zeros_like(gain_part)

    def strip(where):
        gradient = received(count, recv_buf, total, where)
        normed, inverse = norm_parts(tokens[where, :].astype(jnp.float32))
        gain_part[...] += jnp.sum(gradient * normed, axis=0, keepdims=True)
        values = grad_mid[where, :] + norm_back(gradient * gain[...], normed, inverse)
        grad_input[where, :] = values.astype(jnp.bfloat16)

    for_strips(0, grad_input.shape[0], strip)
    me = lax.axis_index("fsdp")
    span = parts.shape[2]
    for shard in range(shards):
        lanes = slice(shard * span, (shard + 1) * span)
        parts[shard, 0:1, :] = gain_part[:, lanes]
        parts[shard, 1:2, :] = second_part[:, lanes]
    copies = []
    for step in range(1, shards):
        peer = lax.rem(me + step, shards)
        copies.append(
            remote(
                parts.at[peer],
                part_recv.at[step - 1],
                part_send_sem.at[step - 1],
                part_recv_sem.at[step - 1],
                fsdp=peer,
            )
        )
    for copy in copies:
        copy.wait()
    value = parts[me]
    for step in range(1, shards):
        value = value + part_recv[step - 1]
    sums[...] = value
    copies = []
    for step in range(1, count):
        copies.append(
            remote(
                sums,
                sums_recv.at[step - 1],
                sums_send_sem.at[step - 1],
                sums_recv_sem.at[step - 1],
                ctx=lax.rem(lax.axis_index("ctx") + step, count),
            )
        )
    for copy in copies:
        copy.wait()
    for step in range(1, count):
        value = value + sums_recv[step - 1]
    gain_sums[...] = value


def input_back(
    count, shards, ident, grad_packed, weight, tokens, gain, grad_mid, second_part
):
    rows, width = tokens.shape
    span = width // shards
    return call_plane(
        functools.partial(input_back_body, count, shards),
        ident,
        (shape((rows, width)), shape((2, span), jnp.float32)),
        (VMEM, VMEM),
        [VMEM] * 6,
        [
            pltpu.VMEM((1, width), jnp.float32),
            pltpu.VMEM((shards, 2, span), jnp.float32),
            pltpu.VMEM((shards - 1, 2, span), jnp.float32),
            pltpu.VMEM((2, span), jnp.float32),
            pltpu.VMEM((count - 1, 2, span), jnp.float32),
        ]
        + scatter_scratch(count, rows, width)
        + [
            pltpu.SemaphoreType.DMA((shards - 1,)),
            pltpu.SemaphoreType.DMA((shards - 1,)),
            pltpu.SemaphoreType.DMA((count - 1,)),
            pltpu.SemaphoreType.DMA((count - 1,)),
        ],
        5 * 10**10,
        40,
        (grad_packed, weight, tokens, gain, grad_mid, second_part),
    )


def swap(array, along):
    pairs = [(i, (i + 2) % 4) if along else (i, i + 1 - 2 * (i % 2)) for i in range(4)]
    return lax.ppermute(array, "ctx", pairs)


def plane_gather(array):
    if lax.axis_size("ctx") != 4:
        return lax.all_gather(array, "ctx", axis=0)
    half = array.shape[0] // 2
    across, along = (swap(array, False), swap(array, True))
    low, high = (swap(across[:half], True), swap(along[half:], False))
    return (array, across, along, low, high)


def take_half(partial, owner, side):
    rows = partial.shape[0] // lax.axis_size("ctx")
    half = rows // 2
    return lax.dynamic_slice_in_dim(partial, owner * rows + side * half, half, 0)


def plane_relay(partial):
    if lax.axis_size("ctx") != 4:
        return (partial,)
    me, across, along, corner = plane_places()
    take = functools.partial(take_half, partial)
    low = swap(jnp.stack([take(corner, 0), take(across, 0)]), False)
    high = swap(jnp.stack([take(corner, 1), take(along, 1)]), True)
    return (low, high)


def add_parts(first, second):
    return first.astype(jnp.float32) + second.astype(jnp.float32)


def plane_last(partial, relayed):
    if lax.axis_size("ctx") != 4:
        return (lax.psum_scatter(relayed[0], "ctx", scatter_dimension=0, tiled=True),)
    me, across, along, corner = plane_places()
    take = functools.partial(take_half, partial)
    low, high = relayed
    last_low = swap(add_parts(take(along, 0), low[0]).astype(jnp.bfloat16), True)
    last_high = swap(add_parts(take(across, 1), high[0]).astype(jnp.bfloat16), False)
    return (last_low, last_high)


def plane_scatter(partial, relayed, last):
    if lax.axis_size("ctx") != 4:
        return last[0].astype(jnp.float32)
    me = lax.axis_index("ctx")
    return jnp.concatenate(
        [
            add_parts(take_half(partial, me, side), relayed[side][1])
            + last[side].astype(jnp.float32)
            for side in (0, 1)
        ],
        axis=0,
    )


def hidden_body(rows, gate_weight, up_weight, gate_up, hidden):
    width = hidden.shape[1]
    gate = product(rows[...], gate_weight[...])
    gate_up[:, :width] = gate
    upward = product(rows[...], up_weight[...])
    gate_up[:, width:] = upward
    hidden[...] = (gate * jax.nn.sigmoid(gate) * upward).astype(jnp.bfloat16)


def hidden_forward(second_all, gate_up_weight):
    length, depth = second_all.shape
    width = gate_up_weight.shape[1] // 2
    (gate_weight, up_weight), specs = column_halves(gate_up_weight)
    step = QUERY_ROWS
    return pl.pallas_call(
        hidden_body,
        grid=(length // step,),
        out_shape=(shape((length, 2 * width), jnp.float32), shape((length, width))),
        in_specs=[pl.BlockSpec((step, depth), lambda i: (i, 0))] + list(specs),
        out_specs=(
            pl.BlockSpec((step, 2 * width), lambda i: (i, 0)),
            pl.BlockSpec((step, width), lambda i: (i, 0)),
        ),
        compiler_params=pltpu.CompilerParams(vmem_limit_bytes=52 << 20),
        cost_estimate=pl.CostEstimate(
            flops=4 * length * depth * width, bytes_accessed=3 * 10**7, transcendentals=10**6
        ),
    )(second_all, gate_weight, up_weight)


def hidden_back_body(grad_rows, down_weight, gate_up, grad_gate_up):
    width = down_weight.shape[0]
    grad_hidden = times_transposed(grad_rows[...], down_weight[...])
    gate, upward = (gate_up[:, :width], gate_up[:, width:])
    sigmoid_gate = jax.nn.sigmoid(gate)
    silu_gate = gate * sigmoid_gate
    grad_gate = grad_hidden * upward * sigmoid_gate * (1.0 + gate * (1.0 - sigmoid_gate))
    grad_gate_up[:, :width] = grad_gate.astype(jnp.bfloat16)
    grad_gate_up[:, width:] = (grad_hidden * silu_gate).astype(jnp.bfloat16)


def hidden_backward(grad_out_all, down_weight, gate_up):
    length, depth = grad_out_all.shape
    width = down_weight.shape[0]
    step = QUERY_ROWS
    return pl.pallas_call(
        hidden_back_body,
        grid=(length // step,),
        out_shape=shape((length, 2 * width)),
        in_specs=[
            pl.BlockSpec((step, depth), lambda i: (i, 0)),
            pl.BlockSpec((width, depth), lambda i: (0, 0)),
            pl.BlockSpec((step, 2 * width), lambda i: (i, 0)),
        ],
        out_specs=pl.BlockSpec((step, 2 * width), lambda i: (i, 0)),
        compiler_params=pltpu.CompilerParams(vmem_limit_bytes=48 << 20),
        cost_estimate=pl.CostEstimate(
            flops=2 * length * depth * width, bytes_accessed=3 * 10**7, transcendentals=10**6
        ),
    )(grad_out_all, down_weight, gate_up)


def attention_grads_body(inputs, grad_packed, attended, branch_all, packed):
    width = grad_packed.shape[1]
    packed[:, :width] = product(inputs[...].T, grad_packed[...]).astype(jnp.bfloat16)
    rows = HEAD_DIM
    heads = attended[...].T
    upper = lax.rem(pl.program_id(0), PAIR) == 1
    heads = jnp.where(upper, heads[rows:], heads[:rows])
    out = product(heads, branch_all[...]).astype(jnp.bfloat16)
    part = out.shape[1] // (packed.shape[0] // rows)
    for index in range(packed.shape[0] // rows):
        packed[index * rows : (index + 1) * rows, width:] = out[
            :, index * part : (index + 1) * part
        ]


def attention_grads(shards, first_all, grad_packed, attended, branch_all):
    length, depth = first_all.shape
    span = depth // shards
    width = grad_packed.shape[1] + attended.shape[1]
    return pl.pallas_call(
        attention_grads_body,
        grid=(shards,),
        out_shape=shape((depth, width)),
        in_specs=[
            pl.BlockSpec((length, span), lambda i: (0, i)),
            pl.BlockSpec(grad_packed.shape, lambda i: (0, 0)),
            pl.BlockSpec((length, LANES), lambda i: (0, i // PAIR)),
            pl.BlockSpec(branch_all.shape, lambda i: (0, 0)),
        ],
        out_specs=pl.BlockSpec((span, width), lambda i: (i, 0)),
        compiler_params=pltpu.CompilerParams(vmem_limit_bytes=48 << 20),
        cost_estimate=pl.CostEstimate(
            flops=2 * length * depth * width, bytes_accessed=2 * 10**7, transcendentals=0
        ),
    )(first_all, grad_packed, attended, branch_all)


def sort_parts(parts, sorted_parts, corner_low):
    me, across, along, corner = plane_places()
    own, from_across, from_along, low, high = parts
    sorted_parts[me] = own[...]
    sorted_parts[across] = from_across[...]
    sorted_parts[along] = from_along[...]

    @pl.when(corner_low)
    def _():
        sorted_parts[corner] = low[...]

    @pl.when(jnp.logical_not(corner_low))
    def _():
        sorted_parts[corner] = high[...]


def place_hidden_body(shards, *refs):
    parts, (gate, up, sorted_parts) = (refs[:5], refs[5:])
    steps = pl.num_programs(0)
    sort_parts(parts, sorted_parts, pl.program_id(0) < steps // 2)
    count = sorted_parts.shape[0]
    width = sorted_parts.shape[2] // 2
    span = width // shards
    for target, offset in ((gate, 0), (up, width)):
        values = [
            sorted_parts[part, :, offset : offset + width].astype(jnp.float32)
            for part in range(count)
        ]
        target[...] = jnp.concatenate(
            [
                values[part][:, shard * span : (shard + 1) * span]
                for shard in range(shards)
                for part in range(count)
            ],
            axis=1,
        )


def place_hidden(shards, parts):
    rows, width = parts[0].shape
    step = 32
    half = rows // step // 2
    outs = shape((rows, 2 * width), jnp.float32)
    whole = pl.BlockSpec((step, width), lambda i: (i, 0))
    low = pl.BlockSpec((step, width), lambda i: (jnp.minimum(i, half - 1), 0))
    high = pl.BlockSpec((step, width), lambda i: (jnp.maximum(i - half, 0), 0))
    result = pl.BlockSpec((step, 2 * width), lambda i: (i, 0))
    return pl.pallas_call(
        functools.partial(place_hidden_body, shards),
        grid=(rows // step,),
        out_shape=(outs, outs),
        in_specs=[whole, whole, whole, low, high],
        out_specs=(result, result),
        scratch_shapes=[pltpu.VMEM((4, step, width), jnp.bfloat16)],
        cost_estimate=pl.CostEstimate(flops=0, bytes_accessed=2 * 10**7, transcendentals=0),
        compiler_params=pltpu.CompilerParams(vmem_limit_bytes=24 << 20),
    )(*parts)


def place_rows_body(own, from_across, from_along, low, high, out):
    me, across, along, corner = plane_places()
    rows = own.shape[0]

    def put(owner, offset, ref):
        size = ref.shape[0]
        start = pl.multiple_of(owner * rows + offset, 8)
        out[pl.ds(start, size), :] = ref[...].astype(out.dtype)

    put(me, 0, own)
    put(across, 0, from_across)
    put(along, 0, from_along)
    put(corner, 0, low)
    put(corner, rows // 2, high)


def place_rows(parts, kind):
    rows, width = parts[0].shape
    return pl.pallas_call(
        place_rows_body,
        out_shape=shape((4 * rows, width), kind),
        in_specs=[VMEM] * 5,
        out_specs=VMEM,
        cost_estimate=pl.CostEstimate(flops=0, bytes_accessed=10**7, transcendentals=0),
        compiler_params=pltpu.CompilerParams(vmem_limit_bytes=24 << 20),
    )(*parts)


def place_attention_body(shards, own, from_across, from_along, low, high, query, key, value, output, sorted_parts):
    me, across, along, corner = plane_places()
    rows = own.shape[0]
    sorted_parts[me] = own[...]
    sorted_parts[across] = from_across[...]
    sorted_parts[along] = from_along[...]
    sorted_parts[corner, : rows // 2] = low[...]
    sorted_parts[corner, rows // 2 :] = high[...]
    count = sorted_parts.shape[0]
    width = query.shape[1] // count
    span = width // shards
    values = [sorted_parts[part, :, :width].astype(jnp.float32) for part in range(count)]
    query[...] = jnp.concatenate(
        [
            values[part][:, shard * span : (shard + 1) * span]
            for shard in range(shards)
            for part in range(count)
        ],
        axis=1,
    )
    sums = None
    for part in range(count):
        term = sorted_parts[part, :, width : width + 2 * KV_WIDTH].astype(jnp.float32)
        sums = term if sums is None else sums + term
    key[...] = sums[:, :KV_WIDTH]
    value[...] = sums[:, KV_WIDTH:]
    height = rows // count
    for part in range(count):
        for index in range(count):
            tile = sorted_parts[part, index * height : (index + 1) * height, width + 2 * KV_WIDTH :]
            output[part * height : (part + 1) * height, index * width : (index + 1) * width] = (
                tile.astype(jnp.float32)
            )


def place_attention(shards, parts):
    rows, width = parts[0].shape
    wide = shape((rows, D), jnp.float32)
    narrow = shape((rows, KV_WIDTH), jnp.float32)
    return pl.pallas_call(
        functools.partial(place_attention_body, shards),
        out_shape=(wide, narrow, narrow, wide),
        in_specs=[VMEM] * 5,
        out_specs=(VMEM,) * 4,
        scratch_shapes=[pltpu.VMEM((4, rows, width), jnp.bfloat16)],
        cost_estimate=pl.CostEstimate(flops=0, bytes_accessed=10**7, transcendentals=0),
        compiler_params=pltpu.CompilerParams(vmem_limit_bytes=32 << 20),
    )(*parts)


def rotary_tables(length):
    frequency = jnp.exp(
        -math.log(10000.0) * jnp.arange(HEAD_DIM // 2).astype(jnp.float32) * (2.0 / HEAD_DIM)
    )
    angles = jnp.arange(length).astype(jnp.float32)[:, None] * frequency[None, :]
    cosine, sine = (jnp.cos(angles), jnp.sin(angles))
    return (
        jnp.concatenate([cosine] * (2 * PAIR), axis=1),
        jnp.concatenate([-sine, sine] * PAIR, axis=1),
    )


def low_lanes(dims, size):
    return lax.rem(lax.broadcasted_iota(jnp.int32, dims, len(dims) - 1), 2 * size) < size


def turn(values, cosine, sine):
    half = HEAD_DIM // 2
    swapped = jnp.where(
        low_lanes(values.shape, half),
        pltpu.roll(values, LANES - half, 1),
        pltpu.roll(values, half, 1),
    )
    return values * cosine + swapped * sine


def two_heads(values):
    low = low_lanes(values.shape, HEAD_DIM)
    zero = jnp.zeros_like(values)
    return jnp.concatenate([jnp.where(low, values, zero), jnp.where(low, zero, values)], axis=0)


def pick_heads(values):
    rows = values.shape[1] // PAIR
    return jnp.concatenate(
        [values[:HEAD_DIM, :rows], values[HEAD_DIM:, rows:]], axis=0
    )


def later_key(dims):
    key = lax.broadcasted_iota(jnp.int32, dims, 0)
    query = lax.rem(lax.broadcasted_iota(jnp.int32, dims, 1), QUERY_ROWS)
    return key > query


def block_rows_at(order, block, rows):
    return pl.ds(pl.multiple_of(order[block] * rows, rows), rows)


def rows_in_order(order, source, index, rows):
    per = QUERY_ROWS // rows
    return jnp.concatenate(
        [source[block_rows_at(order, index * per + i, rows), :] for i in range(per)], axis=0
    )


def attend_body(
    block_rows,
    order,
    tokens_all,
    gain,
    weight,
    cosine,
    sine,
    attended,
    queries,
    keys,
    values,
    log_totals,
    first_all,
    values_across,
):
    length, width = queries.shape
    kv_heads = keys.shape[0]
    pairs = width // LANES
    blocks = length // QUERY_ROWS

    def project(index, carry):
        place = pl.ds(pl.multiple_of(index * QUERY_ROWS, QUERY_ROWS), QUERY_ROWS)
        normed, _ = norm_parts(
            rows_in_order(order, tokens_all, index, block_rows).astype(jnp.float32)
        )
        rows = (normed * gain[...]).astype(jnp.bfloat16)
        for i in range(QUERY_ROWS // block_rows):
            first_all[block_rows_at(order, index * (QUERY_ROWS // block_rows) + i, block_rows), :] = (
                rows[i * block_rows : (i + 1) * block_rows]
            )
        cos_rows, sin_rows = (cosine[place, :], sine[place, :])
        projected = product(rows, weight[:, :width])
        for pair in range(pairs):
            lanes = slice(pair * LANES, (pair + 1) * LANES)
            turned = turn(projected[:, lanes], cos_rows, sin_rows).astype(jnp.bfloat16)
            queries[place, lanes] = turned * jnp.asarray(1.0 / math.sqrt(HEAD_DIM), jnp.bfloat16)
        projected = product(rows, weight[:, width : width + 2 * kv_heads * HEAD_DIM])
        for head in range(2 * kv_heads):
            tile = projected[:, head // PAIR * LANES : (head // PAIR + 1) * LANES]
            if head < kv_heads:
                tile = turn(tile, cos_rows, sin_rows)
            low = low_lanes(tile.shape, HEAD_DIM)
            moved = pltpu.roll(tile, HEAD_DIM, 1)
            both = jnp.where(low, tile, moved) if head % PAIR == 0 else jnp.where(low, moved, tile)
            if head < kv_heads:
                keys[head, place, :] = both.astype(jnp.bfloat16)
            else:
                values[head - kv_heads, place, :] = both.astype(jnp.bfloat16)
                values_across[head - kv_heads, :, place] = both.T.astype(jnp.bfloat16)
        return carry

    lax.fori_loop(0, blocks, project, 0)

    def attend(pair, carry):
        kv_head = pair // (pairs // kv_heads)
        lanes = pl.ds(pl.multiple_of(pair * LANES, LANES), LANES)
        for index in range(blocks):
            seen = (index + 1) * QUERY_ROWS
            rows = two_heads(queries[index * QUERY_ROWS : seen, lanes])
            scores = times_transposed(keys[kv_head, :seen, :], rows)
            own = scores[seen - QUERY_ROWS :]
            own = jnp.where(later_key(own.shape), -1e30, own)
            if index:
                scores = jnp.concatenate([scores[: seen - QUERY_ROWS], own], axis=0)
            else:
                scores = own
            largest = jnp.max(scores, axis=0, keepdims=True)
            exponent = jnp.exp(scores - largest)
            totals = jnp.sum(exponent, axis=0, keepdims=True)
            mixed = product(values_across[kv_head, :, :seen], exponent.astype(jnp.bfloat16))
            log_totals[pl.ds(pair * blocks + index, 1), :] = largest + jnp.log(totals)
            mixed = pick_heads(mixed / totals).T.astype(jnp.bfloat16)
            per = QUERY_ROWS // block_rows
            for i in range(per):
                attended[block_rows_at(order, index * per + i, block_rows), lanes] = mixed[
                    i * block_rows : (i + 1) * block_rows
                ]
        return carry

    lax.fori_loop(0, pairs, attend, 0)


def attend_forward(block_rows, width, kv_heads, order, tokens_all, gain, weight, tables):
    length, _ = tokens_all.shape
    blocks = length // QUERY_ROWS
    wide = shape((kv_heads, length, LANES))
    return pl.pallas_call(
        functools.partial(attend_body, block_rows),
        out_shape=(
            shape((length, width)),
            shape((length, width)),
            wide,
            wide,
            shape((width // LANES * blocks, PAIR * QUERY_ROWS), jnp.float32),
            shape(tokens_all.shape),
        ),
        in_specs=[SMEM] + [VMEM] * 5,
        out_specs=(VMEM,) * 6,
        scratch_shapes=[pltpu.VMEM((kv_heads, LANES, length), jnp.bfloat16)],
        compiler_params=pltpu.CompilerParams(vmem_limit_bytes=48 << 20),
        cost_estimate=pl.CostEstimate(
            flops=3 * 10**10, bytes_accessed=10**7, transcendentals=10**7
        ),
    )(order, tokens_all, gain, weight, *tables)


def attend_back_body(
    block_rows,
    order,
    branch_all,
    output_weight,
    queries,
    keys,
    values,
    attended,
    log_totals,
    cosine,
    sine,
    grad_packed,
    grads,
    row_dots,
    keys_across,
    key_sums,
    value_sums,
):
    length, width = queries.shape
    kv_heads = keys.shape[0]
    pairs = width // LANES
    blocks = length // QUERY_ROWS
    per = QUERY_ROWS // block_rows

    def project(index, carry):
        place = pl.ds(pl.multiple_of(index * QUERY_ROWS, QUERY_ROWS), QUERY_ROWS)
        rows = rows_in_order(order, branch_all, index, block_rows)
        low = times_transposed(rows, output_weight[...]).astype(jnp.bfloat16)
        grads[place, :] = low
        dots = low.astype(jnp.float32) * rows_in_order(order, attended, index, block_rows).astype(
            jnp.float32
        )
        for pair in range(pairs):
            across = dots[:, pair * LANES : (pair + 1) * LANES].T
            sums = [
                jnp.sum(across[i * HEAD_DIM : (i + 1) * HEAD_DIM], axis=0, keepdims=True)
                for i in range(PAIR)
            ]
            row_dots[pl.ds(pair * blocks + index, 1), :] = jnp.concatenate(sums, axis=1)
        for head in range(kv_heads):
            keys_across[head, :, place] = keys[head, place, :].T
        return carry

    lax.fori_loop(0, blocks, project, 0)

    group = pairs // kv_heads

    def attend(kv_head, carry):
        key_sums[kv_head] = jnp.zeros(key_sums.shape[1:], jnp.float32)
        value_sums[kv_head] = jnp.zeros(value_sums.shape[1:], jnp.float32)
        for member in range(group):
            pair = kv_head * group + member
            lanes = pl.ds(pl.multiple_of(pair * LANES, LANES), LANES)
            for index in range(blocks):
                seen = (index + 1) * QUERY_ROWS
                place = slice(index * QUERY_ROWS, seen)
                rows = two_heads(queries[place, lanes])
                grad_rows = two_heads(grads[place, lanes])
                row = pl.ds(pair * blocks + index, 1)
                scores = times_transposed(keys[kv_head, :seen, :], rows)
                weights = jnp.exp(scores - log_totals[row, :])
                own = weights[seen - QUERY_ROWS :]
                own = jnp.where(later_key(own.shape), 0.0, own)
                if index:
                    weights = jnp.concatenate([weights[: seen - QUERY_ROWS], own], axis=0)
                else:
                    weights = own
                grad_probs = times_transposed(values[kv_head, :seen, :], grad_rows)
                grad_scores = (weights * (grad_probs - row_dots[row, :])).astype(jnp.bfloat16)
                value_sums[kv_head, :seen, :] += product(weights.astype(jnp.bfloat16), grad_rows)
                key_sums[kv_head, :seen, :] += product(grad_scores, rows)
                turned = product(keys_across[kv_head, :, :seen], grad_scores)
                turned = pick_heads(turned).T * (1.0 / math.sqrt(HEAD_DIM))
                turned = turn(turned, cosine[place, :], -sine[place, :]).astype(jnp.bfloat16)
                for i in range(per):
                    grad_packed[block_rows_at(order, index * per + i, block_rows), lanes] = turned[
                        i * block_rows : (i + 1) * block_rows
                    ]
        return carry

    lax.fori_loop(0, kv_heads, attend, 0)

    def finish(block, carry):
        place = pl.ds(pl.multiple_of(block * block_rows, block_rows), block_rows)
        target = block_rows_at(order, block, block_rows)

        def head_sum(head):
            if head < kv_heads:
                tile = key_sums[head, place, :]
            else:
                tile = value_sums[head - kv_heads, place, :]
            tile = tile + pltpu.roll(tile, HEAD_DIM, 1)
            if head < kv_heads:
                tile = turn(tile, cosine[place, :], -sine[place, :])
            return tile

        for tile in range(2 * kv_heads // PAIR):
            first, second = (head_sum(tile * PAIR), head_sum(tile * PAIR + 1))
            joined = jnp.where(low_lanes(first.shape, HEAD_DIM), first, second)
            start = width + tile * LANES
            grad_packed[target, start : start + LANES] = joined.astype(jnp.bfloat16)
        return carry

    lax.fori_loop(0, length // block_rows, finish, 0)


def attend_backward(
    block_rows, order, branch_all, output_weight, queries, keys, values, attended, log_totals, tables
):
    length, width = queries.shape
    kv_heads = keys.shape[0]
    return pl.pallas_call(
        functools.partial(attend_back_body, block_rows),
        out_shape=shape((length, width + 2 * kv_heads * HEAD_DIM)),
        in_specs=[SMEM] + [VMEM] * 9,
        out_specs=VMEM,
        scratch_shapes=[
            pltpu.VMEM((length, width), jnp.bfloat16),
            pltpu.VMEM(log_totals.shape, jnp.float32),
            pltpu.VMEM((kv_heads, LANES, length), jnp.bfloat16),
            pltpu.VMEM((kv_heads, length, LANES), jnp.float32),
            pltpu.VMEM((kv_heads, length, LANES), jnp.float32),
        ],
        compiler_params=pltpu.CompilerParams(vmem_limit_bytes=56 << 20),
        cost_estimate=pl.CostEstimate(
            flops=6 * 10**10, bytes_accessed=10**7, transcendentals=10**7
        ),
    )(
        order,
        branch_all,
        output_weight,
        queries,
        keys,
        values,
        attended,
        log_totals,
        *tables,
    )


def for_part(body):
    me = lax.axis_index("ctx")
    for part in range(4):

        @pl.when(me == part)
        def _(part=part):
            body(part)


def strided_columns(array, shards, part):
    span = array.shape[1] // (4 * shards)
    values = array[...].astype(jnp.float32)
    starts = [(shard * 4 + part) * span for shard in range(shards)]
    return jnp.concatenate([values[:, i : i + span] for i in starts], axis=1).astype(array.dtype)


def pack_hidden_body(shards, gate, up, packed):
    def body(part):
        width = packed.shape[1] // 2
        packed[:, :width] = strided_columns(gate, shards, part)
        packed[:, width:] = strided_columns(up, shards, part)

    for_part(body)


def pack_hidden(shards, gate, up):
    rows, width = gate.shape
    step = 64
    block = pl.BlockSpec((step, width), lambda i: (i, 0))
    return pl.pallas_call(
        functools.partial(pack_hidden_body, shards),
        grid=(rows // step,),
        out_shape=shape((rows, width // 2)),
        in_specs=[block, block],
        out_specs=pl.BlockSpec((step, width // 2), lambda i: (i, 0)),
        cost_estimate=pl.CostEstimate(flops=0, bytes_accessed=10**7, transcendentals=0),
        compiler_params=pltpu.CompilerParams(vmem_limit_bytes=24 << 20),
    )(gate, up)


def pack_attention_body(shards, query, key, value, output, packed):
    def body(part):
        width = query.shape[1] // 4
        rows = output.shape[0] // 4
        packed[:, :width] = strided_columns(query, shards, part)
        packed[:, width : width + KV_WIDTH] = key[...]
        packed[:, width + KV_WIDTH : width + 2 * KV_WIDTH] = value[...]
        for index in range(4):
            packed[index * rows : (index + 1) * rows, width + 2 * KV_WIDTH :] = output[
                part * rows : (part + 1) * rows, index * width : (index + 1) * width
            ]

    for_part(body)


def pack_attention(shards, query, key, value, output):
    rows, width = query.shape
    return pl.pallas_call(
        functools.partial(pack_attention_body, shards),
        out_shape=shape((rows, width // 2 + 2 * KV_WIDTH)),
        in_specs=[VMEM] * 4,
        out_specs=VMEM,
        cost_estimate=pl.CostEstimate(flops=0, bytes_accessed=10**7, transcendentals=0),
        compiler_params=pltpu.CompilerParams(vmem_limit_bytes=24 << 20),
    )(query, key, value, output)


def take_columns(matrix, outer, parts, index):
    rows, columns = matrix.shape
    pieces = matrix.reshape(rows, outer, parts, columns // (outer * parts))
    return lax.dynamic_index_in_dim(pieces, index, axis=2, keepdims=False).reshape(rows, -1)


def take_rows(matrix, parts, index):
    count = matrix.shape[0] // parts
    return lax.dynamic_slice_in_dim(matrix, index * count, count, axis=0)


def put_columns(gathered, outer):
    parts, rows, columns = gathered.shape
    return (
        gathered.reshape(parts, rows, outer, columns // outer)
        .transpose(1, 2, 0, 3)
        .reshape(rows, parts * columns)
    )


def gather_shards(array):
    return lax.all_gather(array, "fsdp", axis=0, tiled=True)


def scatter_shards(array):
    return lax.psum_scatter(
        array.astype(jnp.bfloat16), "fsdp", scatter_dimension=0, tiled=True
    )


def per_device(
    tokens,
    dealing,
    first_gain,
    query_weight,
    key_weight,
    value_weight,
    output_weight,
    second_gain,
    gate_weight,
    up_weight,
    down_weight,
    cotangent,
):
    shard_count = lax.axis_size("fsdp")
    part_count = lax.axis_size("ctx")
    ctx_index = lax.axis_index("ctx")
    row_count = tokens.shape[1]
    block_rows = row_count // 2
    seq_rows = row_count * part_count
    part_width = D // part_count
    dealt_heads = D // shard_count // part_count == HEAD_DIM and part_count == 4
    kv_heads = KV_HEADS if dealt_heads else max(1, KV_HEADS // part_count)
    kv_first = 0 if dealt_heads else ctx_index * KV_HEADS // part_count
    blocks = jnp.arange(2 * part_count, dtype=jnp.int32)
    order = jnp.sum(
        jnp.where(dealing[0][None, :] == blocks[:, None], blocks[None, :], 0), axis=1
    ).astype(jnp.int32)
    tables = rotary_tables(seq_rows)

    tie = lax.optimization_barrier
    gains = jnp.stack([first_gain, second_gain])
    key_value = jnp.concatenate([key_weight, value_weight], axis=1)
    if dealt_heads:
        height = D // shard_count // part_count
        packed = gather_shards(
            pack_attention(shard_count, query_weight, key_weight, value_weight, output_weight)
        )
        tokens_all, gains_all = start_gather(part_count, shard_count, 1, tokens[0], gains)
        tokens_all, gate_weight, up_weight, grad_out = tie(
            (tokens_all, gate_weight, up_weight, cotangent[0])
        )
        gate_up_part = gather_shards(pack_hidden(shard_count, gate_weight, up_weight))
        grad_out_parts = plane_gather(grad_out)
        output_part = (
            packed[:, part_width + 2 * KV_WIDTH :]
            .reshape(shard_count, part_count, height, part_width)
            .transpose(0, 2, 1, 3)
            .reshape(part_width, D)
        )
    else:
        tokens_all, gains_all = start_gather(part_count, shard_count, 1, tokens[0], gains)
        grad_out_all = lax.all_gather(cotangent[0], "ctx", axis=0, tiled=True)
        query_part = gather_shards(take_columns(query_weight, 1, part_count, ctx_index))
        output_part = take_rows(gather_shards(output_weight), part_count, ctx_index)
        key_value = gather_shards(key_value).reshape(D, 2, KV_HEADS, HEAD_DIM)
        key_value = lax.dynamic_slice_in_dim(key_value, kv_first, kv_heads, 2).reshape(D, -1)
        packed = jnp.concatenate([query_part, key_value], axis=1)
        gate_up_part = gather_shards(
            jnp.concatenate(
                [
                    take_columns(gate_weight, shard_count, part_count, ctx_index),
                    take_columns(up_weight, shard_count, part_count, ctx_index),
                ],
                axis=1,
            )
        )
    down_part = gather_shards(take_rows(down_weight, part_count, ctx_index))

    gains = gains_all.transpose(1, 0, 2).reshape(2, D).astype(jnp.float32)
    gain_first, gain_second = (gains[0:1], gains[1:2])
    attended, query_rot, key_rot, value_rows, log_totals, first_all = attend_forward(
        block_rows, part_width, kv_heads, order, tokens_all, gain_first, packed, tables
    )
    if dealt_heads:
        attended, *grad_out_corner = tie((attended, *grad_out_parts[3:]))
        grad_out_parts = (*grad_out_parts[:3], *grad_out_corner)
    residual_mid, second_all = middle_gather(
        part_count, 2, attended, output_part, tokens[0], gain_second
    )
    if dealt_heads:
        second_all, *grad_out_parts = tie((second_all, *grad_out_parts))
        grad_out_all = place_rows(grad_out_parts, jnp.bfloat16)

    gate_up, hidden = hidden_forward(second_all, gate_up_part)
    down_term = column_term(hidden, grad_out_all).astype(jnp.bfloat16)
    down_part, down_term = tie((down_part, down_term))
    down_piece = scatter_shards(down_term)
    output_partial = product(hidden, down_part).astype(jnp.bfloat16)
    relayed = plane_relay(output_partial)
    grad_out_all, output_partial = tie((grad_out_all, output_partial))
    grad_gate_up = hidden_backward(grad_out_all, down_part, gate_up)
    gate_up_term = column_term(second_all, grad_gate_up).astype(jnp.bfloat16)
    grad_gate_up, gate_up_term, *relayed = tie((grad_gate_up, gate_up_term, *relayed))
    gate_up_piece = scatter_shards(gate_up_term)
    last = plane_last(output_partial, relayed)
    grad_mid, second_gain_part, branch_all = middle_back(
        part_count, 3, grad_gate_up, gate_up_part, residual_mid, gain_second, cotangent[0]
    )
    branch_all, down_piece, *last = tie((branch_all, down_piece, *last))
    block_output = (residual_mid + plane_scatter(output_partial, relayed, last)).astype(
        jnp.bfloat16
    )
    if dealt_heads:
        down_parts = plane_gather(down_piece)

    grad_packed = attend_backward(
        block_rows,
        order,
        branch_all,
        output_part,
        query_rot,
        key_rot,
        value_rows,
        attended,
        log_totals,
        tables,
    )
    if dealt_heads:
        packed_term = attention_grads(shard_count, first_all, grad_packed, attended, branch_all)
        grad_packed, packed_term, *down_parts = tie((grad_packed, packed_term, *down_parts))
        packed_piece = scatter_shards(packed_term)
    grad_input, gain_shard = input_back(
        part_count,
        shard_count,
        4,
        grad_packed,
        packed,
        tokens[0],
        gain_first,
        grad_mid,
        second_gain_part,
    )
    if dealt_heads:
        grad_input, packed_piece = tie((grad_input, packed_piece))
        gate_shard, up_shard = place_hidden(shard_count, plane_gather(gate_up_piece))
        down_shard = place_rows(down_parts, jnp.float32)
        query_shard, key_shard, value_shard, output_shard = place_attention(
            shard_count, plane_gather(packed_piece)
        )
    else:

        def gather_columns(piece, outer):
            return put_columns(lax.all_gather(piece, "ctx", axis=0), outer).astype(jnp.float32)

        width = FF // part_count
        gate_shard = gather_columns(gate_up_piece[:, :width], shard_count)
        up_shard = gather_columns(gate_up_piece[:, width:], shard_count)
        down_shard = lax.all_gather(down_piece, "ctx", axis=0, tiled=True).astype(jnp.float32)
        grad_query, grad_key_value = (grad_packed[:, :part_width], grad_packed[:, part_width:])
        query_piece = scatter_shards(column_term(first_all, grad_query))
        query_shard = gather_columns(query_piece, 1)
        key_value_piece = scatter_shards(column_term(first_all, grad_key_value))
        output_term = column_term(attended, branch_all)
        spread = jnp.zeros((D, D), jnp.float32)
        spread = lax.dynamic_update_slice_in_dim(
            spread, output_term, ctx_index * output_term.shape[0], 0
        )
        output_shard = lax.psum(scatter_shards(spread), "ctx").astype(jnp.float32)
        wide = jnp.zeros((D // shard_count, 2, KV_HEADS, HEAD_DIM), jnp.bfloat16)
        wide = lax.dynamic_update_slice_in_dim(
            wide, key_value_piece.reshape(-1, 2, kv_heads, HEAD_DIM), kv_first, 2
        )
        key_value_shard = lax.psum(wide.reshape(-1, 2 * KV_WIDTH), "ctx").astype(jnp.float32)
        key_shard, value_shard = (key_value_shard[:, :KV_WIDTH], key_value_shard[:, KV_WIDTH:])
    return (
        block_output[None],
        grad_input[None],
        gain_shard[0],
        query_shard,
        key_shard,
        value_shard,
        output_shard,
        gain_shard[1],
        gate_shard,
        up_shard,
        down_shard,
    )


def solution(mesh):
    in_specs = (
        P("fsdp", "ctx", None),
        P("fsdp", None),
        P("fsdp"),
        P("fsdp", None),
        P("fsdp", None),
        P("fsdp", None),
        P("fsdp", None),
        P("fsdp"),
        P("fsdp", None),
        P("fsdp", None),
        P("fsdp", None),
        P("fsdp", "ctx", None),
    )
    out_specs = (
        P("fsdp", "ctx", None),
        P("fsdp", "ctx", None),
        P("fsdp"),
        P("fsdp", None),
        P("fsdp", None),
        P("fsdp", None),
        P("fsdp", None),
        P("fsdp"),
        P("fsdp", None),
        P("fsdp", None),
        P("fsdp", None),
    )
    return jax.shard_map(
        per_device, mesh=mesh, in_specs=in_specs, out_specs=out_specs, check_vma=False
    )
```

```python
import functools
import math

import jax
import jax.numpy as jnp
from jax import lax
from jax.experimental import pallas as pl
from jax.experimental.pallas import tpu as pltpu
from jax.sharding import PartitionSpec as P

D = 2048
FF = 5632
HEADS = 32
KV_HEADS = 4
HEAD_DIM = 64
KV_WIDTH = 256


epsilon = 1e-05


MESH = pl.DeviceIdType.MESH
VMEM = pl.BlockSpec(memory_space=pltpu.VMEM)
SMEM = pl.BlockSpec(memory_space=pltpu.SMEM)
HBM = pl.BlockSpec(memory_space=pltpu.HBM)
LANES = 128
PAIR = LANES // HEAD_DIM
QUERY_ROWS = 256
VMEM_MEGABYTES = 60


def shape(dims, kind=jnp.bfloat16):
    return jax.ShapeDtypeStruct(dims, kind)


def norm_parts(values):
    inverse = lax.rsqrt(jnp.mean(values * values, axis=-1, keepdims=True) + epsilon)
    return (values * inverse, inverse)


def norm_back(gradient, normed, inverse):
    return inverse * (gradient - normed * jnp.mean(gradient * normed, axis=-1, keepdims=True))


def product(left_side, right_side):
    return jnp.dot(left_side, right_side, preferred_element_type=jnp.float32)


def times_transposed(left_side, right_side):
    return lax.dot_general(
        left_side, right_side, (((1,), (1,)), ((), ())), preferred_element_type=jnp.float32
    )


def column_term(source, gradient):
    return lax.dot_general(
        source, gradient, (((0,), (0,)), ((), ())), preferred_element_type=jnp.float32
    )


STRIP = 32
PIECES = 4


def plane_places():
    me = lax.axis_index("ctx")
    return (me, me + 1 - 2 * lax.rem(me, 2), lax.rem(me + 2, 4), 3 - me)


def signal(barrier, **place):
    pl.semaphore_signal(barrier, inc=1, device_id=place, device_id_type=MESH)


def meet(count, shards=1):
    me = lax.axis_index("ctx")
    barrier = pltpu.get_barrier_semaphore()
    for step in range(1, count):
        signal(barrier, ctx=lax.rem(me + step, count))
    for step in range(1, shards):
        signal(barrier, fsdp=lax.rem(lax.axis_index("fsdp") + step, shards))
    pl.semaphore_wait(barrier, count - 1 + shards - 1)


def remote(source, target, send_sem, recv_sem, **place):
    copy = pltpu.make_async_remote_copy(
        src_ref=source,
        dst_ref=target,
        send_sem=send_sem,
        recv_sem=recv_sem,
        device_id=place,
        device_id_type=MESH,
    )
    copy.start()
    return copy


def gather_sems(count):
    sends = 3 if count == 4 else count - 1
    return [
        pltpu.SemaphoreType.DMA((PIECES,)),
        pltpu.SemaphoreType.DMA((sends, PIECES)),
        pltpu.SemaphoreType.DMA((sends, PIECES)),
    ]


class RowGather:
    def __init__(self, count, own, out, sems):
        self.count, self.own, self.out = (count, own, out)
        self.local_sem, self.send_sem, self.recv_sem = sems
        self.size = own.shape[0] // PIECES
        self.copies = [[] for _ in range(PIECES)]
        self.relays = []

    def place(self, owner, piece):
        start = owner * self.own.shape[0] + piece * self.size
        return self.out.at[pl.ds(pl.multiple_of(start, self.size), self.size)]

    def send(self, piece):
        me = lax.axis_index("ctx")
        source = self.own.at[pl.ds(piece * self.size, self.size)]
        target = self.place(me, piece)
        if self.count == 4:
            _, across, along, _ = plane_places()
            peers = (across, along)
        else:
            peers = [lax.rem(me + step, self.count) for step in range(1, self.count)]
        for index, peer in enumerate(peers):
            self.copies[piece].append(
                remote(
                    source,
                    target,
                    self.send_sem.at[index, piece],
                    self.recv_sem.at[index, piece],
                    ctx=peer,
                )
            )
        local = pltpu.make_async_copy(source, target, self.local_sem.at[piece])
        local.start()
        self.copies[piece].append(local)

    def finish(self):
        self.relay()
        self.drain()

    def relay(self, pieces=(0, PIECES // 2, 1, PIECES // 2 + 1)):
        relays = self.relays
        if self.count != 4:
            return
        _, across, along, _ = plane_places()
        for piece in pieces:
            first = piece < PIECES // 2
            came, left = (0, 1) if first else (1, 0)
            owner, peer = (across, along) if first else (along, across)
            self.copies[piece][came].wait_recv()
            block = self.place(owner, piece)
            relays.append(
                remote(
                    block, block, self.send_sem.at[2, piece], self.recv_sem.at[2, piece], ctx=peer
                )
            )

    def drain(self):
        if self.count != 4:
            for copies in self.copies:
                for copy in copies:
                    copy.wait()
            return
        for piece in range(PIECES):
            to_across, to_along, local = self.copies[piece]
            (to_along if piece < PIECES // 2 else to_across).wait_recv()
            to_across.wait_send()
            to_along.wait_send()
            local.wait()
        for relay in self.relays:
            relay.wait()


CHUNKS = 2


def line_sems(shards):
    hops = shards // 2 - 1
    return [
        pltpu.SemaphoreType.DMA,
        pltpu.SemaphoreType.DMA((2 * hops, CHUNKS)),
        pltpu.SemaphoreType.DMA((2 * hops, CHUNKS)),
        pltpu.SemaphoreType.DMA((2 * hops + 1, CHUNKS)),
        pltpu.SemaphoreType.DMA((2 * hops + 1, CHUNKS)),
    ]


class LineGather:
    def __init__(self, shards, own, out, sems):
        self.own, self.out = (own, out)
        self.local_sem, self.send_sem, self.recv_sem, self.core_send, self.core_recv = sems
        self.me = lax.axis_index("fsdp")
        self.hops = shards // 2 - 1
        self.chip = self.me // 2
        self.twin = self.me + 1 - 2 * lax.rem(self.me, 2)
        self.size = own.shape[0] // CHUNKS

    def block(self, owner, chunk):
        start = owner * self.own.shape[0] + chunk * self.size
        return self.out.at[pl.ds(pl.multiple_of(start, self.size), self.size)]

    def copy(self, distance, way, chunk, sems, index, peer):
        owner = self.me - 2 * (1 - 2 * way) * distance
        target = self.block(owner, chunk)
        part = pl.ds(chunk * self.size, self.size)
        send_sem, recv_sem = sems
        return pltpu.make_async_remote_copy(
            src_ref=self.own.at[part] if distance == 0 else target,
            dst_ref=target,
            send_sem=send_sem.at[index, chunk],
            recv_sem=recv_sem.at[index, chunk],
            device_id={"fsdp": peer},
            device_id_type=MESH,
        )

    def hop(self, way, distance, chunk):
        sems = (self.send_sem, self.recv_sem)
        peer = self.me + 2 * (1 - 2 * way)
        return self.copy(distance, way, chunk, sems, way * self.hops + distance, peer)

    def cross(self, way, distance, chunk):
        index = distance if way == 0 else self.hops + distance
        sems = (self.core_send, self.core_recv)
        return self.copy(distance, way, chunk, sems, index, self.twin)

    def can_send(self, way):
        return self.chip < self.hops if way == 0 else self.chip > 0

    def behind(self, way, distance):
        return self.chip >= distance if way == 0 else self.chip + distance <= self.hops

    def local(self):
        rows = self.own.shape[0]
        target = self.out.at[pl.ds(pl.multiple_of(self.me * rows, rows), rows)]
        return pltpu.make_async_copy(self.own, target, self.local_sem)

    def start(self):
        for chunk in range(CHUNKS):
            for way in (0, 1):
                pl.when(self.can_send(way))(
                    lambda way=way, chunk=chunk: self.hop(way, 0, chunk).start()
                )
        for chunk in range(CHUNKS):
            self.cross(0, 0, chunk).start()
        self.local().start()

    def step(self, distance, chunk):
        for way in (0, 1):

            @pl.when(self.behind(way, distance))
            def _(way=way):
                self.hop(way, distance - 1, chunk).wait_recv()
                if distance < self.hops:
                    pl.when(self.can_send(way))(lambda: self.hop(way, distance, chunk).start())
                self.cross(way, distance, chunk).start()

    def drain(self):
        for chunk in range(CHUNKS):
            for way in (0, 1):
                for distance in range(self.hops):
                    here = jnp.logical_and(self.can_send(way), self.behind(way, distance))
                    pl.when(here)(
                        lambda way=way, d=distance, chunk=chunk: self.hop(way, d, chunk).wait_send()
                    )
                for distance in range(1, self.hops + 1):
                    pl.when(self.behind(way, distance))(
                        lambda way=way, d=distance, chunk=chunk: self.cross(way, d, chunk).wait()
                    )
            self.cross(0, 0, chunk).wait()
        self.local().wait()


TILE = 512


def begin(source, target, sem):
    copy = pltpu.make_async_copy(source, target, sem)
    copy.start()
    return copy


class Scatter:
    def __init__(self, count, left, right, transposed, refs):
        self.count, self.transposed = (count, transposed)
        self.left_buf, self.right_buf, self.load_sem, *refs = refs
        self.send_buf, self.recv_buf, self.kept, self.total, self.send_sem, self.recv_sem = refs
        self.rows, self.width = self.total.shape
        self.tiles = self.width // TILE
        self.loads = {}
        owners = self.owners()
        depth = self.left_buf.shape[1]
        self.load_left(left, owners[0], 0)
        for tile in range(self.tiles):
            columns = pl.ds(tile * TILE, TILE)
            if transposed:
                place = (columns, pl.ds(0, depth))
                source, target = (right.at[place], self.right_buf.at[columns])
            else:
                source, target = (right.at[:, columns], self.right_buf.at[:, columns])
            self.loads["tile", tile] = begin(source, target, self.load_sem.at[count + tile])
        for index in range(1, count):
            self.load_left(left, owners[index], index)

    def owners(self):
        me = lax.axis_index("ctx")
        if self.count != 4:
            return [lax.rem(me + step, self.count) for step in range(1, self.count)] + [me]
        _, across, along, corner = plane_places()
        return [corner, across, along, me]

    def block_rows(self, owner):
        return pl.ds(pl.multiple_of(owner * self.rows, self.rows), self.rows)

    def load_left(self, left, owner, index):
        rows = self.block_rows(owner)
        self.loads["left", index] = begin(
            left.at[rows], self.left_buf.at[rows], self.load_sem.at[index]
        )

    def tile(self, owner, columns):
        piece = self.left_buf[self.block_rows(owner), :]
        if self.transposed:
            return times_transposed(piece, self.right_buf[columns, :])
        return product(piece, self.right_buf[:, columns])

    def block(self, index, store):
        owner = self.owners()[index]
        self.loads["left", index].wait()

        def column(tile, carry):
            columns = pl.ds(pl.multiple_of(tile * TILE, TILE), TILE)
            store(columns, self.tile(owner, columns))
            return carry

        lax.fori_loop(0, self.tiles, column, 0)

    def send(self, slot, part, columns, sem, peer):
        return remote(
            self.send_buf.at[slot, part, columns],
            self.recv_buf.at[slot, part, columns],
            self.send_sem.at[sem],
            self.recv_sem.at[sem],
            ctx=peer,
        )

    def store_own(self, columns, value):
        self.total[:, columns] = value

    def run(self):
        if self.count == 4:
            self.run_relayed()
        else:
            self.run_direct()

    def run_direct(self):
        for tile in range(self.tiles):
            self.loads["tile", tile].wait()
        copies = []
        everything = (pl.ds(0, self.rows), pl.ds(0, self.width))
        for index, owner in enumerate(self.owners()[:-1]):

            def store_sent(columns, value, index=index):
                self.send_buf[index, :, columns] = value.astype(self.send_buf.dtype)

            self.block(index, store_sent)
            copies.append(self.send(index, *everything, index, owner))
        self.block(self.count - 1, self.store_own)
        self.relays, self.copies = ([], copies)

    def run_relayed(self):
        corner, across, along, me = self.owners()
        send_buf, kept, tiles = (self.send_buf, self.kept, self.tiles)
        half = self.rows // 2
        low, high = (pl.ds(0, half), pl.ds(half, half))
        whole = pl.ds(0, self.width)
        relays = []
        self.loads["left", 0].wait()
        for tile in range(tiles):
            columns = pl.ds(tile * TILE, TILE)
            self.loads["tile", tile].wait()
            send_buf[0, :, columns] = self.tile(corner, columns).astype(send_buf.dtype)
            relays.append(
                (
                    self.send(0, low, columns, tile, across),
                    self.send(0, high, columns, tiles + tile, along),
                )
            )

        def store_across(columns, value):
            send_buf[1, low, columns] = value[:half].astype(send_buf.dtype)
            kept[high, columns] = value[half:]

        def store_along(columns, value):
            send_buf[1, high, columns] = value[half:].astype(send_buf.dtype)
            kept[low, columns] = value[:half]

        self.block(1, store_across)
        copies = [self.send(1, low, whole, 4 * tiles, across)]
        self.block(2, store_along)
        copies.append(self.send(1, high, whole, 4 * tiles + 1, along))
        self.block(3, self.store_own)
        for tile in range(tiles):
            columns = pl.ds(tile * TILE, TILE)
            for side, peer in ((0, along), (1, across)):
                relays[tile][side].wait_recv()
                part = (low, high)[side]

                def add(where, columns=columns):
                    value = kept[where, columns] + self.recv_buf[0, where, columns].astype(
                        jnp.float32
                    )
                    send_buf[2, where, columns] = value.astype(send_buf.dtype)

                for_strips(side * half, half, add)
                sem = (2 + side) * tiles + tile
                copies.append(self.send(2, part, columns, sem, peer))
        self.relays, self.copies = (relays, copies)

    def finish(self):
        for pair in self.relays:
            for copy in pair:
                copy.wait_send()
        for copy in self.copies:
            copy.wait()


def scatter_scratch(count, rows, width, left, right, transposed, depth):
    slots = 3 if count == 4 else count - 1
    sems = 4 * (width // TILE) + 2 if count == 4 else count - 1
    return [
        pltpu.VMEM(left.shape, jnp.bfloat16),
        pltpu.VMEM((width, depth) if transposed else (depth, width), jnp.bfloat16),
        pltpu.SemaphoreType.DMA((count + width // TILE,)),
        pltpu.VMEM((slots, rows, width), jnp.bfloat16),
        pltpu.VMEM((slots, rows, width), jnp.bfloat16),
        pltpu.VMEM((rows, width) if count == 4 else (8, LANES), jnp.float32),
        pltpu.VMEM((rows, width), jnp.float32),
        pltpu.SemaphoreType.DMA((sems,)),
        pltpu.SemaphoreType.DMA((sems,)),
    ]


SCATTER_REFS = 9


def side_loads(sources, refs):
    *targets, sem = refs
    return [begin(source, target, sem.at[i]) for i, (source, target) in enumerate(zip(sources, targets))]


def side_scratch(*arrays):
    return [pltpu.VMEM(a.shape, a.dtype) for a in arrays] + [
        pltpu.SemaphoreType.DMA((len(arrays),))
    ]


def received(count, recv_buf, total, rows):
    value = total[rows, :]
    for slot in (1, 2) if count == 4 else range(count - 1):
        value = value + recv_buf[slot, rows, :].astype(jnp.float32)
    return value


def for_strips(first, rows, body):
    def strip(index, carry):
        body(pl.ds(pl.multiple_of(first + index * STRIP, STRIP), STRIP))
        return carry

    lax.fori_loop(0, rows // STRIP, strip, 0)


def call_plane(body, ident, outs, out_specs, in_specs, scratch, flops, megabytes, args):
    return pl.pallas_call(
        body,
        out_shape=outs,
        in_specs=in_specs,
        out_specs=out_specs,
        scratch_shapes=scratch,
        compiler_params=pltpu.CompilerParams(
            collective_id=ident, has_side_effects=True, vmem_limit_bytes=megabytes << 20
        ),
        cost_estimate=pl.CostEstimate(
            flops=flops, bytes_accessed=flops // 300, transcendentals=0
        ),
    )(*args)


def for_part(body):
    me = lax.axis_index("ctx")
    for part in range(4):

        @pl.when(me == part)
        def _(part=part):
            body(part)


def strided_columns(values, shards, part):
    span = values.shape[1] // (4 * shards)
    starts = [(shard * 4 + part) * span for shard in range(shards)]
    wide = values.astype(jnp.float32)
    return jnp.concatenate([wide[:, i : i + span] for i in starts], axis=1).astype(values.dtype)


def pack_attention(shards, query, key, value, output, packed):
    def body(part):
        width = query.shape[1] // 4
        rows = output.shape[0] // 4
        packed[:, :width] = strided_columns(query[...], shards, part)
        packed[:, width : width + KV_WIDTH] = key[...]
        packed[:, width + KV_WIDTH : width + 2 * KV_WIDTH] = value[...]
        for index in range(4):
            packed[index * rows : (index + 1) * rows, width + 2 * KV_WIDTH :] = output[
                part * rows : (part + 1) * rows, index * width : (index + 1) * width
            ]

    for_part(body)


def pack_hidden(shards, gate, up, packed):
    def body(part):
        width = packed.shape[1] // 2

        def strip(where):
            packed[where, :width] = strided_columns(gate[where, :], shards, part)
            packed[where, width:] = strided_columns(up[where, :], shards, part)

        for_strips(0, packed.shape[0], strip)

    for_part(body)


def write_tables(cosine, sine):
    half = HEAD_DIM // 2

    def strip(where):
        dims = (STRIP, LANES)
        lane = lax.broadcasted_iota(jnp.int32, dims, 1)
        place = lax.broadcasted_iota(jnp.int32, dims, 0) + where.start
        index = lax.rem(lane, half).astype(jnp.float32)
        frequency = jnp.exp(-math.log(10000.0) * index * (2.0 / HEAD_DIM))
        angles = place.astype(jnp.float32) * frequency
        cosine[where, :] = jnp.cos(angles)
        sine[where, :] = jnp.where(low_lanes(dims, half), -jnp.sin(angles), jnp.sin(angles))

    for_strips(0, cosine.shape[0], strip)


def start_body(count, shards, tokens, first_gain, second_gain, *refs):
    if count == 4:
        weights, refs = (refs[:6], refs[6:])
    tokens_all, gain_first, gain_second, cosine, sine, *refs = refs
    if count == 4:
        weights_all, packed_hidden, *refs = refs
    gains, gains_all, gain_send, gain_recv, *refs = refs
    meet(count, shards)
    first = RowGather(count, tokens, tokens_all, refs[:3])
    half = PIECES // 2
    first.send(0)
    first.send(half)
    if count == 4:
        packed, gate, up, load_sem, *line_refs = refs[3:]
        loads = [
            pltpu.make_async_copy(weights[4 + i], target, load_sem.at[i])
            for i, target in enumerate((gate, up))
        ]
        for load in loads:
            load.start()
        pack_attention(shards, *weights[:4], packed)
        line = LineGather(shards, packed, weights_all, line_refs)
        line.start()
    me = lax.axis_index("fsdp")
    gains[0:1, :] = first_gain[...]
    gains[1:2, :] = second_gain[...]
    gains_all[me] = gains[...]
    copies = []
    for step in range(1, shards):
        copies.append(
            remote(
                gains,
                gains_all.at[me],
                gain_send.at[step - 1],
                gain_recv.at[step - 1],
                fsdp=lax.rem(me + step, shards),
            )
        )
    if count != 4:
        write_tables(cosine, sine)
        first.send(1)
        first.send(half + 1)
        first.finish()
    else:
        steps = [(d, c) for d in range(1, line.hops + 1) for c in range(CHUNKS)]
        line.step(*steps[0])
        first.relay((0, half))
        first.send(1)
        first.send(half + 1)
        write_tables(cosine, sine)
        for step in steps[1:3]:
            line.step(*step)
        for load in loads:
            load.wait()
        pack_hidden(shards, gate, up, packed_hidden)
        first.relay((1, half + 1))
        for step in steps[3:-1]:
            line.step(*step)
        first.drain()
    for copy in copies:
        copy.wait()
    span = gains.shape[1]
    for shard in range(shards):
        lanes = slice(shard * span, (shard + 1) * span)
        gain_first[:, lanes] = gains_all[shard, 0:1, :].astype(jnp.float32)
        gain_second[:, lanes] = gains_all[shard, 1:2, :].astype(jnp.float32)
    if count == 4:
        line.step(*steps[-1])
        line.drain()


def start_gather(count, shards, ident, tokens, first_gain, second_gain, *weights):
    rows, width = tokens.shape
    span = first_gain.shape[1]
    wide = shape((1, width), jnp.float32)
    table = shape((count * rows, LANES), jnp.float32)
    outs = [shape((count * rows, width)), wide, wide, table, table]
    out_specs = [HBM] + [VMEM] * 4
    in_specs = [HBM, VMEM, VMEM]
    scratch = [
        pltpu.VMEM((2, span), jnp.bfloat16),
        pltpu.VMEM((shards, 2, span), jnp.bfloat16),
        pltpu.SemaphoreType.DMA((shards - 1,)),
        pltpu.SemaphoreType.DMA((shards - 1,)),
    ] + gather_sems(count)
    if weights:
        height = weights[0].shape[0]
        packed = width // 2 + 2 * KV_WIDTH
        outs += [shape((shards * height, packed)), shape((height, FF // 2))]
        out_specs += [HBM, VMEM]
        in_specs += [VMEM] * 4 + [HBM] * 2
        scratch += [
            pltpu.VMEM((height, packed), jnp.bfloat16),
            pltpu.VMEM((height, FF), jnp.bfloat16),
            pltpu.VMEM((height, FF), jnp.bfloat16),
            pltpu.SemaphoreType.DMA((2,)),
        ] + line_sems(shards)
    return call_plane(
        functools.partial(start_body, count, shards),
        ident,
        tuple(outs),
        tuple(out_specs),
        in_specs,
        scratch,
        5 * 10**10,
        VMEM_MEGABYTES,
        (tokens, first_gain, second_gain, *weights),
    )


def strips_and_send(gather, strip):
    size = gather.size
    for piece in range(PIECES):
        for_strips(piece * size, size, strip)
        gather.send(piece)
    gather.finish()


def middle_body(count, attended, weight, tokens, gain, residual, second_all, own, *refs):
    scatter = Scatter(count, attended, weight, False, refs[:SCATTER_REFS])
    side = refs[SCATTER_REFS : SCATTER_REFS + 2]
    loads = side_loads([tokens], side)
    meet(count)
    scatter.run()
    scatter.finish()
    for load in loads:
        load.wait()

    def strip(where):
        values = side[0][where, :].astype(jnp.float32) + received(
            count, scatter.recv_buf, scatter.total, where
        )
        residual[where, :] = values
        normed, _ = norm_parts(values)
        own[where, :] = (normed * gain[...]).astype(jnp.bfloat16)

    strips_and_send(RowGather(count, own, second_all, refs[SCATTER_REFS + 2 :]), strip)


def middle_gather(count, ident, attended, weight, tokens, gain):
    rows, width = tokens.shape
    return call_plane(
        functools.partial(middle_body, count),
        ident,
        (shape((rows, width), jnp.float32), shape((count * rows, width))),
        (VMEM, HBM),
        [HBM] * 3 + [VMEM],
        [pltpu.VMEM((rows, width), jnp.bfloat16)]
        + scatter_scratch(count, rows, width, attended, weight, False, attended.shape[1])
        + side_scratch(tokens)
        + gather_sems(count),
        6 * 10**10,
        VMEM_MEGABYTES,
        (attended, weight, tokens, gain),
    )


def middle_back_body(
    count, grad_gate_up, gate_up_weight, residual, grad_out, gain, grad_mid, gain_part, branch_all, own,
    *refs
):
    scatter = Scatter(count, grad_gate_up, gate_up_weight, True, refs[:SCATTER_REFS])
    side = refs[SCATTER_REFS : SCATTER_REFS + 3]
    loads = side_loads([residual, grad_out], side)
    meet(count)
    scatter.run()
    scatter.finish()
    gain_part[...] = jnp.zeros_like(gain_part)
    for load in loads:
        load.wait()

    def strip(where):
        gradient = received(count, scatter.recv_buf, scatter.total, where)
        normed, inverse = norm_parts(side[0][where, :])
        gain_part[...] += jnp.sum(gradient * normed, axis=0, keepdims=True)
        values = side[1][where, :].astype(jnp.float32) + norm_back(
            gradient * gain[...], normed, inverse
        )
        grad_mid[where, :] = values
        own[where, :] = values.astype(jnp.bfloat16)

    strips_and_send(RowGather(count, own, branch_all, refs[SCATTER_REFS + 3 :]), strip)


def column_halves(array):
    rows, width = array.shape
    if width // 2 % LANES:
        return ((array[:, : width // 2], array[:, width // 2 :]), (VMEM, VMEM))
    specs = [pl.BlockSpec((rows, width // 2), lambda *index, side=side: (0, side)) for side in (0, 1)]
    return ((array, array), specs)


def middle_back(count, ident, grad_gate_up, gate_up_weight, residual, gain, grad_out):
    rows, width = residual.shape
    return call_plane(
        functools.partial(middle_back_body, count),
        ident,
        (
            shape((rows, width), jnp.float32),
            shape((1, width), jnp.float32),
            shape((count * rows, width)),
        ),
        (VMEM, VMEM, HBM),
        [HBM] * 4 + [VMEM],
        [pltpu.VMEM((rows, width), jnp.bfloat16)]
        + scatter_scratch(
            count, rows, width, grad_gate_up, gate_up_weight, True, grad_gate_up.shape[1]
        )
        + side_scratch(residual, grad_out)
        + gather_sems(count),
        6 * 10**10,
        VMEM_MEGABYTES,
        (grad_gate_up, gate_up_weight, residual, grad_out, gain),
    )


def input_back_body(
    count, shards, grad_packed, weight, tokens, grad_mid, piece, gain, second_part, grad_input, gain_sums,
    piece_all, gain_part, parts, part_recv, sums, sums_recv, part_send_sem, part_recv_sem, sums_send_sem,
    sums_recv_sem, *refs
):
    scatter = Scatter(count, grad_packed, weight, True, refs[:SCATTER_REFS])
    side = refs[SCATTER_REFS : SCATTER_REFS + 3]
    loads = side_loads([tokens, grad_mid], side)
    gather = RowGather(count, piece, piece_all, refs[SCATTER_REFS + 3 :])
    meet(count, shards)
    scatter.run()
    for part in range(PIECES):
        gather.send(part)
    scatter.finish()
    gain_part[...] = jnp.zeros_like(gain_part)
    for load in loads:
        load.wait()

    def strip(where):
        gradient = received(count, scatter.recv_buf, scatter.total, where)
        normed, inverse = norm_parts(side[0][where, :].astype(jnp.float32))
        gain_part[...] += jnp.sum(gradient * normed, axis=0, keepdims=True)
        values = side[1][where, :] + norm_back(gradient * gain[...], normed, inverse)
        grad_input[where, :] = values.astype(jnp.bfloat16)

    for_strips(0, grad_input.shape[0], strip)
    gather.relay()
    me = lax.axis_index("fsdp")
    span = parts.shape[2]
    for shard in range(shards):
        lanes = slice(shard * span, (shard + 1) * span)
        parts[shard, 0:1, :] = gain_part[:, lanes]
        parts[shard, 1:2, :] = second_part[:, lanes]
    copies = []
    for step in range(1, shards):
        peer = lax.rem(me + step, shards)
        copies.append(
            remote(
                parts.at[peer],
                part_recv.at[step - 1],
                part_send_sem.at[step - 1],
                part_recv_sem.at[step - 1],
                fsdp=peer,
            )
        )
    for copy in copies:
        copy.wait()
    value = parts[me]
    for step in range(1, shards):
        value = value + part_recv[step - 1]
    sums[...] = value
    copies = []
    for step in range(1, count):
        copies.append(
            remote(
                sums,
                sums_recv.at[step - 1],
                sums_send_sem.at[step - 1],
                sums_recv_sem.at[step - 1],
                ctx=lax.rem(lax.axis_index("ctx") + step, count),
            )
        )
    for copy in copies:
        copy.wait()
    for step in range(1, count):
        value = value + sums_recv[step - 1]
    gain_sums[...] = value
    gather.drain()


def input_back(
    count, shards, ident, grad_packed, weight, tokens, gain, grad_mid, second_part, piece
):
    rows, width = tokens.shape
    span = width // shards
    return call_plane(
        functools.partial(input_back_body, count, shards),
        ident,
        (
            shape((rows, width)),
            shape((2, span), jnp.float32),
            shape((count * piece.shape[0], piece.shape[1])),
        ),
        (VMEM, VMEM, HBM),
        [HBM] * 5 + [VMEM] * 2,
        [
            pltpu.VMEM((1, width), jnp.float32),
            pltpu.VMEM((shards, 2, span), jnp.float32),
            pltpu.VMEM((shards - 1, 2, span), jnp.float32),
            pltpu.VMEM((2, span), jnp.float32),
            pltpu.VMEM((count - 1, 2, span), jnp.float32),
            pltpu.SemaphoreType.DMA((shards - 1,)),
            pltpu.SemaphoreType.DMA((shards - 1,)),
            pltpu.SemaphoreType.DMA((count - 1,)),
            pltpu.SemaphoreType.DMA((count - 1,)),
        ]
        + scatter_scratch(count, rows, width, grad_packed, weight, True, grad_packed.shape[1])
        + side_scratch(tokens, grad_mid)
        + gather_sems(count),
        5 * 10**10,
        VMEM_MEGABYTES,
        (grad_packed, weight, tokens, grad_mid, piece, gain, second_part),
    )


def swap(array, along):
    pairs = [(i, (i + 2) % 4) if along else (i, i + 1 - 2 * (i % 2)) for i in range(4)]
    return lax.ppermute(array, "ctx", pairs)


def plane_near(array):
    return (array, swap(array, False), swap(array, True))


def plane_far(near):
    _, across, along = near
    half = across.shape[0] // 2
    return (*near, swap(across[:half], True), swap(along[half:], False))


def plane_gather(array):
    return plane_far(plane_near(array))


def take_half(partial, owner, side):
    rows = partial.shape[0] // lax.axis_size("ctx")
    half = rows // 2
    return lax.dynamic_slice_in_dim(partial, owner * rows + side * half, half, 0)


def plane_relay(partial):
    if lax.axis_size("ctx") != 4:
        return (partial,)
    me, across, along, corner = plane_places()
    take = functools.partial(take_half, partial)
    low = swap(jnp.stack([take(corner, 0), take(across, 0)]), False)
    high = swap(jnp.stack([take(corner, 1), take(along, 1)]), True)
    return (low, high)


def add_parts(first, second):
    return first.astype(jnp.float32) + second.astype(jnp.float32)


def plane_last(partial, relayed):
    if lax.axis_size("ctx") != 4:
        return (lax.psum_scatter(relayed[0], "ctx", scatter_dimension=0, tiled=True),)
    me, across, along, corner = plane_places()
    take = functools.partial(take_half, partial)
    low, high = relayed
    last_low = swap(add_parts(take(along, 0), low[0]).astype(jnp.bfloat16), True)
    last_high = swap(add_parts(take(across, 1), high[0]).astype(jnp.bfloat16), False)
    return (last_low, last_high)


def plane_scatter(partial, relayed, last):
    if lax.axis_size("ctx") != 4:
        return last[0].astype(jnp.float32)
    me = lax.axis_index("ctx")
    return jnp.concatenate(
        [
            add_parts(take_half(partial, me, side), relayed[side][1])
            + last[side].astype(jnp.float32)
            for side in (0, 1)
        ],
        axis=0,
    )


def hidden_body(rows, gate_weight, up_weight, gate_up, hidden, rows_across, hidden_across):
    width = hidden.shape[1]
    rows_across[...] = rows[...].T
    gate = product(rows[...], gate_weight[...])
    gate_up[:, :width] = gate
    upward = product(rows[...], up_weight[...])
    gate_up[:, width:] = upward
    low = (gate * jax.nn.sigmoid(gate) * upward).astype(jnp.bfloat16)
    hidden[...] = low
    hidden_across[...] = low.T


def hidden_forward(second_all, gate_up_weight):
    length, depth = second_all.shape
    width = gate_up_weight.shape[1] // 2
    (gate_weight, up_weight), specs = column_halves(gate_up_weight)
    step = QUERY_ROWS
    return pl.pallas_call(
        hidden_body,
        grid=(length // step,),
        out_shape=(
            shape((length, 2 * width), jnp.float32),
            shape((length, width)),
            shape((depth, length)),
            shape((width, length)),
        ),
        in_specs=[pl.BlockSpec((step, depth), lambda i: (i, 0))] + list(specs),
        out_specs=(
            pl.BlockSpec((step, 2 * width), lambda i: (i, 0)),
            pl.BlockSpec((step, width), lambda i: (i, 0)),
            pl.BlockSpec((depth, step), lambda i: (0, i)),
            pl.BlockSpec((width, step), lambda i: (0, i)),
        ),
        compiler_params=pltpu.CompilerParams(vmem_limit_bytes=VMEM_MEGABYTES << 20),
        cost_estimate=pl.CostEstimate(
            flops=4 * length * depth * width, bytes_accessed=3 * 10**7, transcendentals=10**6
        ),
    )(second_all, gate_weight, up_weight)


def hidden_back_body(grad_rows, down_weight, gate_up, hidden, grad_gate_up, partial):
    width = down_weight.shape[0]
    partial[...] = product(hidden[...], down_weight[...]).astype(jnp.bfloat16)
    grad_hidden = times_transposed(grad_rows[...], down_weight[...])
    gate, upward = (gate_up[:, :width], gate_up[:, width:])
    sigmoid_gate = jax.nn.sigmoid(gate)
    silu_gate = gate * sigmoid_gate
    grad_gate = grad_hidden * upward * sigmoid_gate * (1.0 + gate * (1.0 - sigmoid_gate))
    grad_gate_up[:, :width] = grad_gate.astype(jnp.bfloat16)
    grad_gate_up[:, width:] = (grad_hidden * silu_gate).astype(jnp.bfloat16)


def hidden_backward(grad_out_all, down_weight, gate_up, hidden):
    length, depth = grad_out_all.shape
    width = down_weight.shape[0]
    step = QUERY_ROWS
    return pl.pallas_call(
        hidden_back_body,
        grid=(length // step,),
        out_shape=(shape((length, 2 * width)), shape((length, depth))),
        in_specs=[
            pl.BlockSpec((step, depth), lambda i: (i, 0)),
            pl.BlockSpec((width, depth), lambda i: (0, 0)),
            pl.BlockSpec((step, 2 * width), lambda i: (i, 0)),
            pl.BlockSpec((step, width), lambda i: (i, 0)),
        ],
        out_specs=(
            pl.BlockSpec((step, 2 * width), lambda i: (i, 0)),
            pl.BlockSpec((step, depth), lambda i: (i, 0)),
        ),
        compiler_params=pltpu.CompilerParams(vmem_limit_bytes=VMEM_MEGABYTES << 20),
        cost_estimate=pl.CostEstimate(
            flops=4 * length * depth * width, bytes_accessed=3 * 10**7, transcendentals=10**6
        ),
    )(grad_out_all, down_weight, gate_up, hidden)


def meet_twin():
    me = lax.axis_index("fsdp")
    barrier = pltpu.get_barrier_semaphore()
    signal(barrier, fsdp=me + 1 - 2 * lax.rem(me, 2))
    pl.semaphore_wait(barrier, 1)


def shard_rows(array, shards, core):
    span = array.shape[0] // shards
    starts = [pl.multiple_of((2 * i + core) * span, 16) for i in range(shards // 2)]
    return jnp.concatenate([array[pl.ds(start, span), :] for start in starts], axis=0)


GRAD_TILE = 256


class CoreSum:
    def __init__(self, send_buf, recv_buf, send_sem, recv_sem):
        self.send_buf, self.recv_buf = (send_buf, recv_buf)
        self.send_sem, self.recv_sem = (send_sem, recv_sem)

    def copy(self, tile):
        me = lax.axis_index("fsdp")
        columns = pl.ds(pl.multiple_of(tile * GRAD_TILE, GRAD_TILE), GRAD_TILE)
        return pltpu.make_async_remote_copy(
            src_ref=self.send_buf.at[:, columns],
            dst_ref=self.recv_buf.at[:, columns],
            send_sem=self.send_sem.at[tile],
            recv_sem=self.recv_sem.at[tile],
            device_id={"fsdp": me + 1 - 2 * lax.rem(me, 2)},
            device_id_type=MESH,
        )


def column_tile(tile):
    return pl.ds(pl.multiple_of(tile * GRAD_TILE, GRAD_TILE), GRAD_TILE)


def core_grads_body(shards, across, gradient, *refs):
    *outs, half, send_buf, recv_buf, send_sem, recv_sem = refs
    core = lax.rem(lax.axis_index("fsdp"), 2)
    tiles = gradient.shape[1] // GRAD_TILE
    sums = CoreSum(send_buf, recv_buf, send_sem, recv_sem)
    half[...] = shard_rows(across, shards, 1 - core)
    meet_twin()

    def send(tile, carry):
        columns = column_tile(tile)
        send_buf[:, columns] = product(half[...], gradient[:, columns]).astype(jnp.bfloat16)
        sums.copy(tile).start()
        return carry

    lax.fori_loop(0, tiles, send, 0)
    half[...] = shard_rows(across, shards, core)

    def total(tile):
        columns = column_tile(tile)
        value = product(half[...], gradient[:, columns])
        sums.copy(tile).wait()
        return (value + recv_buf[:, columns].astype(jnp.float32)).astype(jnp.bfloat16)

    done = 0
    first = 0
    for out in outs:
        width = out.shape[1]
        whole = (first + width) // GRAD_TILE

        def keep(tile, carry, out=out, first=first):
            start = pl.multiple_of(tile * GRAD_TILE - first, LANES)
            out[:, pl.ds(start, GRAD_TILE)] = total(tile)
            return carry

        lax.fori_loop(done // GRAD_TILE, whole, keep, 0)
        done = whole * GRAD_TILE
        rest = first + width - done
        if rest and out is not outs[-1]:
            value = total(whole)
            out[:, width - rest :] = value[:, :rest]
            following = outs[outs.index(out) + 1]
            following[:, : GRAD_TILE - rest] = value[:, rest:]
            done += GRAD_TILE
        first += width


def core_grads(shards, ident, source, gradient, parts=1):
    depth, length = source.shape
    width = gradient.shape[1]
    tiles = width // GRAD_TILE
    return call_plane(
        functools.partial(core_grads_body, shards),
        ident,
        (shape((depth // 2, width // parts)),) * parts,
        (VMEM,) * parts,
        [VMEM] * 2,
        [
            pltpu.VMEM((depth // 2, length), jnp.bfloat16),
            pltpu.VMEM((depth // 2, width), jnp.bfloat16),
            pltpu.VMEM((depth // 2, width), jnp.bfloat16),
            pltpu.SemaphoreType.DMA((tiles,)),
            pltpu.SemaphoreType.DMA((tiles,)),
        ],
        2 * length * depth * width,
        VMEM_MEGABYTES,
        (source, gradient),
    )


def attention_grads_body(
    shards, across, gradient, heads, branch_all, out, half, outs, send_buf, recv_buf, send_sem, recv_sem
):
    core = lax.rem(lax.axis_index("fsdp"), 2)
    width = gradient.shape[1]
    tiles = width // GRAD_TILE
    total = out.shape[1] // GRAD_TILE
    part = out.shape[1] - width
    span = out.shape[0] // (shards // 2)
    height = HEAD_DIM
    sums = CoreSum(send_buf, recv_buf, send_sem, recv_sem)
    meet_twin()

    def heads_product(index, carry):
        columns = pl.ds(pl.multiple_of(index * 512, 512), 512)
        outs[:, columns] = product(heads[...], branch_all[:, columns])
        return carry

    lax.fori_loop(0, branch_all.shape[1] // 512, heads_product, 0)

    def pieces(side):
        for chip in range(shards // 2):
            rows = pl.ds(pl.multiple_of((2 * chip + side) * height, height), height)
            for index in range(span // height):
                start = chip * span + index * height
                yield slice(start, start + height), outs[rows, index * part : (index + 1) * part]

    for rows, value in pieces(1 - core):
        send_buf[rows, width:] = value.astype(jnp.bfloat16)
    for tile in range(tiles, total):
        sums.copy(tile).start()
    half[...] = shard_rows(across, shards, 1 - core)

    def send(tile, carry):
        columns = column_tile(tile)
        send_buf[:, columns] = product(half[...], gradient[:, columns]).astype(jnp.bfloat16)
        sums.copy(tile).start()
        return carry

    lax.fori_loop(0, tiles, send, 0)
    half[...] = shard_rows(across, shards, core)

    def keep(tile, carry):
        columns = column_tile(tile)
        value = product(half[...], gradient[:, columns])
        sums.copy(tile).wait()
        out[:, columns] = (value + recv_buf[:, columns].astype(jnp.float32)).astype(jnp.bfloat16)
        return carry

    lax.fori_loop(0, tiles, keep, 0)
    for tile in range(tiles, total):
        sums.copy(tile).wait()
    for rows, value in pieces(core):
        value = value + recv_buf[rows, width:].astype(jnp.float32)
        out[rows, width:] = value.astype(jnp.bfloat16)


def attention_grads(shards, ident, first_across, grad_packed, heads_across, branch_all):
    depth, length = first_across.shape
    heads = heads_across.shape[0]
    width = grad_packed.shape[1] + heads
    tiles = width // GRAD_TILE
    return call_plane(
        functools.partial(attention_grads_body, shards),
        ident,
        shape((depth // 2, width)),
        VMEM,
        [VMEM] * 4,
        [
            pltpu.VMEM((depth // 2, length), jnp.bfloat16),
            pltpu.VMEM((heads, branch_all.shape[1]), jnp.float32),
            pltpu.VMEM((depth // 2, width), jnp.bfloat16),
            pltpu.VMEM((depth // 2, width), jnp.bfloat16),
            pltpu.SemaphoreType.DMA((tiles,)),
            pltpu.SemaphoreType.DMA((tiles,)),
        ],
        2 * length * depth * width,
        VMEM_MEGABYTES,
        (first_across, grad_packed, heads_across, branch_all),
    )


def sort_parts(parts, sorted_parts, corner_low):
    me, across, along, corner = plane_places()
    own, from_across, from_along, low, high = parts
    sorted_parts[me] = own[...]
    sorted_parts[across] = from_across[...]
    sorted_parts[along] = from_along[...]

    @pl.when(corner_low)
    def _():
        sorted_parts[corner] = low[...]

    @pl.when(jnp.logical_not(corner_low))
    def _():
        sorted_parts[corner] = high[...]


def interleaved(values, shards):
    span = values[0].shape[1] // shards
    return jnp.concatenate(
        [v[:, shard * span : (shard + 1) * span] for shard in range(shards) for v in values], axis=1
    )


def place_sorted_body(shards, *refs):
    *parts, target = refs
    target[...] = interleaved([part[...].astype(jnp.float32) for part in parts], shards)


def place_sorted(shards, array):
    rows, width = (array.shape[0] // 4, array.shape[1])
    step = 64
    steps = rows // step
    return pl.pallas_call(
        functools.partial(place_sorted_body, shards),
        grid=(steps,),
        out_shape=shape((rows, 4 * width), jnp.float32),
        in_specs=[
            pl.BlockSpec((step, width), lambda i, part=part: (part * steps + i, 0))
            for part in range(4)
        ],
        out_specs=pl.BlockSpec((step, 4 * width), lambda i: (i, 0)),
        cost_estimate=pl.CostEstimate(flops=0, bytes_accessed=10**7, transcendentals=0),
        compiler_params=pltpu.CompilerParams(vmem_limit_bytes=VMEM_MEGABYTES << 20),
    )(array, array, array, array)


def place_hidden_body(shards, *refs):
    parts, (target, sorted_parts) = (refs[:5], refs[5:])
    steps = pl.num_programs(0)
    sort_parts(parts, sorted_parts, pl.program_id(0) < steps // 2)
    values = [sorted_parts[part].astype(jnp.float32) for part in range(sorted_parts.shape[0])]
    target[...] = interleaved(values, shards)


def place_hidden(shards, parts):
    rows, width = parts[0].shape
    step = 64
    half = rows // step // 2
    whole = pl.BlockSpec((step, width), lambda i: (i, 0))
    low = pl.BlockSpec((step, width), lambda i: (jnp.minimum(i, half - 1), 0))
    high = pl.BlockSpec((step, width), lambda i: (jnp.maximum(i - half, 0), 0))
    return pl.pallas_call(
        functools.partial(place_hidden_body, shards),
        grid=(rows // step,),
        out_shape=shape((rows, 4 * width), jnp.float32),
        in_specs=[whole, whole, whole, low, high],
        out_specs=pl.BlockSpec((step, 4 * width), lambda i: (i, 0)),
        scratch_shapes=[pltpu.VMEM((4, step, width), jnp.bfloat16)],
        cost_estimate=pl.CostEstimate(flops=0, bytes_accessed=10**7, transcendentals=0),
        compiler_params=pltpu.CompilerParams(vmem_limit_bytes=VMEM_MEGABYTES << 20),
    )(*parts)


def place_rows_body(own, from_across, from_along, low, high, out):
    me, across, along, corner = plane_places()
    rows = own.shape[0]

    def put(owner, offset, ref):
        size = ref.shape[0]
        start = pl.multiple_of(owner * rows + offset, 8)
        out[pl.ds(start, size), :] = ref[...].astype(out.dtype)

    put(me, 0, own)
    put(across, 0, from_across)
    put(along, 0, from_along)
    put(corner, 0, low)
    put(corner, rows // 2, high)


def place_rows(parts, kind):
    rows, width = parts[0].shape
    return pl.pallas_call(
        place_rows_body,
        out_shape=shape((4 * rows, width), kind),
        in_specs=[VMEM] * 5,
        out_specs=VMEM,
        cost_estimate=pl.CostEstimate(flops=0, bytes_accessed=10**7, transcendentals=0),
        compiler_params=pltpu.CompilerParams(vmem_limit_bytes=VMEM_MEGABYTES << 20),
    )(*parts)


def place_attention_body(shards, own, from_across, from_along, low, high, query, key, value, output, sorted_parts):
    me, across, along, corner = plane_places()
    rows = own.shape[0]
    sorted_parts[me] = own[...]
    sorted_parts[across] = from_across[...]
    sorted_parts[along] = from_along[...]
    sorted_parts[corner, : rows // 2] = low[...]
    sorted_parts[corner, rows // 2 :] = high[...]
    count = sorted_parts.shape[0]
    width = query.shape[1] // count
    span = width // shards
    values = [sorted_parts[part, :, :width].astype(jnp.float32) for part in range(count)]
    query[...] = jnp.concatenate(
        [
            values[part][:, shard * span : (shard + 1) * span]
            for shard in range(shards)
            for part in range(count)
        ],
        axis=1,
    )
    sums = None
    for part in range(count):
        term = sorted_parts[part, :, width : width + 2 * KV_WIDTH].astype(jnp.float32)
        sums = term if sums is None else sums + term
    key[...] = sums[:, :KV_WIDTH]
    value[...] = sums[:, KV_WIDTH:]
    height = rows // count
    for part in range(count):
        for index in range(count):
            tile = sorted_parts[part, index * height : (index + 1) * height, width + 2 * KV_WIDTH :]
            output[part * height : (part + 1) * height, index * width : (index + 1) * width] = (
                tile.astype(jnp.float32)
            )


def place_attention(shards, parts):
    rows, width = parts[0].shape
    wide = shape((rows, D), jnp.float32)
    narrow = shape((rows, KV_WIDTH), jnp.float32)
    return pl.pallas_call(
        functools.partial(place_attention_body, shards),
        out_shape=(wide, narrow, narrow, wide),
        in_specs=[VMEM] * 5,
        out_specs=(VMEM,) * 4,
        scratch_shapes=[pltpu.VMEM((4, rows, width), jnp.bfloat16)],
        cost_estimate=pl.CostEstimate(flops=0, bytes_accessed=10**7, transcendentals=0),
        compiler_params=pltpu.CompilerParams(vmem_limit_bytes=VMEM_MEGABYTES << 20),
    )(*parts)


def low_lanes(dims, size):
    return lax.rem(lax.broadcasted_iota(jnp.int32, dims, len(dims) - 1), 2 * size) < size


def turn(values, cosine, sine):
    half = HEAD_DIM // 2
    swapped = jnp.where(
        low_lanes(values.shape, half),
        pltpu.roll(values, LANES - half, 1),
        pltpu.roll(values, half, 1),
    )
    return values * cosine + swapped * sine


def two_heads(values):
    low = low_lanes(values.shape, HEAD_DIM)
    zero = jnp.zeros_like(values)
    return jnp.concatenate([jnp.where(low, values, zero), jnp.where(low, zero, values)], axis=0)


def pick_heads(values):
    rows = values.shape[1] // PAIR
    return jnp.concatenate(
        [values[:HEAD_DIM, :rows], values[HEAD_DIM:, rows:]], axis=0
    )


def later_key(dims):
    key = lax.broadcasted_iota(jnp.int32, dims, 0)
    query = lax.rem(lax.broadcasted_iota(jnp.int32, dims, 1), QUERY_ROWS)
    return key > query


def block_rows_at(order, block, rows):
    return pl.ds(pl.multiple_of(order[block] * rows, rows), rows)


def rows_in_order(order, source, index, rows):
    per = QUERY_ROWS // rows
    return jnp.concatenate(
        [source[block_rows_at(order, index * per + i, rows), :] for i in range(per)], axis=0
    )


def slots(dealing, order):
    for slot in range(dealing.shape[1]):
        order[dealing[0, slot]] = slot


def unpack_output(weight, output_part):
    width = output_part.shape[0]
    if weight.shape[1] <= width + 2 * KV_WIDTH:
        return
    parts = output_part.shape[1] // width
    shards = width // HEAD_DIM
    for shard in range(shards):
        for part in range(parts):
            start = (shard * parts + part) * HEAD_DIM
            output_part[
                shard * HEAD_DIM : (shard + 1) * HEAD_DIM, part * width : (part + 1) * width
            ] = weight[start : start + HEAD_DIM, weight.shape[1] - width :]


def attend_body(
    block_rows,
    dealing,
    tokens_all,
    gain,
    weight,
    cosine,
    sine,
    attended,
    queries,
    keys,
    values,
    log_totals,
    first_across,
    heads_across,
    output_part,
    values_across,
    order,
):
    slots(dealing, order)
    unpack_output(weight, output_part)
    length, width = queries.shape
    kv_heads = keys.shape[0]
    pairs = width // LANES
    blocks = length // QUERY_ROWS

    def project(index, carry):
        place = pl.ds(pl.multiple_of(index * QUERY_ROWS, QUERY_ROWS), QUERY_ROWS)
        normed, _ = norm_parts(
            rows_in_order(order, tokens_all, index, block_rows).astype(jnp.float32)
        )
        rows = (normed * gain[...]).astype(jnp.bfloat16)
        turned_rows = rows.T
        for i in range(QUERY_ROWS // block_rows):
            first_across[
                :, block_rows_at(order, index * (QUERY_ROWS // block_rows) + i, block_rows)
            ] = turned_rows[:, i * block_rows : (i + 1) * block_rows]
        cos_rows, sin_rows = (cosine[place, :], sine[place, :])
        projected = product(rows, weight[:, :width])
        for pair in range(pairs):
            lanes = slice(pair * LANES, (pair + 1) * LANES)
            turned = turn(projected[:, lanes], cos_rows, sin_rows).astype(jnp.bfloat16)
            queries[place, lanes] = turned * jnp.asarray(1.0 / math.sqrt(HEAD_DIM), jnp.bfloat16)
        projected = product(rows, weight[:, width : width + 2 * kv_heads * HEAD_DIM])
        for head in range(2 * kv_heads):
            tile = projected[:, head // PAIR * LANES : (head // PAIR + 1) * LANES]
            if head < kv_heads:
                tile = turn(tile, cos_rows, sin_rows)
            low = low_lanes(tile.shape, HEAD_DIM)
            moved = pltpu.roll(tile, HEAD_DIM, 1)
            both = jnp.where(low, tile, moved) if head % PAIR == 0 else jnp.where(low, moved, tile)
            if head < kv_heads:
                keys[head, place, :] = both.astype(jnp.bfloat16)
            else:
                values[head - kv_heads, place, :] = both.astype(jnp.bfloat16)
                values_across[head - kv_heads, :, place] = both.T.astype(jnp.bfloat16)
        return carry

    lax.fori_loop(0, blocks, project, 0)

    def attend(pair, carry):
        kv_head = pair // (pairs // kv_heads)
        lanes = pl.ds(pl.multiple_of(pair * LANES, LANES), LANES)
        for index in range(blocks):
            seen = (index + 1) * QUERY_ROWS
            rows = two_heads(queries[index * QUERY_ROWS : seen, lanes])
            scores = times_transposed(keys[kv_head, :seen, :], rows)
            own = scores[seen - QUERY_ROWS :]
            own = jnp.where(later_key(own.shape), -1e30, own)
            if index:
                scores = jnp.concatenate([scores[: seen - QUERY_ROWS], own], axis=0)
            else:
                scores = own
            largest = jnp.max(scores, axis=0, keepdims=True)
            exponent = jnp.exp(scores - largest)
            totals = jnp.sum(exponent, axis=0, keepdims=True)
            mixed = product(values_across[kv_head, :, :seen], exponent.astype(jnp.bfloat16))
            log_totals[pl.ds(pair * blocks + index, 1), :] = largest + jnp.log(totals)
            across = pick_heads(mixed / totals).astype(jnp.bfloat16)
            for i in range(QUERY_ROWS // block_rows):
                heads_across[
                    lanes, block_rows_at(order, index * (QUERY_ROWS // block_rows) + i, block_rows)
                ] = across[:, i * block_rows : (i + 1) * block_rows]
            mixed = across.T
            per = QUERY_ROWS // block_rows
            for i in range(per):
                attended[block_rows_at(order, index * per + i, block_rows), lanes] = mixed[
                    i * block_rows : (i + 1) * block_rows
                ]
        return carry

    lax.fori_loop(0, pairs, attend, 0)


def attend_forward(block_rows, width, kv_heads, dealing, tokens_all, gain, weight, tables):
    length, _ = tokens_all.shape
    blocks = length // QUERY_ROWS
    wide = shape((kv_heads, length, LANES))
    return pl.pallas_call(
        functools.partial(attend_body, block_rows),
        out_shape=(
            shape((length, width)),
            shape((length, width)),
            wide,
            wide,
            shape((width // LANES * blocks, PAIR * QUERY_ROWS), jnp.float32),
            shape(tokens_all.shape[::-1]),
            shape((width, length)),
            shape((width, tokens_all.shape[1])),
        ),
        in_specs=[SMEM] + [VMEM] * 5,
        out_specs=(VMEM,) * 8,
        scratch_shapes=[
            pltpu.VMEM((kv_heads, LANES, length), jnp.bfloat16),
            pltpu.SMEM((length // block_rows,), jnp.int32),
        ],
        compiler_params=pltpu.CompilerParams(vmem_limit_bytes=VMEM_MEGABYTES << 20),
        cost_estimate=pl.CostEstimate(
            flops=3 * 10**10, bytes_accessed=10**7, transcendentals=10**7
        ),
    )(dealing, tokens_all, gain, weight, *tables)


def attend_back_body(
    block_rows,
    dealing,
    branch_all,
    output_weight,
    queries,
    keys,
    values,
    attended,
    log_totals,
    cosine,
    sine,
    grad_packed,
    grads,
    row_dots,
    keys_across,
    key_sums,
    value_sums,
    order,
):
    slots(dealing, order)
    length, width = queries.shape
    kv_heads = keys.shape[0]
    pairs = width // LANES
    blocks = length // QUERY_ROWS
    per = QUERY_ROWS // block_rows

    def project(index, carry):
        place = pl.ds(pl.multiple_of(index * QUERY_ROWS, QUERY_ROWS), QUERY_ROWS)
        rows = rows_in_order(order, branch_all, index, block_rows)
        low = times_transposed(rows, output_weight[...]).astype(jnp.bfloat16)
        grads[place, :] = low
        dots = low.astype(jnp.float32) * rows_in_order(order, attended, index, block_rows).astype(
            jnp.float32
        )
        for pair in range(pairs):
            across = dots[:, pair * LANES : (pair + 1) * LANES].T
            sums = [
                jnp.sum(across[i * HEAD_DIM : (i + 1) * HEAD_DIM], axis=0, keepdims=True)
                for i in range(PAIR)
            ]
            row_dots[pl.ds(pair * blocks + index, 1), :] = jnp.concatenate(sums, axis=1)
        for head in range(kv_heads):
            keys_across[head, :, place] = keys[head, place, :].T
        return carry

    lax.fori_loop(0, blocks, project, 0)

    group = pairs // kv_heads

    def attend(kv_head, carry):
        key_sums[kv_head] = jnp.zeros(key_sums.shape[1:], jnp.float32)
        value_sums[kv_head] = jnp.zeros(value_sums.shape[1:], jnp.float32)
        for member in range(group):
            pair = kv_head * group + member
            lanes = pl.ds(pl.multiple_of(pair * LANES, LANES), LANES)
            for index in range(blocks):
                seen = (index + 1) * QUERY_ROWS
                place = slice(index * QUERY_ROWS, seen)
                rows = two_heads(queries[place, lanes])
                grad_rows = two_heads(grads[place, lanes])
                row = pl.ds(pair * blocks + index, 1)
                scores = times_transposed(keys[kv_head, :seen, :], rows)
                weights = jnp.exp(scores - log_totals[row, :])
                own = weights[seen - QUERY_ROWS :]
                own = jnp.where(later_key(own.shape), 0.0, own)
                if index:
                    weights = jnp.concatenate([weights[: seen - QUERY_ROWS], own], axis=0)
                else:
                    weights = own
                grad_probs = times_transposed(values[kv_head, :seen, :], grad_rows)
                grad_scores = (weights * (grad_probs - row_dots[row, :])).astype(jnp.bfloat16)
                value_sums[kv_head, :seen, :] += product(weights.astype(jnp.bfloat16), grad_rows)
                key_sums[kv_head, :seen, :] += product(grad_scores, rows)
                turned = product(keys_across[kv_head, :, :seen], grad_scores)
                turned = pick_heads(turned).T * (1.0 / math.sqrt(HEAD_DIM))
                turned = turn(turned, cosine[place, :], -sine[place, :]).astype(jnp.bfloat16)
                for i in range(per):
                    grad_packed[block_rows_at(order, index * per + i, block_rows), lanes] = turned[
                        i * block_rows : (i + 1) * block_rows
                    ]
        return carry

    lax.fori_loop(0, kv_heads, attend, 0)

    def finish(block, carry):
        place = pl.ds(pl.multiple_of(block * block_rows, block_rows), block_rows)
        target = block_rows_at(order, block, block_rows)

        def head_sum(head):
            if head < kv_heads:
                tile = key_sums[head, place, :]
            else:
                tile = value_sums[head - kv_heads, place, :]
            tile = tile + pltpu.roll(tile, HEAD_DIM, 1)
            if head < kv_heads:
                tile = turn(tile, cosine[place, :], -sine[place, :])
            return tile

        for tile in range(2 * kv_heads // PAIR):
            first, second = (head_sum(tile * PAIR), head_sum(tile * PAIR + 1))
            joined = jnp.where(low_lanes(first.shape, HEAD_DIM), first, second)
            start = width + tile * LANES
            grad_packed[target, start : start + LANES] = joined.astype(jnp.bfloat16)
        return carry

    lax.fori_loop(0, length // block_rows, finish, 0)


def attend_backward(
    block_rows, dealing, branch_all, output_weight, queries, keys, values, attended, log_totals, tables
):
    length, width = queries.shape
    kv_heads = keys.shape[0]
    return pl.pallas_call(
        functools.partial(attend_back_body, block_rows),
        out_shape=shape((length, width + 2 * kv_heads * HEAD_DIM)),
        in_specs=[SMEM] + [VMEM] * 9,
        out_specs=VMEM,
        scratch_shapes=[
            pltpu.VMEM((length, width), jnp.bfloat16),
            pltpu.VMEM(log_totals.shape, jnp.float32),
            pltpu.VMEM((kv_heads, LANES, length), jnp.bfloat16),
            pltpu.VMEM((kv_heads, length, LANES), jnp.float32),
            pltpu.VMEM((kv_heads, length, LANES), jnp.float32),
            pltpu.SMEM((length // block_rows,), jnp.int32),
        ],
        compiler_params=pltpu.CompilerParams(vmem_limit_bytes=VMEM_MEGABYTES << 20),
        cost_estimate=pl.CostEstimate(
            flops=6 * 10**10, bytes_accessed=10**7, transcendentals=10**7
        ),
    )(
        dealing,
        branch_all,
        output_weight,
        queries,
        keys,
        values,
        attended,
        log_totals,
        *tables,
    )


def take_columns(matrix, outer, parts, index):
    rows, columns = matrix.shape
    pieces = matrix.reshape(rows, outer, parts, columns // (outer * parts))
    return lax.dynamic_index_in_dim(pieces, index, axis=2, keepdims=False).reshape(rows, -1)


def take_rows(matrix, parts, index):
    count = matrix.shape[0] // parts
    return lax.dynamic_slice_in_dim(matrix, index * count, count, axis=0)


def put_columns(gathered, outer):
    parts, rows, columns = gathered.shape
    return (
        gathered.reshape(parts, rows, outer, columns // outer)
        .transpose(1, 2, 0, 3)
        .reshape(rows, parts * columns)
    )


def gather_shards(array):
    return lax.all_gather(array, "fsdp", axis=0, tiled=True)


def scatter_shards(array, by_core=False):
    shards = lax.axis_size("fsdp")
    groups = [list(range(core, shards, 2)) for core in range(2)] if by_core else None
    return lax.psum_scatter(
        array.astype(jnp.bfloat16),
        "fsdp",
        scatter_dimension=0,
        tiled=True,
        axis_index_groups=groups,
    )


def per_device(
    tokens,
    dealing,
    first_gain,
    query_weight,
    key_weight,
    value_weight,
    output_weight,
    second_gain,
    gate_weight,
    up_weight,
    down_weight,
    cotangent,
):
    shard_count = lax.axis_size("fsdp")
    part_count = lax.axis_size("ctx")
    ctx_index = lax.axis_index("ctx")
    row_count = tokens.shape[1]
    block_rows = row_count // 2
    seq_rows = row_count * part_count
    part_width = D // part_count
    dealt_heads = D // shard_count // part_count == HEAD_DIM and part_count == 4
    kv_heads = KV_HEADS if dealt_heads else max(1, KV_HEADS // part_count)
    kv_first = 0 if dealt_heads else ctx_index * KV_HEADS // part_count
    tie = lax.optimization_barrier
    start = functools.partial(
        start_gather, part_count, shard_count, 1, tokens[0], first_gain[None], second_gain[None]
    )
    if dealt_heads:
        tokens_all, gain_first, gain_second, cosine, sine, packed, packed_hidden = start(
            query_weight, key_weight, value_weight, output_weight, gate_weight, up_weight
        )
        packed, packed_hidden = tie((packed, packed_hidden))
        gate_up_part = gather_shards(packed_hidden)
    else:
        tokens_all, gain_first, gain_second, cosine, sine = start()
        grad_out_all = lax.all_gather(cotangent[0], "ctx", axis=0, tiled=True)
        query_part = gather_shards(take_columns(query_weight, 1, part_count, ctx_index))
        output_part = take_rows(gather_shards(output_weight), part_count, ctx_index)
        key_value = gather_shards(jnp.concatenate([key_weight, value_weight], axis=1))
        key_value = key_value.reshape(D, 2, KV_HEADS, HEAD_DIM)
        key_value = lax.dynamic_slice_in_dim(key_value, kv_first, kv_heads, 2).reshape(D, -1)
        packed = jnp.concatenate([query_part, key_value], axis=1)
        gate_up_part = gather_shards(
            jnp.concatenate(
                [
                    take_columns(gate_weight, shard_count, part_count, ctx_index),
                    take_columns(up_weight, shard_count, part_count, ctx_index),
                ],
                axis=1,
            )
        )
    tables = (cosine, sine)
    down_part = gather_shards(take_rows(down_weight, part_count, ctx_index))

    forward = attend_forward(
        block_rows, part_width, kv_heads, dealing, tokens_all, gain_first, packed, tables
    )
    attended, query_rot, key_rot, value_rows, log_totals, first_across, heads_across = forward[:7]
    if dealt_heads:
        output_part = forward[7]
    residual_mid, second_all = middle_gather(
        part_count, 2, attended, output_part, tokens[0], gain_second
    )
    if dealt_heads:
        second_all, grad_out = tie((second_all, cotangent[0]))
        near = plane_near(grad_out)

    gate_up, hidden, second_across, hidden_across = hidden_forward(second_all, gate_up_part)
    if dealt_heads:
        hidden_across, *near = tie((hidden_across, *near))
        grad_out_all = place_rows(plane_far(near), jnp.bfloat16)
        (down_term,) = core_grads(shard_count, 5, hidden_across, grad_out_all)
    else:
        down_term = column_term(hidden, grad_out_all)
    down_part, down_term = tie((down_part, down_term))
    down_piece = scatter_shards(down_term, dealt_heads)
    grad_gate_up, output_partial = hidden_backward(grad_out_all, down_part, gate_up, hidden)
    relayed = plane_relay(output_partial)
    if dealt_heads:
        terms = core_grads(shard_count, 6, second_across, grad_gate_up, 2)
    else:
        gate_up_term = column_term(second_all, grad_gate_up).astype(jnp.bfloat16)
        terms = (gate_up_term[:, : FF // part_count], gate_up_term[:, FF // part_count :])
    grad_gate_up, *tied = tie((grad_gate_up, *terms, *relayed))
    terms, relayed = (tied[:2], tied[2:])
    gate_piece = scatter_shards(terms[0], dealt_heads)
    up_piece = scatter_shards(terms[1], dealt_heads)
    last = plane_last(output_partial, relayed)
    grad_mid, second_gain_part, branch_all = middle_back(
        part_count, 3, grad_gate_up, gate_up_part, residual_mid, gain_second, cotangent[0]
    )
    branch_all, down_piece, gate_piece, *last = tie((branch_all, down_piece, gate_piece, *last))
    block_output = (residual_mid + plane_scatter(output_partial, relayed, last)).astype(
        jnp.bfloat16
    )
    if dealt_heads:
        down_parts = plane_gather(down_piece)
        gate_parts = plane_gather(gate_piece)

    grad_packed = attend_backward(
        block_rows,
        dealing,
        branch_all,
        output_part,
        query_rot,
        key_rot,
        value_rows,
        attended,
        log_totals,
        tables,
    )
    if dealt_heads:
        packed_term = attention_grads(
            shard_count, 7, first_across, grad_packed, heads_across, branch_all
        )
        grad_packed, packed_term, *parts = tie((grad_packed, packed_term, *down_parts, *gate_parts))
        down_parts, gate_parts = (parts[:5], parts[5:])
        packed_piece = scatter_shards(packed_term, True)
    grad_input, gain_shard, up_all = input_back(
        part_count,
        shard_count,
        4,
        grad_packed,
        packed,
        tokens[0],
        gain_first,
        grad_mid,
        second_gain_part,
        up_piece,
    )
    if dealt_heads:
        grad_input, packed_piece = tie((grad_input, packed_piece))
        gate_shard = place_hidden(shard_count, gate_parts)
        up_shard = place_sorted(shard_count, up_all)
        down_shard = place_rows(down_parts, jnp.float32)
        query_shard, key_shard, value_shard, output_shard = place_attention(
            shard_count, plane_gather(packed_piece)
        )
    else:

        def gather_columns(piece, outer):
            return put_columns(lax.all_gather(piece, "ctx", axis=0), outer).astype(jnp.float32)

        gate_shard = gather_columns(gate_piece, shard_count)
        up_shard = put_columns(
            up_all.reshape(part_count, -1, FF // part_count), shard_count
        ).astype(jnp.float32)
        down_shard = lax.all_gather(down_piece, "ctx", axis=0, tiled=True).astype(jnp.float32)
        grad_query, grad_key_value = (grad_packed[:, :part_width], grad_packed[:, part_width:])
        query_piece = scatter_shards(product(first_across, grad_query))
        query_shard = gather_columns(query_piece, 1)
        key_value_piece = scatter_shards(product(first_across, grad_key_value))
        output_term = column_term(attended, branch_all)
        spread = jnp.zeros((D, D), jnp.float32)
        spread = lax.dynamic_update_slice_in_dim(
            spread, output_term, ctx_index * output_term.shape[0], 0
        )
        output_shard = lax.psum(scatter_shards(spread), "ctx").astype(jnp.float32)
        wide = jnp.zeros((D // shard_count, 2, KV_HEADS, HEAD_DIM), jnp.bfloat16)
        wide = lax.dynamic_update_slice_in_dim(
            wide, key_value_piece.reshape(-1, 2, kv_heads, HEAD_DIM), kv_first, 2
        )
        key_value_shard = lax.psum(wide.reshape(-1, 2 * KV_WIDTH), "ctx").astype(jnp.float32)
        key_shard, value_shard = (key_value_shard[:, :KV_WIDTH], key_value_shard[:, KV_WIDTH:])
    return (
        block_output[None],
        grad_input[None],
        gain_shard[0],
        query_shard,
        key_shard,
        value_shard,
        output_shard,
        gain_shard[1],
        gate_shard,
        up_shard,
        down_shard,
    )


def solution(mesh):
    in_specs = (
        P("fsdp", "ctx", None),
        P("fsdp", None),
        P("fsdp"),
        P("fsdp", None),
        P("fsdp", None),
        P("fsdp", None),
        P("fsdp", None),
        P("fsdp"),
        P("fsdp", None),
        P("fsdp", None),
        P("fsdp", None),
        P("fsdp", "ctx", None),
    )
    out_specs = (
        P("fsdp", "ctx", None),
        P("fsdp", "ctx", None),
        P("fsdp"),
        P("fsdp", None),
        P("fsdp", None),
        P("fsdp", None),
        P("fsdp", None),
        P("fsdp"),
        P("fsdp", None),
        P("fsdp", None),
        P("fsdp", None),
    )
    return jax.shard_map(
        per_device, mesh=mesh, in_specs=in_specs, out_specs=out_specs, check_vma=False
    )
```

```python
import functools
import math

import jax
import jax.numpy as jnp
from jax import lax
from jax.experimental import pallas as pl
from jax.experimental.pallas import tpu as pltpu
from jax.sharding import PartitionSpec as P

D = 2048
FF = 5632
HEADS = 32
KV_HEADS = 4
HEAD_DIM = 64
KV_WIDTH = 256


epsilon = 1e-05


MESH = pl.DeviceIdType.MESH
VMEM = pl.BlockSpec(memory_space=pltpu.VMEM)
SMEM = pl.BlockSpec(memory_space=pltpu.SMEM)
HBM = pl.BlockSpec(memory_space=pltpu.HBM)
LANES = 128
PAIR = LANES // HEAD_DIM
QUERY_ROWS = 256
VMEM_MEGABYTES = 60


def shape(dims, kind=jnp.bfloat16):
    return jax.ShapeDtypeStruct(dims, kind)


def norm_parts(values):
    inverse = lax.rsqrt(jnp.mean(values * values, axis=-1, keepdims=True) + epsilon)
    return (values * inverse, inverse)


def norm_back(gradient, normed, inverse):
    return inverse * (gradient - normed * jnp.mean(gradient * normed, axis=-1, keepdims=True))


def product(left_side, right_side):
    return jnp.dot(left_side, right_side, preferred_element_type=jnp.float32)


def times_transposed(left_side, right_side):
    return lax.dot_general(
        left_side, right_side, (((1,), (1,)), ((), ())), preferred_element_type=jnp.float32
    )


def column_term(source, gradient):
    return lax.dot_general(
        source, gradient, (((0,), (0,)), ((), ())), preferred_element_type=jnp.float32
    )


STRIP = 32
PIECES = 4


def plane_places():
    me = lax.axis_index("ctx")
    return (me, me + 1 - 2 * lax.rem(me, 2), lax.rem(me + 2, 4), 3 - me)


def signal(barrier, **place):
    pl.semaphore_signal(barrier, inc=1, device_id=place, device_id_type=MESH)


def meet(count, shards=1):
    me = lax.axis_index("ctx")
    barrier = pltpu.get_barrier_semaphore()
    for step in range(1, count):
        signal(barrier, ctx=lax.rem(me + step, count))
    for step in range(1, shards):
        signal(barrier, fsdp=lax.rem(lax.axis_index("fsdp") + step, shards))
    pl.semaphore_wait(barrier, count - 1 + shards - 1)


def remote(source, target, send_sem, recv_sem, **place):
    copy = pltpu.make_async_remote_copy(
        src_ref=source,
        dst_ref=target,
        send_sem=send_sem,
        recv_sem=recv_sem,
        device_id=place,
        device_id_type=MESH,
    )
    copy.start()
    return copy


def gather_sems(count):
    sends = 3 if count == 4 else count - 1
    return [
        pltpu.SemaphoreType.DMA((PIECES,)),
        pltpu.SemaphoreType.DMA((sends, PIECES)),
        pltpu.SemaphoreType.DMA((sends, PIECES)),
    ]


class RowGather:
    def __init__(self, count, own, out, sems):
        self.count, self.own, self.out = (count, own, out)
        self.local_sem, self.send_sem, self.recv_sem = sems
        self.size = own.shape[0] // PIECES
        self.copies = [[] for _ in range(PIECES)]
        self.relays = []

    def place(self, owner, piece):
        start = owner * self.own.shape[0] + piece * self.size
        return self.out.at[pl.ds(pl.multiple_of(start, self.size), self.size)]

    def send(self, piece):
        me = lax.axis_index("ctx")
        source = self.own.at[pl.ds(piece * self.size, self.size)]
        target = self.place(me, piece)
        if self.count == 4:
            _, across, along, _ = plane_places()
            peers = (across, along)
        else:
            peers = [lax.rem(me + step, self.count) for step in range(1, self.count)]
        for index, peer in enumerate(peers):
            self.copies[piece].append(
                remote(
                    source,
                    target,
                    self.send_sem.at[index, piece],
                    self.recv_sem.at[index, piece],
                    ctx=peer,
                )
            )
        local = pltpu.make_async_copy(source, target, self.local_sem.at[piece])
        local.start()
        self.copies[piece].append(local)

    def finish(self):
        self.relay()
        self.drain()

    def relay(self, pieces=(0, PIECES // 2, 1, PIECES // 2 + 1)):
        relays = self.relays
        if self.count != 4:
            return
        _, across, along, _ = plane_places()
        for piece in pieces:
            first = piece < PIECES // 2
            came, left = (0, 1) if first else (1, 0)
            owner, peer = (across, along) if first else (along, across)
            self.copies[piece][came].wait_recv()
            block = self.place(owner, piece)
            relays.append(
                remote(
                    block, block, self.send_sem.at[2, piece], self.recv_sem.at[2, piece], ctx=peer
                )
            )

    def drain(self):
        if self.count != 4:
            for copies in self.copies:
                for copy in copies:
                    copy.wait()
            return
        for piece in range(PIECES):
            to_across, to_along, local = self.copies[piece]
            (to_along if piece < PIECES // 2 else to_across).wait_recv()
            to_across.wait_send()
            to_along.wait_send()
            local.wait()
        for relay in self.relays:
            relay.wait()


CHUNKS = 2


def line_sems(shards):
    hops = shards // 2 - 1
    return [
        pltpu.SemaphoreType.DMA,
        pltpu.SemaphoreType.DMA((2 * hops, CHUNKS)),
        pltpu.SemaphoreType.DMA((2 * hops, CHUNKS)),
        pltpu.SemaphoreType.DMA((2 * hops + 1, CHUNKS)),
        pltpu.SemaphoreType.DMA((2 * hops + 1, CHUNKS)),
    ]


class LineGather:
    def __init__(self, shards, own, out, sems):
        self.own, self.out = (own, out)
        self.local_sem, self.send_sem, self.recv_sem, self.core_send, self.core_recv = sems
        self.me = lax.axis_index("fsdp")
        self.hops = shards // 2 - 1
        self.chip = self.me // 2
        self.twin = self.me + 1 - 2 * lax.rem(self.me, 2)
        self.size = own.shape[0] // CHUNKS

    def block(self, owner, chunk):
        start = owner * self.own.shape[0] + chunk * self.size
        return self.out.at[pl.ds(pl.multiple_of(start, self.size), self.size)]

    def copy(self, distance, way, chunk, sems, index, peer):
        owner = self.me - 2 * (1 - 2 * way) * distance
        target = self.block(owner, chunk)
        part = pl.ds(chunk * self.size, self.size)
        send_sem, recv_sem = sems
        return pltpu.make_async_remote_copy(
            src_ref=self.own.at[part] if distance == 0 else target,
            dst_ref=target,
            send_sem=send_sem.at[index, chunk],
            recv_sem=recv_sem.at[index, chunk],
            device_id={"fsdp": peer},
            device_id_type=MESH,
        )

    def hop(self, way, distance, chunk):
        sems = (self.send_sem, self.recv_sem)
        peer = self.me + 2 * (1 - 2 * way)
        return self.copy(distance, way, chunk, sems, way * self.hops + distance, peer)

    def cross(self, way, distance, chunk):
        index = distance if way == 0 else self.hops + distance
        sems = (self.core_send, self.core_recv)
        return self.copy(distance, way, chunk, sems, index, self.twin)

    def can_send(self, way):
        return self.chip < self.hops if way == 0 else self.chip > 0

    def behind(self, way, distance):
        return self.chip >= distance if way == 0 else self.chip + distance <= self.hops

    def local(self):
        rows = self.own.shape[0]
        target = self.out.at[pl.ds(pl.multiple_of(self.me * rows, rows), rows)]
        return pltpu.make_async_copy(self.own, target, self.local_sem)

    def start(self, chunk):
        for way in (0, 1):
            pl.when(self.can_send(way))(lambda way=way: self.hop(way, 0, chunk).start())
        self.cross(0, 0, chunk).start()
        if chunk == 0:
            self.local().start()

    def step(self, distance, chunk):
        for way in (0, 1):

            @pl.when(self.behind(way, distance))
            def _(way=way):
                self.hop(way, distance - 1, chunk).wait_recv()
                if distance < self.hops:
                    pl.when(self.can_send(way))(lambda: self.hop(way, distance, chunk).start())
                self.cross(way, distance, chunk).start()

    def drain(self):
        for chunk in range(CHUNKS):
            for way in (0, 1):
                for distance in range(self.hops):
                    here = jnp.logical_and(self.can_send(way), self.behind(way, distance))
                    pl.when(here)(
                        lambda way=way, d=distance, chunk=chunk: self.hop(way, d, chunk).wait_send()
                    )
                for distance in range(1, self.hops + 1):
                    pl.when(self.behind(way, distance))(
                        lambda way=way, d=distance, chunk=chunk: self.cross(way, d, chunk).wait()
                    )
            self.cross(0, 0, chunk).wait()
        self.local().wait()


TILE = 512


def begin(source, target, sem):
    copy = pltpu.make_async_copy(source, target, sem)
    copy.start()
    return copy


class Scatter:
    def __init__(self, count, left, right, transposed, refs):
        self.count, self.transposed = (count, transposed)
        self.left_buf, self.right_buf, self.load_sem, *refs = refs
        self.send_buf, self.recv_buf, self.kept, self.total, self.send_sem, self.recv_sem = refs
        self.rows, self.width = self.total.shape
        self.tiles = self.width // TILE
        self.loads = {}
        owners = self.owners()
        depth = self.left_buf.shape[1]
        self.load_left(left, owners[0], 0)
        for tile in range(self.tiles):
            columns = pl.ds(tile * TILE, TILE)
            if transposed:
                place = (columns, pl.ds(0, depth))
                source, target = (right.at[place], self.right_buf.at[columns])
            else:
                source, target = (right.at[:, columns], self.right_buf.at[:, columns])
            self.loads["tile", tile] = begin(source, target, self.load_sem.at[count + tile])
        for index in range(1, count):
            self.load_left(left, owners[index], index)

    def owners(self):
        me = lax.axis_index("ctx")
        if self.count != 4:
            return [lax.rem(me + step, self.count) for step in range(1, self.count)] + [me]
        _, across, along, corner = plane_places()
        return [corner, across, along, me]

    def block_rows(self, owner):
        return pl.ds(pl.multiple_of(owner * self.rows, self.rows), self.rows)

    def load_left(self, left, owner, index):
        rows = self.block_rows(owner)
        self.loads["left", index] = begin(
            left.at[rows], self.left_buf.at[rows], self.load_sem.at[index]
        )

    def tile(self, owner, columns):
        piece = self.left_buf[self.block_rows(owner), :]
        if self.transposed:
            return times_transposed(piece, self.right_buf[columns, :])
        return product(piece, self.right_buf[:, columns])

    def block(self, index, store):
        owner = self.owners()[index]
        self.loads["left", index].wait()

        def column(tile, carry):
            columns = pl.ds(pl.multiple_of(tile * TILE, TILE), TILE)
            store(columns, self.tile(owner, columns))
            return carry

        lax.fori_loop(0, self.tiles, column, 0)

    def send(self, slot, part, columns, sem, peer):
        return remote(
            self.send_buf.at[slot, part, columns],
            self.recv_buf.at[slot, part, columns],
            self.send_sem.at[sem],
            self.recv_sem.at[sem],
            ctx=peer,
        )

    def store_own(self, columns, value):
        self.total[:, columns] = value

    def run(self, others=()):
        if self.count == 4:
            self.run_relayed(list(others))
        else:
            self.run_direct()
            for other in others:
                other()

    def run_direct(self):
        for tile in range(self.tiles):
            self.loads["tile", tile].wait()
        copies = []
        everything = (pl.ds(0, self.rows), pl.ds(0, self.width))
        for index, owner in enumerate(self.owners()[:-1]):

            def store_sent(columns, value, index=index):
                self.send_buf[index, :, columns] = value.astype(self.send_buf.dtype)

            self.block(index, store_sent)
            copies.append(self.send(index, *everything, index, owner))
        self.block(self.count - 1, self.store_own)
        self.relays, self.copies = ([], copies)

    def run_relayed(self, others):
        corner, across, along, me = self.owners()
        send_buf, kept, tiles = (self.send_buf, self.kept, self.tiles)
        half = self.rows // 2
        low, high = (pl.ds(0, half), pl.ds(half, half))
        whole = pl.ds(0, self.width)
        relays = []
        self.loads["left", 0].wait()
        for tile in range(tiles):
            columns = pl.ds(tile * TILE, TILE)
            self.loads["tile", tile].wait()
            send_buf[0, :, columns] = self.tile(corner, columns).astype(send_buf.dtype)
            relays.append(
                (
                    self.send(0, low, columns, tile, across),
                    self.send(0, high, columns, tiles + tile, along),
                )
            )

        def store_across(columns, value):
            send_buf[1, low, columns] = value[:half].astype(send_buf.dtype)
            kept[high, columns] = value[half:]

        def store_along(columns, value):
            send_buf[1, high, columns] = value[half:].astype(send_buf.dtype)
            kept[low, columns] = value[:half]

        self.block(1, store_across)
        copies = [self.send(1, low, whole, 4 * tiles, across)]
        self.block(2, store_along)
        copies.append(self.send(1, high, whole, 4 * tiles + 1, along))
        self.block(3, self.store_own)
        for _ in range(len(others) - tiles - 1):
            others.pop(0)()
        for tile in range(tiles):
            columns = pl.ds(tile * TILE, TILE)
            for side, peer in ((0, along), (1, across)):
                if others and side == 0:
                    others.pop(0)()
                relays[tile][side].wait_recv()
                part = (low, high)[side]

                def add(where, columns=columns):
                    value = kept[where, columns] + self.recv_buf[0, where, columns].astype(
                        jnp.float32
                    )
                    send_buf[2, where, columns] = value.astype(send_buf.dtype)

                for_strips(side * half, half, add)
                sem = (2 + side) * tiles + tile
                copies.append(self.send(2, part, columns, sem, peer))
        self.relays, self.copies = (relays, copies)
        for other in others:
            other()

    def finish(self):
        for pair in self.relays:
            for copy in pair:
                copy.wait_send()
        for copy in self.copies:
            copy.wait()


def scatter_scratch(count, rows, width, left, right, transposed, depth):
    slots = 3 if count == 4 else count - 1
    sems = 4 * (width // TILE) + 2 if count == 4 else count - 1
    return [
        pltpu.VMEM(left.shape, jnp.bfloat16),
        pltpu.VMEM((width, depth) if transposed else (depth, width), jnp.bfloat16),
        pltpu.SemaphoreType.DMA((count + width // TILE,)),
        pltpu.VMEM((slots, rows, width), jnp.bfloat16),
        pltpu.VMEM((slots, rows, width), jnp.bfloat16),
        pltpu.VMEM((rows, width) if count == 4 else (8, LANES), jnp.float32),
        pltpu.VMEM((rows, width), jnp.float32),
        pltpu.SemaphoreType.DMA((sems,)),
        pltpu.SemaphoreType.DMA((sems,)),
    ]


SCATTER_REFS = 9


def side_loads(sources, refs):
    *targets, sem = refs
    return [begin(source, target, sem.at[i]) for i, (source, target) in enumerate(zip(sources, targets))]


def side_scratch(*arrays):
    return [pltpu.VMEM(a.shape, a.dtype) for a in arrays] + [
        pltpu.SemaphoreType.DMA((len(arrays),))
    ]


def received(count, recv_buf, total, rows):
    value = total[rows, :]
    for slot in (1, 2) if count == 4 else range(count - 1):
        value = value + recv_buf[slot, rows, :].astype(jnp.float32)
    return value


def for_strips(first, rows, body):
    def strip(index, carry):
        body(pl.ds(pl.multiple_of(first + index * STRIP, STRIP), STRIP))
        return carry

    lax.fori_loop(0, rows // STRIP, strip, 0)


def call_plane(body, ident, outs, out_specs, in_specs, scratch, flops, megabytes, args):
    return pl.pallas_call(
        body,
        out_shape=outs,
        in_specs=in_specs,
        out_specs=out_specs,
        scratch_shapes=scratch,
        compiler_params=pltpu.CompilerParams(
            collective_id=ident, has_side_effects=True, vmem_limit_bytes=megabytes << 20
        ),
        cost_estimate=pl.CostEstimate(
            flops=flops, bytes_accessed=flops // 300, transcendentals=0
        ),
    )(*args)


def for_part(body):
    me = lax.axis_index("ctx")
    for part in range(4):

        @pl.when(me == part)
        def _(part=part):
            body(part)


def strided_columns(values, shards, part):
    span = values.shape[1] // (4 * shards)
    starts = [(shard * 4 + part) * span for shard in range(shards)]
    wide = values.astype(jnp.float32)
    return jnp.concatenate([wide[:, i : i + span] for i in starts], axis=1).astype(values.dtype)


def pack_attention(shards, query, key, value, output, packed):
    def body(part):
        width = query.shape[1] // 4
        rows = output.shape[0] // 4
        packed[:, :width] = strided_columns(query[...], shards, part)
        packed[:, width : width + KV_WIDTH] = key[...]
        packed[:, width + KV_WIDTH : width + 2 * KV_WIDTH] = value[...]
        for index in range(4):
            packed[index * rows : (index + 1) * rows, width + 2 * KV_WIDTH :] = output[
                part * rows : (part + 1) * rows, index * width : (index + 1) * width
            ]

    for_part(body)


def pack_hidden(shards, gate, up, packed):
    def body(part):
        width = packed.shape[1] // 2

        def strip(where):
            packed[where, :width] = strided_columns(gate[where, :], shards, part)
            packed[where, width:] = strided_columns(up[where, :], shards, part)

        for_strips(0, packed.shape[0], strip)

    for_part(body)


def write_tables(cosine, sine):
    half = HEAD_DIM // 2

    def strip(where):
        dims = (STRIP, LANES)
        lane = lax.broadcasted_iota(jnp.int32, dims, 1)
        place = lax.broadcasted_iota(jnp.int32, dims, 0) + where.start
        index = lax.rem(lane, half).astype(jnp.float32)
        frequency = jnp.exp(-math.log(10000.0) * index * (2.0 / HEAD_DIM))
        angles = place.astype(jnp.float32) * frequency
        cosine[where, :] = jnp.cos(angles)
        sine[where, :] = jnp.where(low_lanes(dims, half), -jnp.sin(angles), jnp.sin(angles))

    for_strips(0, cosine.shape[0], strip)


def start_body(count, shards, tokens, first_gain, second_gain, *refs):
    if count == 4:
        weights, refs = (refs[:6], refs[6:])
    tokens_all, gain_first, gain_second, cosine, sine, *refs = refs
    if count == 4:
        weights_all, packed_hidden, *refs = refs
    gains, gains_all, gain_send, gain_recv, *refs = refs
    first = RowGather(count, tokens, tokens_all, refs[:3])
    half = PIECES // 2
    if count == 4:
        packed, gate, up, load_sem, *line_refs = refs[3:]
        loads = [
            begin(weights[4 + i], target, load_sem.at[i]) for i, target in enumerate((gate, up))
        ]
        line = LineGather(shards, packed, weights_all, line_refs)
        pack_attention(shards, *weights[:4], packed)
    meet(count, shards)
    if count == 4:
        line.start(0)
    first.send(0)
    first.send(half)
    me = lax.axis_index("fsdp")
    gains[0:1, :] = first_gain[...]
    gains[1:2, :] = second_gain[...]
    gains_all[me] = gains[...]
    copies = []
    for step in range(1, shards):
        copies.append(
            remote(
                gains,
                gains_all.at[me],
                gain_send.at[step - 1],
                gain_recv.at[step - 1],
                fsdp=lax.rem(me + step, shards),
            )
        )
    if count != 4:
        write_tables(cosine, sine)
        first.send(1)
        first.send(half + 1)
        first.finish()
    else:
        steps = [(d, c) for d in range(1, line.hops + 1) for c in range(CHUNKS)]
        write_tables(cosine, sine)
        for chunk in range(1, CHUNKS):
            line.start(chunk)
        line.step(*steps[0])
        first.relay((0, half))
        first.send(1)
        first.send(half + 1)
        for step in steps[1:3]:
            line.step(*step)
        for load in loads:
            load.wait()
        pack_hidden(shards, gate, up, packed_hidden)
        first.relay((1, half + 1))
        for step in steps[3:-1]:
            line.step(*step)
        first.drain()
    for copy in copies:
        copy.wait()
    span = gains.shape[1]
    for shard in range(shards):
        lanes = slice(shard * span, (shard + 1) * span)
        gain_first[:, lanes] = gains_all[shard, 0:1, :].astype(jnp.float32)
        gain_second[:, lanes] = gains_all[shard, 1:2, :].astype(jnp.float32)
    if count == 4:
        line.step(*steps[-1])
        line.drain()


def start_gather(count, shards, ident, tokens, first_gain, second_gain, *weights):
    rows, width = tokens.shape
    span = first_gain.shape[1]
    wide = shape((1, width), jnp.float32)
    table = shape((count * rows, LANES), jnp.float32)
    outs = [shape((count * rows, width)), wide, wide, table, table]
    out_specs = [HBM] + [VMEM] * 4
    in_specs = [HBM, VMEM, VMEM]
    scratch = [
        pltpu.VMEM((2, span), jnp.bfloat16),
        pltpu.VMEM((shards, 2, span), jnp.bfloat16),
        pltpu.SemaphoreType.DMA((shards - 1,)),
        pltpu.SemaphoreType.DMA((shards - 1,)),
    ] + gather_sems(count)
    if weights:
        height = weights[0].shape[0]
        packed = width // 2 + 2 * KV_WIDTH
        outs += [shape((shards * height, packed)), shape((height, FF // 2))]
        out_specs += [HBM, VMEM]
        in_specs += [VMEM] * 4 + [HBM] * 2
        scratch += [
            pltpu.VMEM((height, packed), jnp.bfloat16),
            pltpu.VMEM((height, FF), jnp.bfloat16),
            pltpu.VMEM((height, FF), jnp.bfloat16),
            pltpu.SemaphoreType.DMA((2,)),
        ] + line_sems(shards)
    return call_plane(
        functools.partial(start_body, count, shards),
        ident,
        tuple(outs),
        tuple(out_specs),
        in_specs,
        scratch,
        5 * 10**10,
        VMEM_MEGABYTES,
        (tokens, first_gain, second_gain, *weights),
    )


def strips_and_send(gather, strip):
    size = gather.size
    for piece in range(PIECES):
        for_strips(piece * size, size, strip)
        gather.send(piece)
    gather.finish()


def middle_body(count, attended, weight, tokens, gain, residual, second_all, own, *refs):
    scatter = Scatter(count, attended, weight, False, refs[:SCATTER_REFS])
    side = refs[SCATTER_REFS : SCATTER_REFS + 2]
    loads = side_loads([tokens], side)
    meet(count)
    scatter.run()
    scatter.finish()
    for load in loads:
        load.wait()

    def strip(where):
        values = side[0][where, :].astype(jnp.float32) + received(
            count, scatter.recv_buf, scatter.total, where
        )
        residual[where, :] = values
        normed, _ = norm_parts(values)
        own[where, :] = (normed * gain[...]).astype(jnp.bfloat16)

    strips_and_send(RowGather(count, own, second_all, refs[SCATTER_REFS + 2 :]), strip)


def middle_gather(count, ident, attended, weight, tokens, gain):
    rows, width = tokens.shape
    return call_plane(
        functools.partial(middle_body, count),
        ident,
        (shape((rows, width), jnp.float32), shape((count * rows, width))),
        (VMEM, HBM),
        [HBM] * 3 + [VMEM],
        [pltpu.VMEM((rows, width), jnp.bfloat16)]
        + scatter_scratch(count, rows, width, attended, weight, False, attended.shape[1])
        + side_scratch(tokens)
        + gather_sems(count),
        6 * 10**10,
        VMEM_MEGABYTES,
        (attended, weight, tokens, gain),
    )


def middle_back_body(
    count, grad_gate_up, gate_up_weight, residual, grad_out, gain, grad_mid, gain_part, branch_all, own,
    *refs
):
    scatter = Scatter(count, grad_gate_up, gate_up_weight, True, refs[:SCATTER_REFS])
    side = refs[SCATTER_REFS : SCATTER_REFS + 3]
    loads = side_loads([residual, grad_out], side)
    meet(count)
    scatter.run()
    scatter.finish()
    gain_part[...] = jnp.zeros_like(gain_part)
    for load in loads:
        load.wait()

    def strip(where):
        gradient = received(count, scatter.recv_buf, scatter.total, where)
        normed, inverse = norm_parts(side[0][where, :])
        gain_part[...] += jnp.sum(gradient * normed, axis=0, keepdims=True)
        values = side[1][where, :].astype(jnp.float32) + norm_back(
            gradient * gain[...], normed, inverse
        )
        grad_mid[where, :] = values
        own[where, :] = values.astype(jnp.bfloat16)

    strips_and_send(RowGather(count, own, branch_all, refs[SCATTER_REFS + 3 :]), strip)


def column_halves(array):
    rows, width = array.shape
    if width // 2 % LANES:
        return ((array[:, : width // 2], array[:, width // 2 :]), (VMEM, VMEM))
    specs = [pl.BlockSpec((rows, width // 2), lambda *index, side=side: (0, side)) for side in (0, 1)]
    return ((array, array), specs)


def middle_back(count, ident, grad_gate_up, gate_up_weight, residual, gain, grad_out):
    rows, width = residual.shape
    return call_plane(
        functools.partial(middle_back_body, count),
        ident,
        (
            shape((rows, width), jnp.float32),
            shape((1, width), jnp.float32),
            shape((count * rows, width)),
        ),
        (VMEM, VMEM, HBM),
        [HBM] * 4 + [VMEM],
        [pltpu.VMEM((rows, width), jnp.bfloat16)]
        + scatter_scratch(
            count, rows, width, grad_gate_up, gate_up_weight, True, grad_gate_up.shape[1]
        )
        + side_scratch(residual, grad_out)
        + gather_sems(count),
        6 * 10**10,
        VMEM_MEGABYTES,
        (grad_gate_up, gate_up_weight, residual, grad_out, gain),
    )


def input_back_body(
    count, shards, grad_packed, weight, tokens, grad_mid, piece, gain, second_part, grad_input, gain_sums,
    piece_all, gain_part, parts, part_recv, sums, sums_recv, part_send_sem, part_recv_sem, sums_send_sem,
    sums_recv_sem, *refs
):
    scatter = Scatter(count, grad_packed, weight, True, refs[:SCATTER_REFS])
    side = refs[SCATTER_REFS : SCATTER_REFS + 3]
    loads = side_loads([tokens, grad_mid], side)
    gather = RowGather(count, piece, piece_all, refs[SCATTER_REFS + 3 :])
    meet(count, shards)
    scatter.run()
    for part in range(PIECES):
        gather.send(part)
    scatter.finish()
    gain_part[...] = jnp.zeros_like(gain_part)
    for load in loads:
        load.wait()

    def strip(where):
        gradient = received(count, scatter.recv_buf, scatter.total, where)
        normed, inverse = norm_parts(side[0][where, :].astype(jnp.float32))
        gain_part[...] += jnp.sum(gradient * normed, axis=0, keepdims=True)
        values = side[1][where, :] + norm_back(gradient * gain[...], normed, inverse)
        grad_input[where, :] = values.astype(jnp.bfloat16)

    for_strips(0, grad_input.shape[0], strip)
    gather.relay()
    me = lax.axis_index("fsdp")
    span = parts.shape[2]
    for shard in range(shards):
        lanes = slice(shard * span, (shard + 1) * span)
        parts[shard, 0:1, :] = gain_part[:, lanes]
        parts[shard, 1:2, :] = second_part[:, lanes]
    copies = []
    for step in range(1, shards):
        peer = lax.rem(me + step, shards)
        copies.append(
            remote(
                parts.at[peer],
                part_recv.at[step - 1],
                part_send_sem.at[step - 1],
                part_recv_sem.at[step - 1],
                fsdp=peer,
            )
        )
    for copy in copies:
        copy.wait()
    value = parts[me]
    for step in range(1, shards):
        value = value + part_recv[step - 1]
    sums[...] = value
    copies = []
    for step in range(1, count):
        copies.append(
            remote(
                sums,
                sums_recv.at[step - 1],
                sums_send_sem.at[step - 1],
                sums_recv_sem.at[step - 1],
                ctx=lax.rem(lax.axis_index("ctx") + step, count),
            )
        )
    for copy in copies:
        copy.wait()
    for step in range(1, count):
        value = value + sums_recv[step - 1]
    gain_sums[...] = value
    gather.drain()


def input_back(
    count, shards, ident, grad_packed, weight, tokens, gain, grad_mid, second_part, piece
):
    rows, width = tokens.shape
    span = width // shards
    return call_plane(
        functools.partial(input_back_body, count, shards),
        ident,
        (
            shape((rows, width)),
            shape((2, span), jnp.float32),
            shape((count * piece.shape[0], piece.shape[1])),
        ),
        (VMEM, VMEM, HBM),
        [HBM] * 5 + [VMEM] * 2,
        [
            pltpu.VMEM((1, width), jnp.float32),
            pltpu.VMEM((shards, 2, span), jnp.float32),
            pltpu.VMEM((shards - 1, 2, span), jnp.float32),
            pltpu.VMEM((2, span), jnp.float32),
            pltpu.VMEM((count - 1, 2, span), jnp.float32),
            pltpu.SemaphoreType.DMA((shards - 1,)),
            pltpu.SemaphoreType.DMA((shards - 1,)),
            pltpu.SemaphoreType.DMA((count - 1,)),
            pltpu.SemaphoreType.DMA((count - 1,)),
        ]
        + scatter_scratch(count, rows, width, grad_packed, weight, True, grad_packed.shape[1])
        + side_scratch(tokens, grad_mid)
        + gather_sems(count),
        5 * 10**10,
        VMEM_MEGABYTES,
        (grad_packed, weight, tokens, grad_mid, piece, gain, second_part),
    )


def swap(array, along):
    pairs = [(i, (i + 2) % 4) if along else (i, i + 1 - 2 * (i % 2)) for i in range(4)]
    return lax.ppermute(array, "ctx", pairs)


def plane_near(array):
    return (array, swap(array, False), swap(array, True))


def plane_far(near):
    _, across, along = near
    half = across.shape[0] // 2
    return (*near, swap(across[:half], True), swap(along[half:], False))


def plane_gather(array):
    return plane_far(plane_near(array))


def hidden_body(rows, gate_weight, up_weight, gate_up, hidden, rows_across, hidden_across):
    width = hidden.shape[1]
    rows_across[...] = rows[...].T
    gate = product(rows[...], gate_weight[...])
    gate_up[:, :width] = gate
    upward = product(rows[...], up_weight[...])
    gate_up[:, width:] = upward
    low = (gate * jax.nn.sigmoid(gate) * upward).astype(jnp.bfloat16)
    hidden[...] = low
    hidden_across[...] = low.T


def hidden_forward(second_all, gate_up_weight):
    length, depth = second_all.shape
    width = gate_up_weight.shape[1] // 2
    (gate_weight, up_weight), specs = column_halves(gate_up_weight)
    step = QUERY_ROWS
    return pl.pallas_call(
        hidden_body,
        grid=(length // step,),
        out_shape=(
            shape((length, 2 * width), jnp.float32),
            shape((length, width)),
            shape((depth, length)),
            shape((width, length)),
        ),
        in_specs=[pl.BlockSpec((step, depth), lambda i: (i, 0))] + list(specs),
        out_specs=(
            pl.BlockSpec((step, 2 * width), lambda i: (i, 0)),
            pl.BlockSpec((step, width), lambda i: (i, 0)),
            pl.BlockSpec((depth, step), lambda i: (0, i)),
            pl.BlockSpec((width, step), lambda i: (0, i)),
        ),
        compiler_params=pltpu.CompilerParams(vmem_limit_bytes=VMEM_MEGABYTES << 20),
        cost_estimate=pl.CostEstimate(
            flops=4 * length * depth * width, bytes_accessed=3 * 10**7, transcendentals=10**6
        ),
    )(second_all, gate_weight, up_weight)


def hidden_back_body(grad_rows, down_weight, gate_up, grad_gate_up):
    width = down_weight.shape[0]
    grad_hidden = times_transposed(grad_rows[...], down_weight[...])
    gate, upward = (gate_up[:, :width], gate_up[:, width:])
    sigmoid_gate = jax.nn.sigmoid(gate)
    silu_gate = gate * sigmoid_gate
    grad_gate = grad_hidden * upward * sigmoid_gate * (1.0 + gate * (1.0 - sigmoid_gate))
    grad_gate_up[:, :width] = grad_gate.astype(jnp.bfloat16)
    grad_gate_up[:, width:] = (grad_hidden * silu_gate).astype(jnp.bfloat16)


def hidden_backward(grad_out_all, down_weight, gate_up):
    length, depth = grad_out_all.shape
    width = down_weight.shape[0]
    step = QUERY_ROWS
    return pl.pallas_call(
        hidden_back_body,
        grid=(length // step,),
        out_shape=shape((length, 2 * width)),
        in_specs=[
            pl.BlockSpec((step, depth), lambda i: (i, 0)),
            pl.BlockSpec((width, depth), lambda i: (0, 0)),
            pl.BlockSpec((step, 2 * width), lambda i: (i, 0)),
        ],
        out_specs=pl.BlockSpec((step, 2 * width), lambda i: (i, 0)),
        compiler_params=pltpu.CompilerParams(vmem_limit_bytes=VMEM_MEGABYTES << 20),
        cost_estimate=pl.CostEstimate(
            flops=4 * length * depth * width, bytes_accessed=3 * 10**7, transcendentals=10**6
        ),
    )(grad_out_all, down_weight, gate_up)


def meet_twin(neighbours=False):
    me = lax.axis_index("fsdp")
    barrier = pltpu.get_barrier_semaphore()
    signal(barrier, fsdp=me + 1 - 2 * lax.rem(me, 2))
    if neighbours:
        _, across, along, _ = plane_places()
        signal(barrier, ctx=across)
        signal(barrier, ctx=along)
    pl.semaphore_wait(barrier, 3 if neighbours else 1)


def shard_rows(array, shards, core):
    span = array.shape[0] // shards
    starts = [pl.multiple_of((2 * i + core) * span, 16) for i in range(shards // 2)]
    return jnp.concatenate([array[pl.ds(start, span), :] for start in starts], axis=0)


GRAD_TILE = 256


class CoreSum:
    def __init__(self, send_buf, recv_buf, send_sem, recv_sem):
        self.send_buf, self.recv_buf = (send_buf, recv_buf)
        self.send_sem, self.recv_sem = (send_sem, recv_sem)

    def copy(self, tile):
        me = lax.axis_index("fsdp")
        columns = pl.ds(pl.multiple_of(tile * GRAD_TILE, GRAD_TILE), GRAD_TILE)
        return pltpu.make_async_remote_copy(
            src_ref=self.send_buf.at[:, columns],
            dst_ref=self.recv_buf.at[:, columns],
            send_sem=self.send_sem.at[tile],
            recv_sem=self.recv_sem.at[tile],
            device_id={"fsdp": me + 1 - 2 * lax.rem(me, 2)},
            device_id_type=MESH,
        )


def column_tile(tile):
    return pl.ds(pl.multiple_of(tile * GRAD_TILE, GRAD_TILE), GRAD_TILE)


def core_grads_body(shards, across, gradient, out, half, send_buf, recv_buf, send_sem, recv_sem):
    core = lax.rem(lax.axis_index("fsdp"), 2)
    tiles = gradient.shape[1] // GRAD_TILE
    sums = CoreSum(send_buf, recv_buf, send_sem, recv_sem)
    half[...] = shard_rows(across, shards, 1 - core)
    meet_twin()

    def send(tile, carry):
        columns = column_tile(tile)
        send_buf[:, columns] = product(half[...], gradient[:, columns]).astype(jnp.bfloat16)
        sums.copy(tile).start()
        return carry

    lax.fori_loop(0, tiles, send, 0)
    half[...] = shard_rows(across, shards, core)

    def keep(tile, carry):
        columns = column_tile(tile)
        value = product(half[...], gradient[:, columns])
        sums.copy(tile).wait()
        out[:, columns] = (value + recv_buf[:, columns].astype(jnp.float32)).astype(jnp.bfloat16)
        return carry

    lax.fori_loop(0, tiles, keep, 0)


def core_grads(shards, ident, source, gradient):
    depth, length = source.shape
    width = gradient.shape[1]
    tiles = width // GRAD_TILE
    return call_plane(
        functools.partial(core_grads_body, shards),
        ident,
        shape((depth // 2, width)),
        VMEM,
        [VMEM] * 2,
        [
            pltpu.VMEM((depth // 2, length), jnp.bfloat16),
            pltpu.VMEM((depth // 2, width), jnp.bfloat16),
            pltpu.VMEM((depth // 2, width), jnp.bfloat16),
            pltpu.SemaphoreType.DMA((tiles,)),
            pltpu.SemaphoreType.DMA((tiles,)),
        ],
        2 * length * depth * width,
        VMEM_MEGABYTES,
        (source, gradient),
    )


def hidden_grads_body(
    count, shards, across, gradient, hidden, down_weight, gate_out, up_out, output, half, gradient_buf,
    send_buf, recv_buf, send_sem, recv_sem, load_sem, *refs
):
    core = lax.rem(lax.axis_index("fsdp"), 2)
    scatter = Scatter(count, hidden, down_weight, False, refs[:SCATTER_REFS])
    span = half.shape[1] // (shards // 2)
    grad_loads = []
    for which in range(2):
        owner = (1 - core, core)[which]
        for chip in range(shards // 2):
            start = pl.multiple_of((2 * chip + owner) * span, 16)
            target = half.at[which, pl.ds(chip * span, span)]
            sem = load_sem.at[which, chip]
            grad_loads.append(begin(across.at[pl.ds(start, span)], target, sem))
    grad_loads.append(begin(gradient, gradient_buf, load_sem.at[2, 0]))
    meet(count, shards)
    sums = CoreSum(send_buf, recv_buf, send_sem, recv_sem)
    tiles = gradient_buf.shape[1] // GRAD_TILE
    width = gate_out.shape[1]

    def send(tile, carry):
        columns = column_tile(tile)
        value = product(half[0], gradient_buf[:, columns])
        send_buf[:, columns] = value.astype(jnp.bfloat16)
        sums.copy(tile).start()
        return carry

    def keep(tile, carry):
        columns = column_tile(tile)
        value = product(half[1], gradient_buf[:, columns])
        sums.copy(tile).wait()
        value = (value + recv_buf[:, columns].astype(jnp.float32)).astype(jnp.bfloat16)
        send_buf[:, columns] = value
        return carry

    def wait_loads():
        for load in grad_loads:
            load.wait()

    bounds = [0, 3, 6, 9, tiles]
    others = [wait_loads]
    for body in (send, keep):
        for first, last in zip(bounds, bounds[1:]):
            others.append(lambda body=body, a=first, b=last: lax.fori_loop(a, b, body, 0))
    scatter.run(others)
    stores = [
        begin(send_buf.at[:, pl.ds(i * width, width)], out, load_sem.at[2, 1 + i])
        for i, out in enumerate((gate_out, up_out))
    ]
    scatter.finish()

    def strip(where):
        output[where, :] = received(count, scatter.recv_buf, scatter.total, where)

    for_strips(0, output.shape[0], strip)
    for store in stores:
        store.wait()


def hidden_grads(count, shards, ident, across, gradient, hidden, down_weight):
    depth, length = across.shape
    width = gradient.shape[1]
    tiles = width // GRAD_TILE
    rows = length // count
    half = shape((depth // 2, width // 2))
    return call_plane(
        functools.partial(hidden_grads_body, count, shards),
        ident,
        (half, half, shape((rows, depth), jnp.float32)),
        (HBM, HBM, VMEM),
        [HBM] * 4,
        [
            pltpu.VMEM((2, depth // 2, length), jnp.bfloat16),
            pltpu.VMEM((length, width), jnp.bfloat16),
            pltpu.VMEM((depth // 2, width), jnp.bfloat16),
            pltpu.VMEM((depth // 2, width), jnp.bfloat16),
            pltpu.SemaphoreType.DMA((tiles,)),
            pltpu.SemaphoreType.DMA((tiles,)),
            pltpu.SemaphoreType.DMA((3, shards // 2)),
        ]
        + scatter_scratch(count, rows, depth, hidden, down_weight, False, hidden.shape[1]),
        6 * 10**10,
        VMEM_MEGABYTES,
        (across, gradient, hidden, down_weight),
    )


def attention_grads_body(
    shards, across, gradient, heads, branch_all, *refs
):
    near, out, far, refs = (refs[:4], refs[4], refs[5:9], refs[9:])
    half, outs, send_buf, recv_buf, send_sem, recv_sem, far_send, far_recv = refs
    core = lax.rem(lax.axis_index("fsdp"), 2)
    width = gradient.shape[1]
    tiles = width // GRAD_TILE
    total = out.shape[1] // GRAD_TILE
    part = out.shape[1] - width
    span = out.shape[0] // (shards // 2)
    height = HEAD_DIM
    sums = CoreSum(send_buf, recv_buf, send_sem, recv_sem)
    meet_twin(True)
    copies = []
    _, to_across, to_along, _ = plane_places()
    for index, target in enumerate(far):
        source = near[index]
        rows = source.shape[0] // 2
        half_rows = pl.ds(rows * (index % 2), rows)
        peer = (to_along, to_across)[index % 2]
        copies.append(
            remote(source.at[half_rows], target, far_send.at[index], far_recv.at[index], ctx=peer)
        )

    def heads_product(index, carry):
        columns = pl.ds(pl.multiple_of(index * 512, 512), 512)
        outs[:, columns] = product(heads[...], branch_all[:, columns])
        return carry

    lax.fori_loop(0, branch_all.shape[1] // 512, heads_product, 0)

    def pieces(side):
        for chip in range(shards // 2):
            rows = pl.ds(pl.multiple_of((2 * chip + side) * height, height), height)
            for index in range(span // height):
                start = chip * span + index * height
                yield slice(start, start + height), outs[rows, index * part : (index + 1) * part]

    for rows, value in pieces(1 - core):
        send_buf[rows, width:] = value.astype(jnp.bfloat16)
    for tile in range(tiles, total):
        sums.copy(tile).start()
    half[...] = shard_rows(across, shards, 1 - core)

    def send(tile, carry):
        columns = column_tile(tile)
        send_buf[:, columns] = product(half[...], gradient[:, columns]).astype(jnp.bfloat16)
        sums.copy(tile).start()
        return carry

    lax.fori_loop(0, tiles, send, 0)
    half[...] = shard_rows(across, shards, core)

    def keep(tile, carry):
        columns = column_tile(tile)
        value = product(half[...], gradient[:, columns])
        sums.copy(tile).wait()
        out[:, columns] = (value + recv_buf[:, columns].astype(jnp.float32)).astype(jnp.bfloat16)
        return carry

    lax.fori_loop(0, tiles, keep, 0)
    for tile in range(tiles, total):
        sums.copy(tile).wait()
    for rows, value in pieces(core):
        value = value + recv_buf[rows, width:].astype(jnp.float32)
        out[rows, width:] = value.astype(jnp.bfloat16)
    for copy in copies:
        copy.wait()


def attention_grads(shards, ident, first_across, grad_packed, heads_across, branch_all, *near):
    depth, length = first_across.shape
    heads = heads_across.shape[0]
    width = grad_packed.shape[1] + heads
    tiles = width // GRAD_TILE
    return call_plane(
        functools.partial(attention_grads_body, shards),
        ident,
        (shape((depth // 2, width)), *[shape((n.shape[0] // 2, n.shape[1])) for n in near]),
        (VMEM,) + (HBM,) * 4,
        [VMEM] * 4 + [HBM] * 4,
        [
            pltpu.VMEM((depth // 2, length), jnp.bfloat16),
            pltpu.VMEM((heads, branch_all.shape[1]), jnp.float32),
            pltpu.VMEM((depth // 2, width), jnp.bfloat16),
            pltpu.VMEM((depth // 2, width), jnp.bfloat16),
            pltpu.SemaphoreType.DMA((tiles,)),
            pltpu.SemaphoreType.DMA((tiles,)),
            pltpu.SemaphoreType.DMA((4,)),
            pltpu.SemaphoreType.DMA((4,)),
        ],
        2 * length * depth * width,
        VMEM_MEGABYTES,
        (first_across, grad_packed, heads_across, branch_all, *near),
    )


def sort_parts(parts, sorted_parts, corner_low):
    me, across, along, corner = plane_places()
    own, from_across, from_along, low, high = parts
    sorted_parts[me] = own[...]
    sorted_parts[across] = from_across[...]
    sorted_parts[along] = from_along[...]

    @pl.when(corner_low)
    def _():
        sorted_parts[corner] = low[...]

    @pl.when(jnp.logical_not(corner_low))
    def _():
        sorted_parts[corner] = high[...]


def interleaved(values, shards):
    span = values[0].shape[1] // shards
    return jnp.concatenate(
        [v[:, shard * span : (shard + 1) * span] for shard in range(shards) for v in values], axis=1
    )


def place_sorted_body(shards, *refs):
    *parts, target = refs
    target[...] = interleaved([part[...].astype(jnp.float32) for part in parts], shards)


def place_sorted(shards, array):
    rows, width = (array.shape[0] // 4, array.shape[1])
    step = 64
    steps = rows // step
    return pl.pallas_call(
        functools.partial(place_sorted_body, shards),
        grid=(steps,),
        out_shape=shape((rows, 4 * width), jnp.float32),
        in_specs=[
            pl.BlockSpec((step, width), lambda i, part=part: (part * steps + i, 0))
            for part in range(4)
        ],
        out_specs=pl.BlockSpec((step, 4 * width), lambda i: (i, 0)),
        cost_estimate=pl.CostEstimate(flops=0, bytes_accessed=10**7, transcendentals=0),
        compiler_params=pltpu.CompilerParams(vmem_limit_bytes=VMEM_MEGABYTES << 20),
    )(array, array, array, array)


def place_hidden_body(shards, *refs):
    parts, (target, sorted_parts) = (refs[:5], refs[5:])
    steps = pl.num_programs(0)
    sort_parts(parts, sorted_parts, pl.program_id(0) < steps // 2)
    values = [sorted_parts[part].astype(jnp.float32) for part in range(sorted_parts.shape[0])]
    target[...] = interleaved(values, shards)


def place_hidden(shards, parts):
    rows, width = parts[0].shape
    step = 64
    half = rows // step // 2
    whole = pl.BlockSpec((step, width), lambda i: (i, 0))
    low = pl.BlockSpec((step, width), lambda i: (jnp.minimum(i, half - 1), 0))
    high = pl.BlockSpec((step, width), lambda i: (jnp.maximum(i - half, 0), 0))
    return pl.pallas_call(
        functools.partial(place_hidden_body, shards),
        grid=(rows // step,),
        out_shape=shape((rows, 4 * width), jnp.float32),
        in_specs=[whole, whole, whole, low, high],
        out_specs=pl.BlockSpec((step, 4 * width), lambda i: (i, 0)),
        scratch_shapes=[pltpu.VMEM((4, step, width), jnp.bfloat16)],
        cost_estimate=pl.CostEstimate(flops=0, bytes_accessed=10**7, transcendentals=0),
        compiler_params=pltpu.CompilerParams(vmem_limit_bytes=VMEM_MEGABYTES << 20),
    )(*parts)


def place_rows_body(own, from_across, from_along, low, high, out):
    me, across, along, corner = plane_places()
    rows = own.shape[0]

    def put(owner, offset, ref):
        size = ref.shape[0]
        start = pl.multiple_of(owner * rows + offset, 8)
        out[pl.ds(start, size), :] = ref[...].astype(out.dtype)

    put(me, 0, own)
    put(across, 0, from_across)
    put(along, 0, from_along)
    put(corner, 0, low)
    put(corner, rows // 2, high)


def place_rows(parts, kind):
    rows, width = parts[0].shape
    return pl.pallas_call(
        place_rows_body,
        out_shape=shape((4 * rows, width), kind),
        in_specs=[VMEM] * 5,
        out_specs=VMEM,
        cost_estimate=pl.CostEstimate(flops=0, bytes_accessed=10**7, transcendentals=0),
        compiler_params=pltpu.CompilerParams(vmem_limit_bytes=VMEM_MEGABYTES << 20),
    )(*parts)


def place_attention_body(shards, own, from_across, from_along, low, high, query, key, value, output, sorted_parts):
    me, across, along, corner = plane_places()
    rows = own.shape[0]
    sorted_parts[me] = own[...]
    sorted_parts[across] = from_across[...]
    sorted_parts[along] = from_along[...]
    sorted_parts[corner, : rows // 2] = low[...]
    sorted_parts[corner, rows // 2 :] = high[...]
    count = sorted_parts.shape[0]
    width = query.shape[1] // count
    span = width // shards
    values = [sorted_parts[part, :, :width].astype(jnp.float32) for part in range(count)]
    query[...] = jnp.concatenate(
        [
            values[part][:, shard * span : (shard + 1) * span]
            for shard in range(shards)
            for part in range(count)
        ],
        axis=1,
    )
    sums = None
    for part in range(count):
        term = sorted_parts[part, :, width : width + 2 * KV_WIDTH].astype(jnp.float32)
        sums = term if sums is None else sums + term
    key[...] = sums[:, :KV_WIDTH]
    value[...] = sums[:, KV_WIDTH:]
    height = rows // count
    for part in range(count):
        for index in range(count):
            tile = sorted_parts[part, index * height : (index + 1) * height, width + 2 * KV_WIDTH :]
            output[part * height : (part + 1) * height, index * width : (index + 1) * width] = (
                tile.astype(jnp.float32)
            )


def place_attention(shards, parts):
    rows, width = parts[0].shape
    wide = shape((rows, D), jnp.float32)
    narrow = shape((rows, KV_WIDTH), jnp.float32)
    return pl.pallas_call(
        functools.partial(place_attention_body, shards),
        out_shape=(wide, narrow, narrow, wide),
        in_specs=[VMEM] * 5,
        out_specs=(VMEM,) * 4,
        scratch_shapes=[pltpu.VMEM((4, rows, width), jnp.bfloat16)],
        cost_estimate=pl.CostEstimate(flops=0, bytes_accessed=10**7, transcendentals=0),
        compiler_params=pltpu.CompilerParams(vmem_limit_bytes=VMEM_MEGABYTES << 20),
    )(*parts)


def low_lanes(dims, size):
    return lax.rem(lax.broadcasted_iota(jnp.int32, dims, len(dims) - 1), 2 * size) < size


def turn(values, cosine, sine):
    half = HEAD_DIM // 2
    swapped = jnp.where(
        low_lanes(values.shape, half),
        pltpu.roll(values, LANES - half, 1),
        pltpu.roll(values, half, 1),
    )
    return values * cosine + swapped * sine


def two_heads(values):
    low = low_lanes(values.shape, HEAD_DIM)
    zero = jnp.zeros_like(values)
    return jnp.concatenate([jnp.where(low, values, zero), jnp.where(low, zero, values)], axis=0)


def pick_heads(values):
    rows = values.shape[1] // PAIR
    return jnp.concatenate(
        [values[:HEAD_DIM, :rows], values[HEAD_DIM:, rows:]], axis=0
    )


def later_key(dims):
    key = lax.broadcasted_iota(jnp.int32, dims, 0)
    query = lax.rem(lax.broadcasted_iota(jnp.int32, dims, 1), QUERY_ROWS)
    return key > query


def block_rows_at(order, block, rows):
    return pl.ds(pl.multiple_of(order[block] * rows, rows), rows)


def rows_in_order(order, source, index, rows):
    per = QUERY_ROWS // rows
    return jnp.concatenate(
        [source[block_rows_at(order, index * per + i, rows), :] for i in range(per)], axis=0
    )


def slots(dealing, order):
    for slot in range(dealing.shape[1]):
        order[dealing[0, slot]] = slot


def unpack_output(weight, output_part):
    width = output_part.shape[0]
    if weight.shape[1] <= width + 2 * KV_WIDTH:
        return
    parts = output_part.shape[1] // width
    shards = width // HEAD_DIM
    for shard in range(shards):
        for part in range(parts):
            start = (shard * parts + part) * HEAD_DIM
            output_part[
                shard * HEAD_DIM : (shard + 1) * HEAD_DIM, part * width : (part + 1) * width
            ] = weight[start : start + HEAD_DIM, weight.shape[1] - width :]


def attend_body(
    block_rows,
    dealing,
    tokens_all,
    gain,
    weight,
    cosine,
    sine,
    attended,
    queries,
    keys,
    values,
    log_totals,
    first_across,
    heads_across,
    output_part,
    values_across,
    order,
):
    slots(dealing, order)
    unpack_output(weight, output_part)
    length, width = queries.shape
    kv_heads = keys.shape[0]
    pairs = width // LANES
    blocks = length // QUERY_ROWS

    def project(index, carry):
        place = pl.ds(pl.multiple_of(index * QUERY_ROWS, QUERY_ROWS), QUERY_ROWS)
        normed, _ = norm_parts(
            rows_in_order(order, tokens_all, index, block_rows).astype(jnp.float32)
        )
        rows = (normed * gain[...]).astype(jnp.bfloat16)
        turned_rows = rows.T
        for i in range(QUERY_ROWS // block_rows):
            first_across[
                :, block_rows_at(order, index * (QUERY_ROWS // block_rows) + i, block_rows)
            ] = turned_rows[:, i * block_rows : (i + 1) * block_rows]
        cos_rows, sin_rows = (cosine[place, :], sine[place, :])
        projected = product(rows, weight[:, :width])
        for pair in range(pairs):
            lanes = slice(pair * LANES, (pair + 1) * LANES)
            turned = turn(projected[:, lanes], cos_rows, sin_rows).astype(jnp.bfloat16)
            queries[place, lanes] = turned * jnp.asarray(1.0 / math.sqrt(HEAD_DIM), jnp.bfloat16)
        projected = product(rows, weight[:, width : width + 2 * kv_heads * HEAD_DIM])
        for head in range(2 * kv_heads):
            tile = projected[:, head // PAIR * LANES : (head // PAIR + 1) * LANES]
            if head < kv_heads:
                tile = turn(tile, cos_rows, sin_rows)
            low = low_lanes(tile.shape, HEAD_DIM)
            moved = pltpu.roll(tile, HEAD_DIM, 1)
            both = jnp.where(low, tile, moved) if head % PAIR == 0 else jnp.where(low, moved, tile)
            if head < kv_heads:
                keys[head, place, :] = both.astype(jnp.bfloat16)
            else:
                values[head - kv_heads, place, :] = both.astype(jnp.bfloat16)
                values_across[head - kv_heads, :, place] = both.T.astype(jnp.bfloat16)
        return carry

    lax.fori_loop(0, blocks, project, 0)

    def attend(pair, carry):
        kv_head = pair // (pairs // kv_heads)
        lanes = pl.ds(pl.multiple_of(pair * LANES, LANES), LANES)
        for index in range(blocks):
            seen = (index + 1) * QUERY_ROWS
            rows = two_heads(queries[index * QUERY_ROWS : seen, lanes])
            scores = times_transposed(keys[kv_head, :seen, :], rows)
            own = scores[seen - QUERY_ROWS :]
            own = jnp.where(later_key(own.shape), -1e30, own)
            if index:
                scores = jnp.concatenate([scores[: seen - QUERY_ROWS], own], axis=0)
            else:
                scores = own
            largest = jnp.max(scores, axis=0, keepdims=True)
            exponent = jnp.exp(scores - largest)
            totals = jnp.sum(exponent, axis=0, keepdims=True)
            mixed = product(values_across[kv_head, :, :seen], exponent.astype(jnp.bfloat16))
            log_totals[pl.ds(pair * blocks + index, 1), :] = largest + jnp.log(totals)
            across = pick_heads(mixed / totals).astype(jnp.bfloat16)
            for i in range(QUERY_ROWS // block_rows):
                heads_across[
                    lanes, block_rows_at(order, index * (QUERY_ROWS // block_rows) + i, block_rows)
                ] = across[:, i * block_rows : (i + 1) * block_rows]
            mixed = across.T
            per = QUERY_ROWS // block_rows
            for i in range(per):
                attended[block_rows_at(order, index * per + i, block_rows), lanes] = mixed[
                    i * block_rows : (i + 1) * block_rows
                ]
        return carry

    lax.fori_loop(0, pairs, attend, 0)


def attend_forward(block_rows, width, kv_heads, dealing, tokens_all, gain, weight, tables):
    length, _ = tokens_all.shape
    blocks = length // QUERY_ROWS
    wide = shape((kv_heads, length, LANES))
    return pl.pallas_call(
        functools.partial(attend_body, block_rows),
        out_shape=(
            shape((length, width)),
            shape((length, width)),
            wide,
            wide,
            shape((width // LANES * blocks, PAIR * QUERY_ROWS), jnp.float32),
            shape(tokens_all.shape[::-1]),
            shape((width, length)),
            shape((width, tokens_all.shape[1])),
        ),
        in_specs=[SMEM] + [VMEM] * 5,
        out_specs=(VMEM,) * 8,
        scratch_shapes=[
            pltpu.VMEM((kv_heads, LANES, length), jnp.bfloat16),
            pltpu.SMEM((length // block_rows,), jnp.int32),
        ],
        compiler_params=pltpu.CompilerParams(vmem_limit_bytes=VMEM_MEGABYTES << 20),
        cost_estimate=pl.CostEstimate(
            flops=3 * 10**10, bytes_accessed=10**7, transcendentals=10**7
        ),
    )(dealing, tokens_all, gain, weight, *tables)


def attend_back_body(
    block_rows,
    dealing,
    branch_all,
    output_weight,
    queries,
    keys,
    values,
    attended,
    log_totals,
    cosine,
    sine,
    grad_packed,
    grads,
    row_dots,
    keys_across,
    key_sums,
    value_sums,
    order,
):
    slots(dealing, order)
    length, width = queries.shape
    kv_heads = keys.shape[0]
    pairs = width // LANES
    blocks = length // QUERY_ROWS
    per = QUERY_ROWS // block_rows

    def project(index, carry):
        place = pl.ds(pl.multiple_of(index * QUERY_ROWS, QUERY_ROWS), QUERY_ROWS)
        rows = rows_in_order(order, branch_all, index, block_rows)
        low = times_transposed(rows, output_weight[...]).astype(jnp.bfloat16)
        grads[place, :] = low
        dots = low.astype(jnp.float32) * rows_in_order(order, attended, index, block_rows).astype(
            jnp.float32
        )
        for pair in range(pairs):
            across = dots[:, pair * LANES : (pair + 1) * LANES].T
            sums = [
                jnp.sum(across[i * HEAD_DIM : (i + 1) * HEAD_DIM], axis=0, keepdims=True)
                for i in range(PAIR)
            ]
            row_dots[pl.ds(pair * blocks + index, 1), :] = jnp.concatenate(sums, axis=1)
        for head in range(kv_heads):
            keys_across[head, :, place] = keys[head, place, :].T
        return carry

    lax.fori_loop(0, blocks, project, 0)

    group = pairs // kv_heads

    def attend(kv_head, carry):
        key_sums[kv_head] = jnp.zeros(key_sums.shape[1:], jnp.float32)
        value_sums[kv_head] = jnp.zeros(value_sums.shape[1:], jnp.float32)
        for member in range(group):
            pair = kv_head * group + member
            lanes = pl.ds(pl.multiple_of(pair * LANES, LANES), LANES)
            for index in range(blocks):
                seen = (index + 1) * QUERY_ROWS
                place = slice(index * QUERY_ROWS, seen)
                rows = two_heads(queries[place, lanes])
                grad_rows = two_heads(grads[place, lanes])
                row = pl.ds(pair * blocks + index, 1)
                scores = times_transposed(keys[kv_head, :seen, :], rows)
                weights = jnp.exp(scores - log_totals[row, :])
                own = weights[seen - QUERY_ROWS :]
                own = jnp.where(later_key(own.shape), 0.0, own)
                if index:
                    weights = jnp.concatenate([weights[: seen - QUERY_ROWS], own], axis=0)
                else:
                    weights = own
                grad_probs = times_transposed(values[kv_head, :seen, :], grad_rows)
                grad_scores = (weights * (grad_probs - row_dots[row, :])).astype(jnp.bfloat16)
                value_sums[kv_head, :seen, :] += product(weights.astype(jnp.bfloat16), grad_rows)
                key_sums[kv_head, :seen, :] += product(grad_scores, rows)
                turned = product(keys_across[kv_head, :, :seen], grad_scores)
                turned = pick_heads(turned).T * (1.0 / math.sqrt(HEAD_DIM))
                turned = turn(turned, cosine[place, :], -sine[place, :]).astype(jnp.bfloat16)
                for i in range(per):
                    grad_packed[block_rows_at(order, index * per + i, block_rows), lanes] = turned[
                        i * block_rows : (i + 1) * block_rows
                    ]
        return carry

    lax.fori_loop(0, kv_heads, attend, 0)

    def finish(block, carry):
        place = pl.ds(pl.multiple_of(block * block_rows, block_rows), block_rows)
        target = block_rows_at(order, block, block_rows)

        def head_sum(head):
            if head < kv_heads:
                tile = key_sums[head, place, :]
            else:
                tile = value_sums[head - kv_heads, place, :]
            tile = tile + pltpu.roll(tile, HEAD_DIM, 1)
            if head < kv_heads:
                tile = turn(tile, cosine[place, :], -sine[place, :])
            return tile

        for tile in range(2 * kv_heads // PAIR):
            first, second = (head_sum(tile * PAIR), head_sum(tile * PAIR + 1))
            joined = jnp.where(low_lanes(first.shape, HEAD_DIM), first, second)
            start = width + tile * LANES
            grad_packed[target, start : start + LANES] = joined.astype(jnp.bfloat16)
        return carry

    lax.fori_loop(0, length // block_rows, finish, 0)


def attend_backward(
    block_rows, dealing, branch_all, output_weight, queries, keys, values, attended, log_totals, tables
):
    length, width = queries.shape
    kv_heads = keys.shape[0]
    return pl.pallas_call(
        functools.partial(attend_back_body, block_rows),
        out_shape=shape((length, width + 2 * kv_heads * HEAD_DIM)),
        in_specs=[SMEM] + [VMEM] * 9,
        out_specs=VMEM,
        scratch_shapes=[
            pltpu.VMEM((length, width), jnp.bfloat16),
            pltpu.VMEM(log_totals.shape, jnp.float32),
            pltpu.VMEM((kv_heads, LANES, length), jnp.bfloat16),
            pltpu.VMEM((kv_heads, length, LANES), jnp.float32),
            pltpu.VMEM((kv_heads, length, LANES), jnp.float32),
            pltpu.SMEM((length // block_rows,), jnp.int32),
        ],
        compiler_params=pltpu.CompilerParams(vmem_limit_bytes=VMEM_MEGABYTES << 20),
        cost_estimate=pl.CostEstimate(
            flops=6 * 10**10, bytes_accessed=10**7, transcendentals=10**7
        ),
    )(
        dealing,
        branch_all,
        output_weight,
        queries,
        keys,
        values,
        attended,
        log_totals,
        *tables,
    )


def take_columns(matrix, outer, parts, index):
    rows, columns = matrix.shape
    pieces = matrix.reshape(rows, outer, parts, columns // (outer * parts))
    return lax.dynamic_index_in_dim(pieces, index, axis=2, keepdims=False).reshape(rows, -1)


def take_rows(matrix, parts, index):
    count = matrix.shape[0] // parts
    return lax.dynamic_slice_in_dim(matrix, index * count, count, axis=0)


def put_columns(gathered, outer):
    parts, rows, columns = gathered.shape
    return (
        gathered.reshape(parts, rows, outer, columns // outer)
        .transpose(1, 2, 0, 3)
        .reshape(rows, parts * columns)
    )


def gather_shards(array):
    return lax.all_gather(array, "fsdp", axis=0, tiled=True)


def scatter_shards(array, by_core=False):
    shards = lax.axis_size("fsdp")
    groups = [list(range(core, shards, 2)) for core in range(2)] if by_core else None
    return lax.psum_scatter(
        array.astype(jnp.bfloat16),
        "fsdp",
        scatter_dimension=0,
        tiled=True,
        axis_index_groups=groups,
    )


def per_device(
    tokens,
    dealing,
    first_gain,
    query_weight,
    key_weight,
    value_weight,
    output_weight,
    second_gain,
    gate_weight,
    up_weight,
    down_weight,
    cotangent,
):
    shard_count = lax.axis_size("fsdp")
    part_count = lax.axis_size("ctx")
    ctx_index = lax.axis_index("ctx")
    row_count = tokens.shape[1]
    block_rows = row_count // 2
    seq_rows = row_count * part_count
    part_width = D // part_count
    dealt_heads = D // shard_count // part_count == HEAD_DIM and part_count == 4
    kv_heads = KV_HEADS if dealt_heads else max(1, KV_HEADS // part_count)
    kv_first = 0 if dealt_heads else ctx_index * KV_HEADS // part_count
    tie = lax.optimization_barrier
    start = functools.partial(
        start_gather, part_count, shard_count, 1, tokens[0], first_gain[None], second_gain[None]
    )
    if dealt_heads:
        tokens_all, gain_first, gain_second, cosine, sine, packed, packed_hidden = start(
            query_weight, key_weight, value_weight, output_weight, gate_weight, up_weight
        )
        packed, packed_hidden = tie((packed, packed_hidden))
        gate_up_part = gather_shards(packed_hidden)
    else:
        tokens_all, gain_first, gain_second, cosine, sine = start()
        grad_out_all = lax.all_gather(cotangent[0], "ctx", axis=0, tiled=True)
        query_part = gather_shards(take_columns(query_weight, 1, part_count, ctx_index))
        output_part = take_rows(gather_shards(output_weight), part_count, ctx_index)
        key_value = gather_shards(jnp.concatenate([key_weight, value_weight], axis=1))
        key_value = key_value.reshape(D, 2, KV_HEADS, HEAD_DIM)
        key_value = lax.dynamic_slice_in_dim(key_value, kv_first, kv_heads, 2).reshape(D, -1)
        packed = jnp.concatenate([query_part, key_value], axis=1)
        gate_up_part = gather_shards(
            jnp.concatenate(
                [
                    take_columns(gate_weight, shard_count, part_count, ctx_index),
                    take_columns(up_weight, shard_count, part_count, ctx_index),
                ],
                axis=1,
            )
        )
    tables = (cosine, sine)
    down_part = gather_shards(take_rows(down_weight, part_count, ctx_index))

    forward = attend_forward(
        block_rows, part_width, kv_heads, dealing, tokens_all, gain_first, packed, tables
    )
    attended, query_rot, key_rot, value_rows, log_totals, first_across, heads_across = forward[:7]
    if dealt_heads:
        output_part = forward[7]
    residual_mid, second_all = middle_gather(
        part_count, 2, attended, output_part, tokens[0], gain_second
    )
    if dealt_heads:
        second_all, grad_out = tie((second_all, cotangent[0]))
        near = plane_near(grad_out)

    gate_up, hidden, second_across, hidden_across = hidden_forward(second_all, gate_up_part)
    if dealt_heads:
        hidden_across, *near = tie((hidden_across, *near))
        grad_out_all = place_rows(plane_far(near), jnp.bfloat16)
        down_term = core_grads(shard_count, 5, hidden_across, grad_out_all)
    else:
        down_term = column_term(hidden, grad_out_all)
    down_part, down_term = tie((down_part, down_term))
    down_piece = scatter_shards(down_term, dealt_heads)
    grad_gate_up = hidden_backward(grad_out_all, down_part, gate_up)
    if dealt_heads:
        *terms, output_sum = hidden_grads(
            part_count, shard_count, 6, second_across, grad_gate_up, hidden, down_part
        )
    else:
        gate_up_term = column_term(second_all, grad_gate_up).astype(jnp.bfloat16)
        terms = (gate_up_term[:, : FF // part_count], gate_up_term[:, FF // part_count :])
        output_partial = product(hidden, down_part).astype(jnp.bfloat16)
        output_sum = lax.psum_scatter(output_partial, "ctx", scatter_dimension=0, tiled=True)
    block_output = (residual_mid + output_sum.astype(jnp.float32)).astype(jnp.bfloat16)
    grad_gate_up, down_piece, *terms = tie((grad_gate_up, down_piece, *terms))
    gate_piece = scatter_shards(terms[0], dealt_heads)
    up_piece = scatter_shards(terms[1], dealt_heads)
    grad_mid, second_gain_part, branch_all = middle_back(
        part_count, 3, grad_gate_up, gate_up_part, residual_mid, gain_second, cotangent[0]
    )
    branch_all, gate_piece, down_piece = tie((branch_all, gate_piece, down_piece))
    if dealt_heads:
        down_near = plane_near(down_piece)
        gate_near = plane_near(gate_piece)

    grad_packed = attend_backward(
        block_rows,
        dealing,
        branch_all,
        output_part,
        query_rot,
        key_rot,
        value_rows,
        attended,
        log_totals,
        tables,
    )
    if dealt_heads:
        packed_term, *far = attention_grads(
            shard_count,
            7,
            first_across,
            grad_packed,
            heads_across,
            branch_all,
            *down_near[1:],
            *gate_near[1:],
        )
        down_parts, gate_parts = ((*down_near, *far[:2]), (*gate_near, *far[2:]))
        grad_packed, packed_term = tie((grad_packed, packed_term))
        packed_piece = scatter_shards(packed_term, True)
    grad_input, gain_shard, up_all = input_back(
        part_count,
        shard_count,
        4,
        grad_packed,
        packed,
        tokens[0],
        gain_first,
        grad_mid,
        second_gain_part,
        up_piece,
    )
    if dealt_heads:
        grad_input, packed_piece = tie((grad_input, packed_piece))
        packed_near = plane_near(packed_piece)
        gate_shard = place_hidden(shard_count, gate_parts)
        up_shard = place_sorted(shard_count, up_all)
        down_shard = place_rows(down_parts, jnp.float32)
        gate_shard, up_shard, *packed_near = tie((gate_shard, up_shard, *packed_near))
        query_shard, key_shard, value_shard, output_shard = place_attention(
            shard_count, plane_far(packed_near)
        )
    else:

        def gather_columns(piece, outer):
            return put_columns(lax.all_gather(piece, "ctx", axis=0), outer).astype(jnp.float32)

        gate_shard = gather_columns(gate_piece, shard_count)
        up_shard = put_columns(
            up_all.reshape(part_count, -1, FF // part_count), shard_count
        ).astype(jnp.float32)
        down_shard = lax.all_gather(down_piece, "ctx", axis=0, tiled=True).astype(jnp.float32)
        grad_query, grad_key_value = (grad_packed[:, :part_width], grad_packed[:, part_width:])
        query_piece = scatter_shards(product(first_across, grad_query))
        query_shard = gather_columns(query_piece, 1)
        key_value_piece = scatter_shards(product(first_across, grad_key_value))
        output_term = column_term(attended, branch_all)
        spread = jnp.zeros((D, D), jnp.float32)
        spread = lax.dynamic_update_slice_in_dim(
            spread, output_term, ctx_index * output_term.shape[0], 0
        )
        output_shard = lax.psum(scatter_shards(spread), "ctx").astype(jnp.float32)
        wide = jnp.zeros((D // shard_count, 2, KV_HEADS, HEAD_DIM), jnp.bfloat16)
        wide = lax.dynamic_update_slice_in_dim(
            wide, key_value_piece.reshape(-1, 2, kv_heads, HEAD_DIM), kv_first, 2
        )
        key_value_shard = lax.psum(wide.reshape(-1, 2 * KV_WIDTH), "ctx").astype(jnp.float32)
        key_shard, value_shard = (key_value_shard[:, :KV_WIDTH], key_value_shard[:, KV_WIDTH:])
    return (
        block_output[None],
        grad_input[None],
        gain_shard[0],
        query_shard,
        key_shard,
        value_shard,
        output_shard,
        gain_shard[1],
        gate_shard,
        up_shard,
        down_shard,
    )


def solution(mesh):
    in_specs = (
        P("fsdp", "ctx", None),
        P("fsdp", None),
        P("fsdp"),
        P("fsdp", None),
        P("fsdp", None),
        P("fsdp", None),
        P("fsdp", None),
        P("fsdp"),
        P("fsdp", None),
        P("fsdp", None),
        P("fsdp", None),
        P("fsdp", "ctx", None),
    )
    out_specs = (
        P("fsdp", "ctx", None),
        P("fsdp", "ctx", None),
        P("fsdp"),
        P("fsdp", None),
        P("fsdp", None),
        P("fsdp", None),
        P("fsdp", None),
        P("fsdp"),
        P("fsdp", None),
        P("fsdp", None),
        P("fsdp", None),
    )
    return jax.shard_map(
        per_device, mesh=mesh, in_specs=in_specs, out_specs=out_specs, check_vma=False
    )
```

```python
import functools
import math

import jax
import jax.numpy as jnp
from jax import lax
from jax.experimental import pallas as pl
from jax.experimental.pallas import tpu as pltpu
from jax.sharding import PartitionSpec as P

D = 2048
FF = 5632
HEADS = 32
KV_HEADS = 4
HEAD_DIM = 64
KV_WIDTH = 256


epsilon = 1e-05


MESH = pl.DeviceIdType.MESH
VMEM = pl.BlockSpec(memory_space=pltpu.VMEM)
SMEM = pl.BlockSpec(memory_space=pltpu.SMEM)
HBM = pl.BlockSpec(memory_space=pltpu.HBM)
LANES = 128
PAIR = LANES // HEAD_DIM
QUERY_ROWS = 256
VMEM_MEGABYTES = 60


def shape(dims, kind=jnp.bfloat16):
    return jax.ShapeDtypeStruct(dims, kind)


def norm_parts(values):
    inverse = lax.rsqrt(jnp.mean(values * values, axis=-1, keepdims=True) + epsilon)
    return (values * inverse, inverse)


def norm_back(gradient, normed, inverse):
    return inverse * (gradient - normed * jnp.mean(gradient * normed, axis=-1, keepdims=True))


def product(left_side, right_side):
    return jnp.dot(left_side, right_side, preferred_element_type=jnp.float32)


def times_transposed(left_side, right_side):
    return lax.dot_general(
        left_side, right_side, (((1,), (1,)), ((), ())), preferred_element_type=jnp.float32
    )


def column_term(source, gradient):
    return lax.dot_general(
        source, gradient, (((0,), (0,)), ((), ())), preferred_element_type=jnp.float32
    )


STRIP = 32
PIECES = 4


def plane_places():
    me = lax.axis_index("ctx")
    return (me, me + 1 - 2 * lax.rem(me, 2), lax.rem(me + 2, 4), 3 - me)


def signal(barrier, **place):
    pl.semaphore_signal(barrier, inc=1, device_id=place, device_id_type=MESH)


def meet(count, shards=1):
    me = lax.axis_index("ctx")
    barrier = pltpu.get_barrier_semaphore()
    for step in range(1, count):
        signal(barrier, ctx=lax.rem(me + step, count))
    for step in range(1, shards):
        signal(barrier, fsdp=lax.rem(lax.axis_index("fsdp") + step, shards))
    pl.semaphore_wait(barrier, count - 1 + shards - 1)


def remote(source, target, send_sem, recv_sem, **place):
    copy = pltpu.make_async_remote_copy(
        src_ref=source,
        dst_ref=target,
        send_sem=send_sem,
        recv_sem=recv_sem,
        device_id=place,
        device_id_type=MESH,
    )
    copy.start()
    return copy


def gather_sems(count):
    sends = 3 if count == 4 else count - 1
    return [
        pltpu.SemaphoreType.DMA((PIECES,)),
        pltpu.SemaphoreType.DMA((sends, PIECES)),
        pltpu.SemaphoreType.DMA((sends, PIECES)),
    ]


class RowGather:
    def __init__(self, count, own, out, sems):
        self.count, self.own, self.out = (count, own, out)
        self.local_sem, self.send_sem, self.recv_sem = sems
        self.size = own.shape[0] // PIECES
        self.copies = [[] for _ in range(PIECES)]
        self.relays = []

    def place(self, owner, piece):
        start = owner * self.own.shape[0] + piece * self.size
        return self.out.at[pl.ds(pl.multiple_of(start, self.size), self.size)]

    def send(self, piece):
        me = lax.axis_index("ctx")
        source = self.own.at[pl.ds(piece * self.size, self.size)]
        target = self.place(me, piece)
        if self.count == 4:
            _, across, along, _ = plane_places()
            peers = (across, along)
        else:
            peers = [lax.rem(me + step, self.count) for step in range(1, self.count)]
        for index, peer in enumerate(peers):
            self.copies[piece].append(
                remote(
                    source,
                    target,
                    self.send_sem.at[index, piece],
                    self.recv_sem.at[index, piece],
                    ctx=peer,
                )
            )
        local = pltpu.make_async_copy(source, target, self.local_sem.at[piece])
        local.start()
        self.copies[piece].append(local)

    def finish(self):
        self.relay()
        self.drain()

    def relay(self, pieces=(0, PIECES // 2, 1, PIECES // 2 + 1)):
        relays = self.relays
        if self.count != 4:
            return
        _, across, along, _ = plane_places()
        for piece in pieces:
            first = piece < PIECES // 2
            came, left = (0, 1) if first else (1, 0)
            owner, peer = (across, along) if first else (along, across)
            self.copies[piece][came].wait_recv()
            block = self.place(owner, piece)
            relays.append(
                remote(
                    block, block, self.send_sem.at[2, piece], self.recv_sem.at[2, piece], ctx=peer
                )
            )

    def drain(self):
        if self.count != 4:
            for copies in self.copies:
                for copy in copies:
                    copy.wait()
            return
        for piece in range(PIECES):
            to_across, to_along, local = self.copies[piece]
            (to_along if piece < PIECES // 2 else to_across).wait_recv()
            to_across.wait_send()
            to_along.wait_send()
            local.wait()
        for relay in self.relays:
            relay.wait()


CHUNKS = 2


def line_sems(shards):
    hops = shards // 2 - 1
    return [
        pltpu.SemaphoreType.DMA,
        pltpu.SemaphoreType.DMA((2 * hops, CHUNKS)),
        pltpu.SemaphoreType.DMA((2 * hops, CHUNKS)),
        pltpu.SemaphoreType.DMA((2 * hops + 1, CHUNKS)),
        pltpu.SemaphoreType.DMA((2 * hops + 1, CHUNKS)),
    ]


class LineGather:
    def __init__(self, shards, own, out, sems):
        self.own, self.out = (own, out)
        self.local_sem, self.send_sem, self.recv_sem, self.core_send, self.core_recv = sems
        self.me = lax.axis_index("fsdp")
        self.hops = shards // 2 - 1
        self.chip = self.me // 2
        self.twin = self.me + 1 - 2 * lax.rem(self.me, 2)
        self.size = own.shape[0] // CHUNKS

    def block(self, owner, chunk):
        start = owner * self.own.shape[0] + chunk * self.size
        return self.out.at[pl.ds(pl.multiple_of(start, self.size), self.size)]

    def copy(self, distance, way, chunk, sems, index, peer):
        owner = self.me - 2 * (1 - 2 * way) * distance
        target = self.block(owner, chunk)
        part = pl.ds(chunk * self.size, self.size)
        send_sem, recv_sem = sems
        return pltpu.make_async_remote_copy(
            src_ref=self.own.at[part] if distance == 0 else target,
            dst_ref=target,
            send_sem=send_sem.at[index, chunk],
            recv_sem=recv_sem.at[index, chunk],
            device_id={"fsdp": peer},
            device_id_type=MESH,
        )

    def hop(self, way, distance, chunk):
        sems = (self.send_sem, self.recv_sem)
        peer = self.me + 2 * (1 - 2 * way)
        return self.copy(distance, way, chunk, sems, way * self.hops + distance, peer)

    def cross(self, way, distance, chunk):
        index = distance if way == 0 else self.hops + distance
        sems = (self.core_send, self.core_recv)
        return self.copy(distance, way, chunk, sems, index, self.twin)

    def can_send(self, way):
        return self.chip < self.hops if way == 0 else self.chip > 0

    def behind(self, way, distance):
        return self.chip >= distance if way == 0 else self.chip + distance <= self.hops

    def local(self):
        rows = self.own.shape[0]
        target = self.out.at[pl.ds(pl.multiple_of(self.me * rows, rows), rows)]
        return pltpu.make_async_copy(self.own, target, self.local_sem)

    def start(self, chunk):
        for way in (0, 1):
            pl.when(self.can_send(way))(lambda way=way: self.hop(way, 0, chunk).start())
        self.cross(0, 0, chunk).start()
        if chunk == 0:
            self.local().start()

    def step(self, distance, chunk):
        for way in (0, 1):

            @pl.when(self.behind(way, distance))
            def _(way=way):
                self.hop(way, distance - 1, chunk).wait_recv()
                if distance < self.hops:
                    pl.when(self.can_send(way))(lambda: self.hop(way, distance, chunk).start())
                self.cross(way, distance, chunk).start()

    def drain(self):
        for chunk in range(CHUNKS):
            for way in (0, 1):
                for distance in range(self.hops):
                    here = jnp.logical_and(self.can_send(way), self.behind(way, distance))
                    pl.when(here)(
                        lambda way=way, d=distance, chunk=chunk: self.hop(way, d, chunk).wait_send()
                    )
                for distance in range(1, self.hops + 1):
                    pl.when(self.behind(way, distance))(
                        lambda way=way, d=distance, chunk=chunk: self.cross(way, d, chunk).wait()
                    )
            self.cross(0, 0, chunk).wait()
        self.local().wait()


TILE = 512


def begin(source, target, sem):
    copy = pltpu.make_async_copy(source, target, sem)
    copy.start()
    return copy


class Scatter:
    def __init__(self, count, left, right, transposed, refs):
        self.count, self.transposed = (count, transposed)
        self.left_buf, self.right_buf, self.load_sem, *refs = refs
        self.send_buf, self.recv_buf, self.kept, self.total, self.send_sem, self.recv_sem = refs
        self.rows, self.width = self.total.shape
        self.tiles = self.width // TILE
        self.loads = {}
        owners = self.owners()
        depth = self.left_buf.shape[1]
        self.load_left(left, owners[0], 0)
        for tile in range(self.tiles):
            columns = pl.ds(tile * TILE, TILE)
            if transposed:
                place = (columns, pl.ds(0, depth))
                source, target = (right.at[place], self.right_buf.at[columns])
            else:
                source, target = (right.at[:, columns], self.right_buf.at[:, columns])
            self.loads["tile", tile] = begin(source, target, self.load_sem.at[count + tile])
        for index in range(1, count):
            self.load_left(left, owners[index], index)

    def owners(self):
        me = lax.axis_index("ctx")
        if self.count != 4:
            return [lax.rem(me + step, self.count) for step in range(1, self.count)] + [me]
        _, across, along, corner = plane_places()
        return [corner, across, along, me]

    def block_rows(self, owner):
        return pl.ds(pl.multiple_of(owner * self.rows, self.rows), self.rows)

    def load_left(self, left, owner, index):
        rows = self.block_rows(owner)
        self.loads["left", index] = begin(
            left.at[rows], self.left_buf.at[rows], self.load_sem.at[index]
        )

    def tile(self, owner, columns):
        piece = self.left_buf[self.block_rows(owner), :]
        if self.transposed:
            return times_transposed(piece, self.right_buf[columns, :])
        return product(piece, self.right_buf[:, columns])

    def block(self, index, store):
        owner = self.owners()[index]
        self.loads["left", index].wait()

        def column(tile, carry):
            columns = pl.ds(pl.multiple_of(tile * TILE, TILE), TILE)
            store(columns, self.tile(owner, columns))
            return carry

        lax.fori_loop(0, self.tiles, column, 0)

    def send(self, slot, part, columns, sem, peer):
        return remote(
            self.send_buf.at[slot, part, columns],
            self.recv_buf.at[slot, part, columns],
            self.send_sem.at[sem],
            self.recv_sem.at[sem],
            ctx=peer,
        )

    def store_own(self, columns, value):
        self.total[:, columns] = value

    def run(self, others=()):
        if self.count == 4:
            self.run_relayed(list(others))
        else:
            self.run_direct()
            for other in others:
                other()

    def run_direct(self):
        for tile in range(self.tiles):
            self.loads["tile", tile].wait()
        copies = []
        everything = (pl.ds(0, self.rows), pl.ds(0, self.width))
        for index, owner in enumerate(self.owners()[:-1]):

            def store_sent(columns, value, index=index):
                self.send_buf[index, :, columns] = value.astype(self.send_buf.dtype)

            self.block(index, store_sent)
            copies.append(self.send(index, *everything, index, owner))
        self.block(self.count - 1, self.store_own)
        self.relays, self.copies = ([], copies)

    def run_relayed(self, others):
        corner, across, along, me = self.owners()
        send_buf, kept, tiles = (self.send_buf, self.kept, self.tiles)
        half = self.rows // 2
        low, high = (pl.ds(0, half), pl.ds(half, half))
        whole = pl.ds(0, self.width)
        relays = []
        self.loads["left", 0].wait()
        for tile in range(tiles):
            columns = pl.ds(tile * TILE, TILE)
            self.loads["tile", tile].wait()
            send_buf[0, :, columns] = self.tile(corner, columns).astype(send_buf.dtype)
            relays.append(
                (
                    self.send(0, low, columns, tile, across),
                    self.send(0, high, columns, tiles + tile, along),
                )
            )

        def store_across(columns, value):
            send_buf[1, low, columns] = value[:half].astype(send_buf.dtype)
            kept[high, columns] = value[half:]

        def store_along(columns, value):
            send_buf[1, high, columns] = value[half:].astype(send_buf.dtype)
            kept[low, columns] = value[:half]

        self.block(1, store_across)
        copies = [self.send(1, low, whole, 4 * tiles, across)]
        self.block(2, store_along)
        copies.append(self.send(1, high, whole, 4 * tiles + 1, along))
        self.block(3, self.store_own)
        for _ in range(len(others) - tiles - 1):
            others.pop(0)()
        for tile in range(tiles):
            columns = pl.ds(tile * TILE, TILE)
            for side, peer in ((0, along), (1, across)):
                if others and side == 0:
                    others.pop(0)()
                relays[tile][side].wait_recv()
                part = (low, high)[side]

                def add(where, columns=columns):
                    value = kept[where, columns] + self.recv_buf[0, where, columns].astype(
                        jnp.float32
                    )
                    send_buf[2, where, columns] = value.astype(send_buf.dtype)

                for_strips(side * half, half, add)
                sem = (2 + side) * tiles + tile
                copies.append(self.send(2, part, columns, sem, peer))
        self.relays, self.copies = (relays, copies)
        for other in others:
            other()

    def finish(self):
        for pair in self.relays:
            for copy in pair:
                copy.wait_send()
        for copy in self.copies:
            copy.wait()


def scatter_scratch(count, rows, width, left, right, transposed, depth):
    slots = 3 if count == 4 else count - 1
    sems = 4 * (width // TILE) + 2 if count == 4 else count - 1
    return [
        pltpu.VMEM(left.shape, jnp.bfloat16),
        pltpu.VMEM((width, depth) if transposed else (depth, width), jnp.bfloat16),
        pltpu.SemaphoreType.DMA((count + width // TILE,)),
        pltpu.VMEM((slots, rows, width), jnp.bfloat16),
        pltpu.VMEM((slots, rows, width), jnp.bfloat16),
        pltpu.VMEM((rows, width) if count == 4 else (8, LANES), jnp.float32),
        pltpu.VMEM((rows, width), jnp.float32),
        pltpu.SemaphoreType.DMA((sems,)),
        pltpu.SemaphoreType.DMA((sems,)),
    ]


SCATTER_REFS = 9


def side_loads(sources, refs):
    *targets, sem = refs
    return [begin(source, target, sem.at[i]) for i, (source, target) in enumerate(zip(sources, targets))]


def side_scratch(*arrays):
    return [pltpu.VMEM(a.shape, a.dtype) for a in arrays] + [
        pltpu.SemaphoreType.DMA((len(arrays),))
    ]


def received(count, recv_buf, total, rows):
    value = total[rows, :]
    for slot in (1, 2) if count == 4 else range(count - 1):
        value = value + recv_buf[slot, rows, :].astype(jnp.float32)
    return value


def for_strips(first, rows, body):
    def strip(index, carry):
        body(pl.ds(pl.multiple_of(first + index * STRIP, STRIP), STRIP))
        return carry

    lax.fori_loop(0, rows // STRIP, strip, 0)


def call_plane(body, ident, outs, out_specs, in_specs, scratch, flops, megabytes, args):
    return pl.pallas_call(
        body,
        out_shape=outs,
        in_specs=in_specs,
        out_specs=out_specs,
        scratch_shapes=scratch,
        compiler_params=pltpu.CompilerParams(
            collective_id=ident, has_side_effects=True, vmem_limit_bytes=megabytes << 20
        ),
        cost_estimate=pl.CostEstimate(
            flops=flops, bytes_accessed=flops // 300, transcendentals=0
        ),
    )(*args)


def for_part(body):
    me = lax.axis_index("ctx")
    for part in range(4):

        @pl.when(me == part)
        def _(part=part):
            body(part)


def strided_columns(values, shards, part):
    span = values.shape[1] // (4 * shards)
    starts = [(shard * 4 + part) * span for shard in range(shards)]
    wide = values.astype(jnp.float32)
    return jnp.concatenate([wide[:, i : i + span] for i in starts], axis=1).astype(values.dtype)


def pack_attention(shards, query, key, value, output, packed):
    def body(part):
        width = query.shape[1] // 4
        rows = output.shape[0] // 4
        packed[:, :width] = strided_columns(query[...], shards, part)
        packed[:, width : width + KV_WIDTH] = key[...]
        packed[:, width + KV_WIDTH : width + 2 * KV_WIDTH] = value[...]
        for index in range(4):
            packed[index * rows : (index + 1) * rows, width + 2 * KV_WIDTH :] = output[
                part * rows : (part + 1) * rows, index * width : (index + 1) * width
            ]

    for_part(body)


def pack_hidden(shards, gate, up, packed):
    def body(part):
        width = packed.shape[1] // 2

        def strip(where):
            packed[where, :width] = strided_columns(gate[where, :], shards, part)
            packed[where, width:] = strided_columns(up[where, :], shards, part)

        for_strips(0, packed.shape[0], strip)

    for_part(body)


def write_tables(cosine, sine):
    half = HEAD_DIM // 2

    def strip(where):
        dims = (STRIP, LANES)
        lane = lax.broadcasted_iota(jnp.int32, dims, 1)
        place = lax.broadcasted_iota(jnp.int32, dims, 0) + where.start
        index = lax.rem(lane, half).astype(jnp.float32)
        frequency = jnp.exp(-math.log(10000.0) * index * (2.0 / HEAD_DIM))
        angles = place.astype(jnp.float32) * frequency
        cosine[where, :] = jnp.cos(angles)
        sine[where, :] = jnp.where(low_lanes(dims, half), -jnp.sin(angles), jnp.sin(angles))

    for_strips(0, cosine.shape[0], strip)


def start_body(count, shards, tokens, first_gain, second_gain, *refs):
    if count == 4:
        weights, refs = (refs[:6], refs[6:])
    tokens_all, gain_first, gain_second, cosine, sine, *refs = refs
    if count == 4:
        weights_all, packed_hidden, *refs = refs
    gains, gains_all, gain_send, gain_recv, *refs = refs
    first = RowGather(count, tokens, tokens_all, refs[:3])
    half = PIECES // 2
    if count == 4:
        packed, gate, up, load_sem, *line_refs = refs[3:]
        loads = [
            begin(weights[4 + i], target, load_sem.at[i]) for i, target in enumerate((gate, up))
        ]
        line = LineGather(shards, packed, weights_all, line_refs)
        pack_attention(shards, *weights[:4], packed)
    meet(count, shards)
    if count == 4:
        line.start(0)
    first.send(0)
    first.send(half)
    me = lax.axis_index("fsdp")
    gains[0:1, :] = first_gain[...]
    gains[1:2, :] = second_gain[...]
    gains_all[me] = gains[...]
    copies = []
    for step in range(1, shards):
        copies.append(
            remote(
                gains,
                gains_all.at[me],
                gain_send.at[step - 1],
                gain_recv.at[step - 1],
                fsdp=lax.rem(me + step, shards),
            )
        )
    if count != 4:
        write_tables(cosine, sine)
        first.send(1)
        first.send(half + 1)
        first.finish()
    else:
        steps = [(d, c) for d in range(1, line.hops + 1) for c in range(CHUNKS)]
        write_tables(cosine, sine)
        for chunk in range(1, CHUNKS):
            line.start(chunk)
        line.step(*steps[0])
        first.relay((0, half))
        first.send(1)
        first.send(half + 1)
        for step in steps[1:3]:
            line.step(*step)
        for load in loads:
            load.wait()
        pack_hidden(shards, gate, up, packed_hidden)
        first.relay((1, half + 1))
        for step in steps[3:-1]:
            line.step(*step)
        first.drain()
    for copy in copies:
        copy.wait()
    span = gains.shape[1]
    for shard in range(shards):
        lanes = slice(shard * span, (shard + 1) * span)
        gain_first[:, lanes] = gains_all[shard, 0:1, :].astype(jnp.float32)
        gain_second[:, lanes] = gains_all[shard, 1:2, :].astype(jnp.float32)
    if count == 4:
        line.step(*steps[-1])
        line.drain()


def start_gather(count, shards, ident, tokens, first_gain, second_gain, *weights):
    rows, width = tokens.shape
    span = first_gain.shape[1]
    wide = shape((1, width), jnp.float32)
    table = shape((count * rows, LANES), jnp.float32)
    outs = [shape((count * rows, width)), wide, wide, table, table]
    out_specs = [HBM] + [VMEM] * 4
    in_specs = [HBM, VMEM, VMEM]
    scratch = [
        pltpu.VMEM((2, span), jnp.bfloat16),
        pltpu.VMEM((shards, 2, span), jnp.bfloat16),
        pltpu.SemaphoreType.DMA((shards - 1,)),
        pltpu.SemaphoreType.DMA((shards - 1,)),
    ] + gather_sems(count)
    if weights:
        height = weights[0].shape[0]
        packed = width // 2 + 2 * KV_WIDTH
        outs += [shape((shards * height, packed)), shape((height, FF // 2))]
        out_specs += [HBM, VMEM]
        in_specs += [VMEM] * 4 + [HBM] * 2
        scratch += [
            pltpu.VMEM((height, packed), jnp.bfloat16),
            pltpu.VMEM((height, FF), jnp.bfloat16),
            pltpu.VMEM((height, FF), jnp.bfloat16),
            pltpu.SemaphoreType.DMA((2,)),
        ] + line_sems(shards)
    return call_plane(
        functools.partial(start_body, count, shards),
        ident,
        tuple(outs),
        tuple(out_specs),
        in_specs,
        scratch,
        5 * 10**10,
        VMEM_MEGABYTES,
        (tokens, first_gain, second_gain, *weights),
    )


def strips_and_send(gather, strip):
    size = gather.size
    for piece in range(PIECES):
        for_strips(piece * size, size, strip)
        gather.send(piece)
    gather.finish()


def middle_body(count, attended, weight, tokens, gain, residual, second_all, own, *refs):
    scatter = Scatter(count, attended, weight, False, refs[:SCATTER_REFS])
    side = refs[SCATTER_REFS : SCATTER_REFS + 2]
    loads = side_loads([tokens], side)
    meet(count)
    scatter.run()
    scatter.finish()
    for load in loads:
        load.wait()

    def strip(where):
        values = side[0][where, :].astype(jnp.float32) + received(
            count, scatter.recv_buf, scatter.total, where
        )
        residual[where, :] = values
        normed, _ = norm_parts(values)
        own[where, :] = (normed * gain[...]).astype(jnp.bfloat16)

    strips_and_send(RowGather(count, own, second_all, refs[SCATTER_REFS + 2 :]), strip)


def middle_gather(count, ident, attended, weight, tokens, gain):
    rows, width = tokens.shape
    return call_plane(
        functools.partial(middle_body, count),
        ident,
        (shape((rows, width), jnp.float32), shape((count * rows, width))),
        (VMEM, HBM),
        [HBM] * 3 + [VMEM],
        [pltpu.VMEM((rows, width), jnp.bfloat16)]
        + scatter_scratch(count, rows, width, attended, weight, False, attended.shape[1])
        + side_scratch(tokens)
        + gather_sems(count),
        6 * 10**10,
        VMEM_MEGABYTES,
        (attended, weight, tokens, gain),
    )


def middle_back_body(
    count, grad_gate_up, gate_up_weight, residual, grad_out, gain, grad_mid, gain_part, branch_all, own,
    *refs
):
    scatter = Scatter(count, grad_gate_up, gate_up_weight, True, refs[:SCATTER_REFS])
    side = refs[SCATTER_REFS : SCATTER_REFS + 3]
    loads = side_loads([residual, grad_out], side)
    meet(count)
    scatter.run()
    scatter.finish()
    gain_part[...] = jnp.zeros_like(gain_part)
    for load in loads:
        load.wait()

    def strip(where):
        gradient = received(count, scatter.recv_buf, scatter.total, where)
        normed, inverse = norm_parts(side[0][where, :])
        gain_part[...] += jnp.sum(gradient * normed, axis=0, keepdims=True)
        values = side[1][where, :].astype(jnp.float32) + norm_back(
            gradient * gain[...], normed, inverse
        )
        grad_mid[where, :] = values
        own[where, :] = values.astype(jnp.bfloat16)

    strips_and_send(RowGather(count, own, branch_all, refs[SCATTER_REFS + 3 :]), strip)


def column_halves(array):
    rows, width = array.shape
    if width // 2 % LANES:
        return ((array[:, : width // 2], array[:, width // 2 :]), (VMEM, VMEM))
    specs = [pl.BlockSpec((rows, width // 2), lambda *index, side=side: (0, side)) for side in (0, 1)]
    return ((array, array), specs)


def middle_back(count, ident, grad_gate_up, gate_up_weight, residual, gain, grad_out):
    rows, width = residual.shape
    return call_plane(
        functools.partial(middle_back_body, count),
        ident,
        (
            shape((rows, width), jnp.float32),
            shape((1, width), jnp.float32),
            shape((count * rows, width)),
        ),
        (VMEM, VMEM, HBM),
        [HBM] * 4 + [VMEM],
        [pltpu.VMEM((rows, width), jnp.bfloat16)]
        + scatter_scratch(
            count, rows, width, grad_gate_up, gate_up_weight, True, grad_gate_up.shape[1]
        )
        + side_scratch(residual, grad_out)
        + gather_sems(count),
        6 * 10**10,
        VMEM_MEGABYTES,
        (grad_gate_up, gate_up_weight, residual, grad_out, gain),
    )


def input_back_body(
    count, shards, grad_packed, weight, tokens, piece, gain, second_part, grad_input, gain_sums,
    piece_all, gain_part, parts, part_recv, sums, sums_recv, part_send_sem, part_recv_sem, sums_send_sem,
    sums_recv_sem, *refs
):
    scatter = Scatter(count, grad_packed, weight, True, refs[:SCATTER_REFS])
    side = refs[SCATTER_REFS : SCATTER_REFS + 2]
    loads = side_loads([tokens], side)
    gather = RowGather(count, piece, piece_all, refs[SCATTER_REFS + 2 :])
    meet(count, shards)
    scatter.run()
    for part in range(PIECES):
        gather.send(part)
    scatter.finish()
    gain_part[...] = jnp.zeros_like(gain_part)
    for load in loads:
        load.wait()

    def strip(where):
        gradient = received(count, scatter.recv_buf, scatter.total, where)
        normed, inverse = norm_parts(side[0][where, :].astype(jnp.float32))
        gain_part[...] += jnp.sum(gradient * normed, axis=0, keepdims=True)
        grad_input[where, :] = norm_back(gradient * gain[...], normed, inverse)

    for_strips(0, grad_input.shape[0], strip)
    gather.relay()
    me = lax.axis_index("fsdp")
    span = parts.shape[2]
    for shard in range(shards):
        lanes = slice(shard * span, (shard + 1) * span)
        parts[shard, 0:1, :] = gain_part[:, lanes]
        parts[shard, 1:2, :] = second_part[:, lanes]
    copies = []
    for step in range(1, shards):
        peer = lax.rem(me + step, shards)
        copies.append(
            remote(
                parts.at[peer],
                part_recv.at[step - 1],
                part_send_sem.at[step - 1],
                part_recv_sem.at[step - 1],
                fsdp=peer,
            )
        )
    for copy in copies:
        copy.wait()
    value = parts[me]
    for step in range(1, shards):
        value = value + part_recv[step - 1]
    sums[...] = value
    copies = []
    for step in range(1, count):
        copies.append(
            remote(
                sums,
                sums_recv.at[step - 1],
                sums_send_sem.at[step - 1],
                sums_recv_sem.at[step - 1],
                ctx=lax.rem(lax.axis_index("ctx") + step, count),
            )
        )
    for copy in copies:
        copy.wait()
    for step in range(1, count):
        value = value + sums_recv[step - 1]
    gain_sums[...] = value
    gather.drain()


def input_back(
    count, shards, ident, grad_packed, weight, tokens, gain, second_part, piece
):
    rows, width = tokens.shape
    span = width // shards
    return call_plane(
        functools.partial(input_back_body, count, shards),
        ident,
        (
            shape((rows, width), jnp.float32),
            shape((2, span), jnp.float32),
            shape((count * piece.shape[0], piece.shape[1])),
        ),
        (VMEM, VMEM, HBM),
        [HBM] * 4 + [VMEM] * 2,
        [
            pltpu.VMEM((1, width), jnp.float32),
            pltpu.VMEM((shards, 2, span), jnp.float32),
            pltpu.VMEM((shards - 1, 2, span), jnp.float32),
            pltpu.VMEM((2, span), jnp.float32),
            pltpu.VMEM((count - 1, 2, span), jnp.float32),
            pltpu.SemaphoreType.DMA((shards - 1,)),
            pltpu.SemaphoreType.DMA((shards - 1,)),
            pltpu.SemaphoreType.DMA((count - 1,)),
            pltpu.SemaphoreType.DMA((count - 1,)),
        ]
        + scatter_scratch(count, rows, width, grad_packed, weight, True, grad_packed.shape[1])
        + side_scratch(tokens)
        + gather_sems(count),
        5 * 10**10,
        VMEM_MEGABYTES,
        (grad_packed, weight, tokens, piece, gain, second_part),
    )


def swap(array, along):
    pairs = [(i, (i + 2) % 4) if along else (i, i + 1 - 2 * (i % 2)) for i in range(4)]
    return lax.ppermute(array, "ctx", pairs)


def plane_near(array):
    return (array, swap(array, False), swap(array, True))


def plane_far(near):
    _, across, along = near
    half = across.shape[0] // 2
    return (*near, swap(across[:half], True), swap(along[half:], False))


def plane_gather(array):
    return plane_far(plane_near(array))


def hidden_body(rows, gate_weight, up_weight, gate_up, hidden, rows_across, hidden_across):
    width = hidden.shape[1]
    rows_across[...] = rows[...].T
    gate = product(rows[...], gate_weight[...])
    gate_up[:, :width] = gate
    upward = product(rows[...], up_weight[...])
    gate_up[:, width:] = upward
    low = (gate * jax.nn.sigmoid(gate) * upward).astype(jnp.bfloat16)
    hidden[...] = low
    hidden_across[...] = low.T


def hidden_forward(second_all, gate_up_weight):
    length, depth = second_all.shape
    width = gate_up_weight.shape[1] // 2
    (gate_weight, up_weight), specs = column_halves(gate_up_weight)
    step = QUERY_ROWS
    return pl.pallas_call(
        hidden_body,
        grid=(length // step,),
        out_shape=(
            shape((length, 2 * width), jnp.float32),
            shape((length, width)),
            shape((depth, length)),
            shape((width, length)),
        ),
        in_specs=[pl.BlockSpec((step, depth), lambda i: (i, 0))] + list(specs),
        out_specs=(
            pl.BlockSpec((step, 2 * width), lambda i: (i, 0)),
            pl.BlockSpec((step, width), lambda i: (i, 0)),
            pl.BlockSpec((depth, step), lambda i: (0, i)),
            pl.BlockSpec((width, step), lambda i: (0, i)),
        ),
        compiler_params=pltpu.CompilerParams(vmem_limit_bytes=VMEM_MEGABYTES << 20),
        cost_estimate=pl.CostEstimate(
            flops=4 * length * depth * width, bytes_accessed=3 * 10**7, transcendentals=10**6
        ),
    )(second_all, gate_weight, up_weight)


def hidden_back_body(grad_rows, down_weight, gate_up, grad_gate_up):
    width = down_weight.shape[0]
    grad_hidden = times_transposed(grad_rows[...], down_weight[...])
    gate, upward = (gate_up[:, :width], gate_up[:, width:])
    sigmoid_gate = jax.nn.sigmoid(gate)
    silu_gate = gate * sigmoid_gate
    grad_gate = grad_hidden * upward * sigmoid_gate * (1.0 + gate * (1.0 - sigmoid_gate))
    grad_gate_up[:, :width] = grad_gate.astype(jnp.bfloat16)
    grad_gate_up[:, width:] = (grad_hidden * silu_gate).astype(jnp.bfloat16)


def hidden_backward(grad_out_all, down_weight, gate_up):
    length, depth = grad_out_all.shape
    width = down_weight.shape[0]
    step = QUERY_ROWS
    return pl.pallas_call(
        hidden_back_body,
        grid=(length // step,),
        out_shape=shape((length, 2 * width)),
        in_specs=[
            pl.BlockSpec((step, depth), lambda i: (i, 0)),
            pl.BlockSpec((width, depth), lambda i: (0, 0)),
            pl.BlockSpec((step, 2 * width), lambda i: (i, 0)),
        ],
        out_specs=pl.BlockSpec((step, 2 * width), lambda i: (i, 0)),
        compiler_params=pltpu.CompilerParams(vmem_limit_bytes=VMEM_MEGABYTES << 20),
        cost_estimate=pl.CostEstimate(
            flops=4 * length * depth * width, bytes_accessed=3 * 10**7, transcendentals=10**6
        ),
    )(grad_out_all, down_weight, gate_up)


def meet_twin(neighbours=False):
    me = lax.axis_index("fsdp")
    barrier = pltpu.get_barrier_semaphore()
    signal(barrier, fsdp=me + 1 - 2 * lax.rem(me, 2))
    if neighbours:
        _, across, along, _ = plane_places()
        signal(barrier, ctx=across)
        signal(barrier, ctx=along)
    pl.semaphore_wait(barrier, 3 if neighbours else 1)


def shard_rows(array, shards, core):
    span = array.shape[0] // shards
    starts = [pl.multiple_of((2 * i + core) * span, 16) for i in range(shards // 2)]
    return jnp.concatenate([array[pl.ds(start, span), :] for start in starts], axis=0)


GRAD_TILE = 256


class CoreSum:
    def __init__(self, send_buf, recv_buf, send_sem, recv_sem):
        self.send_buf, self.recv_buf = (send_buf, recv_buf)
        self.send_sem, self.recv_sem = (send_sem, recv_sem)

    def copy(self, tile):
        me = lax.axis_index("fsdp")
        columns = pl.ds(pl.multiple_of(tile * GRAD_TILE, GRAD_TILE), GRAD_TILE)
        return pltpu.make_async_remote_copy(
            src_ref=self.send_buf.at[:, columns],
            dst_ref=self.recv_buf.at[:, columns],
            send_sem=self.send_sem.at[tile],
            recv_sem=self.recv_sem.at[tile],
            device_id={"fsdp": me + 1 - 2 * lax.rem(me, 2)},
            device_id_type=MESH,
        )


def column_tile(tile):
    return pl.ds(pl.multiple_of(tile * GRAD_TILE, GRAD_TILE), GRAD_TILE)


def core_grads_body(shards, across, gradient, out, half, send_buf, recv_buf, send_sem, recv_sem):
    core = lax.rem(lax.axis_index("fsdp"), 2)
    tiles = gradient.shape[1] // GRAD_TILE
    sums = CoreSum(send_buf, recv_buf, send_sem, recv_sem)
    half[...] = shard_rows(across, shards, 1 - core)
    meet_twin()

    def send(tile, carry):
        columns = column_tile(tile)
        send_buf[:, columns] = product(half[...], gradient[:, columns]).astype(jnp.bfloat16)
        sums.copy(tile).start()
        return carry

    lax.fori_loop(0, tiles, send, 0)
    half[...] = shard_rows(across, shards, core)

    def keep(tile, carry):
        columns = column_tile(tile)
        value = product(half[...], gradient[:, columns])
        sums.copy(tile).wait()
        out[:, columns] = (value + recv_buf[:, columns].astype(jnp.float32)).astype(jnp.bfloat16)
        return carry

    lax.fori_loop(0, tiles, keep, 0)


def core_grads(shards, ident, source, gradient):
    depth, length = source.shape
    width = gradient.shape[1]
    tiles = width // GRAD_TILE
    return call_plane(
        functools.partial(core_grads_body, shards),
        ident,
        shape((depth // 2, width)),
        VMEM,
        [VMEM] * 2,
        [
            pltpu.VMEM((depth // 2, length), jnp.bfloat16),
            pltpu.VMEM((depth // 2, width), jnp.bfloat16),
            pltpu.VMEM((depth // 2, width), jnp.bfloat16),
            pltpu.SemaphoreType.DMA((tiles,)),
            pltpu.SemaphoreType.DMA((tiles,)),
        ],
        2 * length * depth * width,
        VMEM_MEGABYTES,
        (source, gradient),
    )


def hidden_grads_body(
    count, shards, across, grad_rows, gate_up, hidden, down_weight, gate_out, up_out, output,
    gradient_out, half, gradient, rows_buf, gate_up_buf, send_buf, recv_buf, send_sem, recv_sem,
    half_sem, block_sem, store_sem, *refs
):
    core = lax.rem(lax.axis_index("fsdp"), 2)
    scatter = Scatter(count, hidden, down_weight, False, refs)
    width = gate_out.shape[1]
    step = rows_buf.shape[1]
    blocks = gradient.shape[0] // step
    block_loads = {}
    stores = []

    def load_block(index):
        rows = pl.ds(index * step, step)
        pairs = ((grad_rows, rows_buf), (gate_up, gate_up_buf))
        block_loads[index] = [
            begin(source.at[rows], target.at[index % 2], block_sem.at[which, index])
            for which, (source, target) in enumerate(pairs)
        ]

    load_block(0)
    load_block(1)
    span = half.shape[1] // (shards // 2)
    half_loads = []
    for which in range(2):
        owner = (1 - core, core)[which]
        for chip in range(shards // 2):
            start = pl.multiple_of((2 * chip + owner) * span, 16)
            target = half.at[which, pl.ds(chip * span, span)]
            sem = half_sem.at[which, chip]
            half_loads.append(begin(across.at[pl.ds(start, span)], target, sem))
    meet(count, shards)
    sums = CoreSum(send_buf, recv_buf, send_sem, recv_sem)
    tiles = gradient.shape[1] // GRAD_TILE

    def back(index):
        for load in block_loads[index]:
            load.wait()
        rows = pl.ds(index * step, step)
        grad_hidden = times_transposed(rows_buf[index % 2], scatter.right_buf[...])
        gate = gate_up_buf[index % 2, :, :width]
        upward = gate_up_buf[index % 2, :, width:]
        sigmoid_gate = jax.nn.sigmoid(gate)
        silu_gate = gate * sigmoid_gate
        grad_gate = grad_hidden * upward * sigmoid_gate * (1.0 + gate * (1.0 - sigmoid_gate))
        gradient[rows, :width] = grad_gate.astype(jnp.bfloat16)
        gradient[rows, width:] = (grad_hidden * silu_gate).astype(jnp.bfloat16)
        stores.append(begin(gradient.at[rows], gradient_out.at[rows], store_sem.at[index]))
        if index + 2 < blocks:
            load_block(index + 2)

    def send(tile, carry):
        columns = column_tile(tile)
        value = product(half[0], gradient[:, columns])
        send_buf[:, columns] = value.astype(jnp.bfloat16)
        sums.copy(tile).start()
        return carry

    def keep(tile, carry):
        columns = column_tile(tile)
        value = product(half[1], gradient[:, columns])
        sums.copy(tile).wait()
        value = (value + recv_buf[:, columns].astype(jnp.float32)).astype(jnp.bfloat16)
        send_buf[:, columns] = value
        return carry

    def last_back():
        back(blocks - 1)
        for load in half_loads:
            load.wait()

    others = [functools.partial(back, index) for index in range(blocks - 1)] + [last_back]
    bounds = [0, 3, 6, 9, tiles]
    for body in (send, keep):
        for first, last in zip(bounds, bounds[1:]):
            others.append(lambda body=body, a=first, b=last: lax.fori_loop(a, b, body, 0))
    scatter.run(others)
    for index, out in enumerate((gate_out, up_out)):
        source = send_buf.at[:, pl.ds(index * width, width)]
        stores.append(begin(source, out, store_sem.at[blocks + index]))
    scatter.finish()

    def strip(where):
        output[where, :] = received(count, scatter.recv_buf, scatter.total, where)

    for_strips(0, output.shape[0], strip)
    for store in stores:
        store.wait()


def hidden_grads(count, shards, ident, across, grad_rows, gate_up, hidden, down_weight):
    depth, length = across.shape
    width = gate_up.shape[1]
    tiles = width // GRAD_TILE
    rows = length // count
    step = QUERY_ROWS
    half = shape((depth // 2, width // 2))
    return call_plane(
        functools.partial(hidden_grads_body, count, shards),
        ident,
        (half, half, shape((rows, depth), jnp.float32), shape((length, width))),
        (HBM, HBM, VMEM, HBM),
        [HBM] * 5,
        [
            pltpu.VMEM((2, depth // 2, length), jnp.bfloat16),
            pltpu.VMEM((length, width), jnp.bfloat16),
            pltpu.VMEM((2, step, depth), jnp.bfloat16),
            pltpu.VMEM((2, step, width), jnp.float32),
            pltpu.VMEM((depth // 2, width), jnp.bfloat16),
            pltpu.VMEM((depth // 2, width), jnp.bfloat16),
            pltpu.SemaphoreType.DMA((tiles,)),
            pltpu.SemaphoreType.DMA((tiles,)),
            pltpu.SemaphoreType.DMA((2, shards // 2)),
            pltpu.SemaphoreType.DMA((2, length // step)),
            pltpu.SemaphoreType.DMA((length // step + 2,)),
        ]
        + scatter_scratch(count, rows, depth, hidden, down_weight, False, hidden.shape[1]),
        8 * 10**10,
        VMEM_MEGABYTES,
        (across, grad_rows, gate_up, hidden, down_weight),
    )


def attention_grads_body(
    shards, across, gradient, heads, branch_all, *refs
):
    near, out, far, refs = (refs[:4], refs[4], refs[5:9], refs[9:])
    half, outs, send_buf, recv_buf, send_sem, recv_sem, far_send, far_recv = refs
    core = lax.rem(lax.axis_index("fsdp"), 2)
    width = gradient.shape[1]
    tiles = width // GRAD_TILE
    total = out.shape[1] // GRAD_TILE
    part = out.shape[1] - width
    span = out.shape[0] // (shards // 2)
    height = HEAD_DIM
    sums = CoreSum(send_buf, recv_buf, send_sem, recv_sem)
    meet_twin(True)
    copies = []
    _, to_across, to_along, _ = plane_places()
    for index, target in enumerate(far):
        source = near[index]
        rows = source.shape[0] // 2
        half_rows = pl.ds(rows * (index % 2), rows)
        peer = (to_along, to_across)[index % 2]
        copies.append(
            remote(source.at[half_rows], target, far_send.at[index], far_recv.at[index], ctx=peer)
        )

    def heads_product(index, carry):
        columns = pl.ds(pl.multiple_of(index * 512, 512), 512)
        outs[:, columns] = product(heads[...], branch_all[:, columns])
        return carry

    lax.fori_loop(0, branch_all.shape[1] // 512, heads_product, 0)

    def pieces(side):
        for chip in range(shards // 2):
            rows = pl.ds(pl.multiple_of((2 * chip + side) * height, height), height)
            for index in range(span // height):
                start = chip * span + index * height
                yield slice(start, start + height), outs[rows, index * part : (index + 1) * part]

    for rows, value in pieces(1 - core):
        send_buf[rows, width:] = value.astype(jnp.bfloat16)
    for tile in range(tiles, total):
        sums.copy(tile).start()
    half[...] = shard_rows(across, shards, 1 - core)

    def send(tile, carry):
        columns = column_tile(tile)
        send_buf[:, columns] = product(half[...], gradient[:, columns]).astype(jnp.bfloat16)
        sums.copy(tile).start()
        return carry

    lax.fori_loop(0, tiles, send, 0)
    half[...] = shard_rows(across, shards, core)

    def keep(tile, carry):
        columns = column_tile(tile)
        value = product(half[...], gradient[:, columns])
        sums.copy(tile).wait()
        out[:, columns] = (value + recv_buf[:, columns].astype(jnp.float32)).astype(jnp.bfloat16)
        return carry

    lax.fori_loop(0, tiles, keep, 0)
    for tile in range(tiles, total):
        sums.copy(tile).wait()
    for rows, value in pieces(core):
        value = value + recv_buf[rows, width:].astype(jnp.float32)
        out[rows, width:] = value.astype(jnp.bfloat16)
    for copy in copies:
        copy.wait()


def attention_grads(shards, ident, first_across, grad_packed, heads_across, branch_all, *near):
    depth, length = first_across.shape
    heads = heads_across.shape[0]
    width = grad_packed.shape[1] + heads
    tiles = width // GRAD_TILE
    return call_plane(
        functools.partial(attention_grads_body, shards),
        ident,
        (shape((depth // 2, width)), *[shape((n.shape[0] // 2, n.shape[1])) for n in near]),
        (VMEM,) + (HBM,) * 4,
        [VMEM] * 4 + [HBM] * 4,
        [
            pltpu.VMEM((depth // 2, length), jnp.bfloat16),
            pltpu.VMEM((heads, branch_all.shape[1]), jnp.float32),
            pltpu.VMEM((depth // 2, width), jnp.bfloat16),
            pltpu.VMEM((depth // 2, width), jnp.bfloat16),
            pltpu.SemaphoreType.DMA((tiles,)),
            pltpu.SemaphoreType.DMA((tiles,)),
            pltpu.SemaphoreType.DMA((4,)),
            pltpu.SemaphoreType.DMA((4,)),
        ],
        2 * length * depth * width,
        VMEM_MEGABYTES,
        (first_across, grad_packed, heads_across, branch_all, *near),
    )


def sort_parts(parts, sorted_parts, corner_low):
    me, across, along, corner = plane_places()
    own, from_across, from_along, low, high = parts
    sorted_parts[me] = own[...]
    sorted_parts[across] = from_across[...]
    sorted_parts[along] = from_along[...]

    @pl.when(corner_low)
    def _():
        sorted_parts[corner] = low[...]

    @pl.when(jnp.logical_not(corner_low))
    def _():
        sorted_parts[corner] = high[...]


def interleaved(values, shards):
    span = values[0].shape[1] // shards
    return jnp.concatenate(
        [v[:, shard * span : (shard + 1) * span] for shard in range(shards) for v in values], axis=1
    )


def place_sorted_body(shards, *refs):
    *parts, target = refs
    target[...] = interleaved([part[...].astype(jnp.float32) for part in parts], shards)


def place_sorted(shards, array):
    rows, width = (array.shape[0] // 4, array.shape[1])
    step = 64
    steps = rows // step
    return pl.pallas_call(
        functools.partial(place_sorted_body, shards),
        grid=(steps,),
        out_shape=shape((rows, 4 * width), jnp.float32),
        in_specs=[
            pl.BlockSpec((step, width), lambda i, part=part: (part * steps + i, 0))
            for part in range(4)
        ],
        out_specs=pl.BlockSpec((step, 4 * width), lambda i: (i, 0)),
        cost_estimate=pl.CostEstimate(flops=0, bytes_accessed=10**7, transcendentals=0),
        compiler_params=pltpu.CompilerParams(vmem_limit_bytes=24 << 20),
    )(array, array, array, array)


def place_hidden_body(shards, *refs):
    parts, (target, sorted_parts) = (refs[:5], refs[5:])
    steps = pl.num_programs(0)
    sort_parts(parts, sorted_parts, pl.program_id(0) < steps // 2)
    values = [sorted_parts[part].astype(jnp.float32) for part in range(sorted_parts.shape[0])]
    target[...] = interleaved(values, shards)


def place_hidden(shards, parts):
    rows, width = parts[0].shape
    step = 64
    half = rows // step // 2
    whole = pl.BlockSpec((step, width), lambda i: (i, 0))
    low = pl.BlockSpec((step, width), lambda i: (jnp.minimum(i, half - 1), 0))
    high = pl.BlockSpec((step, width), lambda i: (jnp.maximum(i - half, 0), 0))
    return pl.pallas_call(
        functools.partial(place_hidden_body, shards),
        grid=(rows // step,),
        out_shape=shape((rows, 4 * width), jnp.float32),
        in_specs=[whole, whole, whole, low, high],
        out_specs=pl.BlockSpec((step, 4 * width), lambda i: (i, 0)),
        scratch_shapes=[pltpu.VMEM((4, step, width), jnp.bfloat16)],
        cost_estimate=pl.CostEstimate(flops=0, bytes_accessed=10**7, transcendentals=0),
        compiler_params=pltpu.CompilerParams(vmem_limit_bytes=24 << 20),
    )(*parts)


def place_rows_body(own, from_across, from_along, low, high, out):
    me, across, along, corner = plane_places()
    rows = own.shape[0]

    def put(owner, offset, ref):
        size = ref.shape[0]
        start = pl.multiple_of(owner * rows + offset, 8)
        out[pl.ds(start, size), :] = ref[...].astype(out.dtype)

    put(me, 0, own)
    put(across, 0, from_across)
    put(along, 0, from_along)
    put(corner, 0, low)
    put(corner, rows // 2, high)


def place_rows(parts, kind):
    rows, width = parts[0].shape
    return pl.pallas_call(
        place_rows_body,
        out_shape=shape((4 * rows, width), kind),
        in_specs=[VMEM] * 5,
        out_specs=VMEM,
        cost_estimate=pl.CostEstimate(flops=0, bytes_accessed=10**7, transcendentals=0),
        compiler_params=pltpu.CompilerParams(vmem_limit_bytes=24 << 20),
    )(*parts)


def place_attention_body(shards, own, from_across, from_along, low, high, query, key, value, output, sorted_parts):
    me, across, along, corner = plane_places()
    rows = own.shape[0]
    sorted_parts[me] = own[...]
    sorted_parts[across] = from_across[...]
    sorted_parts[along] = from_along[...]
    sorted_parts[corner, : rows // 2] = low[...]
    sorted_parts[corner, rows // 2 :] = high[...]
    count = sorted_parts.shape[0]
    width = query.shape[1] // count
    span = width // shards
    values = [sorted_parts[part, :, :width].astype(jnp.float32) for part in range(count)]
    query[...] = jnp.concatenate(
        [
            values[part][:, shard * span : (shard + 1) * span]
            for shard in range(shards)
            for part in range(count)
        ],
        axis=1,
    )
    sums = None
    for part in range(count):
        term = sorted_parts[part, :, width : width + 2 * KV_WIDTH].astype(jnp.float32)
        sums = term if sums is None else sums + term
    key[...] = sums[:, :KV_WIDTH]
    value[...] = sums[:, KV_WIDTH:]
    height = rows // count
    for part in range(count):
        for index in range(count):
            tile = sorted_parts[part, index * height : (index + 1) * height, width + 2 * KV_WIDTH :]
            output[part * height : (part + 1) * height, index * width : (index + 1) * width] = (
                tile.astype(jnp.float32)
            )


def place_attention(shards, parts):
    rows, width = parts[0].shape
    wide = shape((rows, D), jnp.float32)
    narrow = shape((rows, KV_WIDTH), jnp.float32)
    return pl.pallas_call(
        functools.partial(place_attention_body, shards),
        out_shape=(wide, narrow, narrow, wide),
        in_specs=[VMEM] * 5,
        out_specs=(VMEM,) * 4,
        scratch_shapes=[pltpu.VMEM((4, rows, width), jnp.bfloat16)],
        cost_estimate=pl.CostEstimate(flops=0, bytes_accessed=10**7, transcendentals=0),
        compiler_params=pltpu.CompilerParams(vmem_limit_bytes=24 << 20),
    )(*parts)


def low_lanes(dims, size):
    return lax.rem(lax.broadcasted_iota(jnp.int32, dims, len(dims) - 1), 2 * size) < size


def turn(values, cosine, sine):
    half = HEAD_DIM // 2
    swapped = jnp.where(
        low_lanes(values.shape, half),
        pltpu.roll(values, LANES - half, 1),
        pltpu.roll(values, half, 1),
    )
    return values * cosine + swapped * sine


def two_heads(values):
    low = low_lanes(values.shape, HEAD_DIM)
    zero = jnp.zeros_like(values)
    return jnp.concatenate([jnp.where(low, values, zero), jnp.where(low, zero, values)], axis=0)


def pick_heads(values):
    rows = values.shape[1] // PAIR
    return jnp.concatenate(
        [values[:HEAD_DIM, :rows], values[HEAD_DIM:, rows:]], axis=0
    )


def later_key(dims):
    key = lax.broadcasted_iota(jnp.int32, dims, 0)
    query = lax.rem(lax.broadcasted_iota(jnp.int32, dims, 1), QUERY_ROWS)
    return key > query


def block_rows_at(order, block, rows):
    return pl.ds(pl.multiple_of(order[block] * rows, rows), rows)


def rows_in_order(order, source, index, rows):
    per = QUERY_ROWS // rows
    return jnp.concatenate(
        [source[block_rows_at(order, index * per + i, rows), :] for i in range(per)], axis=0
    )


def slots(dealing, order):
    for slot in range(dealing.shape[1]):
        order[dealing[0, slot]] = slot


def unpack_output(weight, output_part):
    width = output_part.shape[0]
    if weight.shape[1] <= width + 2 * KV_WIDTH:
        return
    parts = output_part.shape[1] // width
    shards = width // HEAD_DIM
    for shard in range(shards):
        for part in range(parts):
            start = (shard * parts + part) * HEAD_DIM
            output_part[
                shard * HEAD_DIM : (shard + 1) * HEAD_DIM, part * width : (part + 1) * width
            ] = weight[start : start + HEAD_DIM, weight.shape[1] - width :]


def attend_body(
    block_rows,
    dealing,
    tokens_all,
    gain,
    weight,
    cosine,
    sine,
    attended,
    queries,
    keys,
    values,
    log_totals,
    first_across,
    heads_across,
    output_part,
    values_across,
    order,
):
    slots(dealing, order)
    unpack_output(weight, output_part)
    length, width = queries.shape
    kv_heads = keys.shape[0]
    pairs = width // LANES
    blocks = length // QUERY_ROWS

    def project(index, carry):
        place = pl.ds(pl.multiple_of(index * QUERY_ROWS, QUERY_ROWS), QUERY_ROWS)
        normed, _ = norm_parts(
            rows_in_order(order, tokens_all, index, block_rows).astype(jnp.float32)
        )
        rows = (normed * gain[...]).astype(jnp.bfloat16)
        turned_rows = rows.T
        for i in range(QUERY_ROWS // block_rows):
            first_across[
                :, block_rows_at(order, index * (QUERY_ROWS // block_rows) + i, block_rows)
            ] = turned_rows[:, i * block_rows : (i + 1) * block_rows]
        cos_rows, sin_rows = (cosine[place, :], sine[place, :])
        projected = product(rows, weight[:, :width])
        for pair in range(pairs):
            lanes = slice(pair * LANES, (pair + 1) * LANES)
            turned = turn(projected[:, lanes], cos_rows, sin_rows).astype(jnp.bfloat16)
            queries[place, lanes] = turned * jnp.asarray(1.0 / math.sqrt(HEAD_DIM), jnp.bfloat16)
        projected = product(rows, weight[:, width : width + 2 * kv_heads * HEAD_DIM])
        for head in range(2 * kv_heads):
            tile = projected[:, head // PAIR * LANES : (head // PAIR + 1) * LANES]
            if head < kv_heads:
                tile = turn(tile, cos_rows, sin_rows)
            low = low_lanes(tile.shape, HEAD_DIM)
            moved = pltpu.roll(tile, HEAD_DIM, 1)
            both = jnp.where(low, tile, moved) if head % PAIR == 0 else jnp.where(low, moved, tile)
            if head < kv_heads:
                keys[head, place, :] = both.astype(jnp.bfloat16)
            else:
                values[head - kv_heads, place, :] = both.astype(jnp.bfloat16)
                values_across[head - kv_heads, :, place] = both.T.astype(jnp.bfloat16)
        return carry

    lax.fori_loop(0, blocks, project, 0)

    def attend(pair, carry):
        kv_head = pair // (pairs // kv_heads)
        lanes = pl.ds(pl.multiple_of(pair * LANES, LANES), LANES)
        for index in range(blocks):
            seen = (index + 1) * QUERY_ROWS
            rows = two_heads(queries[index * QUERY_ROWS : seen, lanes])
            scores = times_transposed(keys[kv_head, :seen, :], rows)
            own = scores[seen - QUERY_ROWS :]
            own = jnp.where(later_key(own.shape), -1e30, own)
            if index:
                scores = jnp.concatenate([scores[: seen - QUERY_ROWS], own], axis=0)
            else:
                scores = own
            largest = jnp.max(scores, axis=0, keepdims=True)
            exponent = jnp.exp(scores - largest)
            totals = jnp.sum(exponent, axis=0, keepdims=True)
            mixed = product(values_across[kv_head, :, :seen], exponent.astype(jnp.bfloat16))
            log_totals[pl.ds(pair * blocks + index, 1), :] = largest + jnp.log(totals)
            across = pick_heads(mixed / totals).astype(jnp.bfloat16)
            for i in range(QUERY_ROWS // block_rows):
                heads_across[
                    lanes, block_rows_at(order, index * (QUERY_ROWS // block_rows) + i, block_rows)
                ] = across[:, i * block_rows : (i + 1) * block_rows]
            mixed = across.T
            per = QUERY_ROWS // block_rows
            for i in range(per):
                attended[block_rows_at(order, index * per + i, block_rows), lanes] = mixed[
                    i * block_rows : (i + 1) * block_rows
                ]
        return carry

    lax.fori_loop(0, pairs, attend, 0)


def attend_forward(block_rows, width, kv_heads, dealing, tokens_all, gain, weight, tables):
    length, _ = tokens_all.shape
    blocks = length // QUERY_ROWS
    wide = shape((kv_heads, length, LANES))
    return pl.pallas_call(
        functools.partial(attend_body, block_rows),
        out_shape=(
            shape((length, width)),
            shape((length, width)),
            wide,
            wide,
            shape((width // LANES * blocks, PAIR * QUERY_ROWS), jnp.float32),
            shape(tokens_all.shape[::-1]),
            shape((width, length)),
            shape((width, tokens_all.shape[1])),
        ),
        in_specs=[SMEM] + [VMEM] * 5,
        out_specs=(VMEM,) * 8,
        scratch_shapes=[
            pltpu.VMEM((kv_heads, LANES, length), jnp.bfloat16),
            pltpu.SMEM((length // block_rows,), jnp.int32),
        ],
        compiler_params=pltpu.CompilerParams(vmem_limit_bytes=VMEM_MEGABYTES << 20),
        cost_estimate=pl.CostEstimate(
            flops=3 * 10**10, bytes_accessed=10**7, transcendentals=10**7
        ),
    )(dealing, tokens_all, gain, weight, *tables)


def attend_back_body(
    block_rows,
    dealing,
    branch_all,
    output_weight,
    queries,
    keys,
    values,
    attended,
    log_totals,
    cosine,
    sine,
    grad_packed,
    grads,
    row_dots,
    keys_across,
    key_sums,
    value_sums,
    order,
):
    slots(dealing, order)
    length, width = queries.shape
    kv_heads = keys.shape[0]
    pairs = width // LANES
    blocks = length // QUERY_ROWS
    per = QUERY_ROWS // block_rows

    def project(index, carry):
        place = pl.ds(pl.multiple_of(index * QUERY_ROWS, QUERY_ROWS), QUERY_ROWS)
        rows = rows_in_order(order, branch_all, index, block_rows)
        low = times_transposed(rows, output_weight[...]).astype(jnp.bfloat16)
        grads[place, :] = low
        dots = low.astype(jnp.float32) * rows_in_order(order, attended, index, block_rows).astype(
            jnp.float32
        )
        for pair in range(pairs):
            across = dots[:, pair * LANES : (pair + 1) * LANES].T
            sums = [
                jnp.sum(across[i * HEAD_DIM : (i + 1) * HEAD_DIM], axis=0, keepdims=True)
                for i in range(PAIR)
            ]
            row_dots[pl.ds(pair * blocks + index, 1), :] = jnp.concatenate(sums, axis=1)
        for head in range(kv_heads):
            keys_across[head, :, place] = keys[head, place, :].T
        return carry

    lax.fori_loop(0, blocks, project, 0)

    group = pairs // kv_heads

    def attend(kv_head, carry):
        key_sums[kv_head] = jnp.zeros(key_sums.shape[1:], jnp.float32)
        value_sums[kv_head] = jnp.zeros(value_sums.shape[1:], jnp.float32)
        for member in range(group):
            pair = kv_head * group + member
            lanes = pl.ds(pl.multiple_of(pair * LANES, LANES), LANES)
            for index in range(blocks):
                seen = (index + 1) * QUERY_ROWS
                place = slice(index * QUERY_ROWS, seen)
                rows = two_heads(queries[place, lanes])
                grad_rows = two_heads(grads[place, lanes])
                row = pl.ds(pair * blocks + index, 1)
                scores = times_transposed(keys[kv_head, :seen, :], rows)
                weights = jnp.exp(scores - log_totals[row, :])
                own = weights[seen - QUERY_ROWS :]
                own = jnp.where(later_key(own.shape), 0.0, own)
                if index:
                    weights = jnp.concatenate([weights[: seen - QUERY_ROWS], own], axis=0)
                else:
                    weights = own
                grad_probs = times_transposed(values[kv_head, :seen, :], grad_rows)
                grad_scores = (weights * (grad_probs - row_dots[row, :])).astype(jnp.bfloat16)
                value_sums[kv_head, :seen, :] += product(weights.astype(jnp.bfloat16), grad_rows)
                key_sums[kv_head, :seen, :] += product(grad_scores, rows)
                turned = product(keys_across[kv_head, :, :seen], grad_scores)
                turned = pick_heads(turned).T * (1.0 / math.sqrt(HEAD_DIM))
                turned = turn(turned, cosine[place, :], -sine[place, :]).astype(jnp.bfloat16)
                for i in range(per):
                    grad_packed[block_rows_at(order, index * per + i, block_rows), lanes] = turned[
                        i * block_rows : (i + 1) * block_rows
                    ]
        return carry

    lax.fori_loop(0, kv_heads, attend, 0)

    def finish(block, carry):
        place = pl.ds(pl.multiple_of(block * block_rows, block_rows), block_rows)
        target = block_rows_at(order, block, block_rows)

        def head_sum(head):
            if head < kv_heads:
                tile = key_sums[head, place, :]
            else:
                tile = value_sums[head - kv_heads, place, :]
            tile = tile + pltpu.roll(tile, HEAD_DIM, 1)
            if head < kv_heads:
                tile = turn(tile, cosine[place, :], -sine[place, :])
            return tile

        for tile in range(2 * kv_heads // PAIR):
            first, second = (head_sum(tile * PAIR), head_sum(tile * PAIR + 1))
            joined = jnp.where(low_lanes(first.shape, HEAD_DIM), first, second)
            start = width + tile * LANES
            grad_packed[target, start : start + LANES] = joined.astype(jnp.bfloat16)
        return carry

    lax.fori_loop(0, length // block_rows, finish, 0)


def attend_backward(
    block_rows, dealing, branch_all, output_weight, queries, keys, values, attended, log_totals, tables
):
    length, width = queries.shape
    kv_heads = keys.shape[0]
    return pl.pallas_call(
        functools.partial(attend_back_body, block_rows),
        out_shape=shape((length, width + 2 * kv_heads * HEAD_DIM)),
        in_specs=[SMEM] + [VMEM] * 9,
        out_specs=VMEM,
        scratch_shapes=[
            pltpu.VMEM((length, width), jnp.bfloat16),
            pltpu.VMEM(log_totals.shape, jnp.float32),
            pltpu.VMEM((kv_heads, LANES, length), jnp.bfloat16),
            pltpu.VMEM((kv_heads, length, LANES), jnp.float32),
            pltpu.VMEM((kv_heads, length, LANES), jnp.float32),
            pltpu.SMEM((length // block_rows,), jnp.int32),
        ],
        compiler_params=pltpu.CompilerParams(vmem_limit_bytes=VMEM_MEGABYTES << 20),
        cost_estimate=pl.CostEstimate(
            flops=6 * 10**10, bytes_accessed=10**7, transcendentals=10**7
        ),
    )(
        dealing,
        branch_all,
        output_weight,
        queries,
        keys,
        values,
        attended,
        log_totals,
        *tables,
    )


def take_columns(matrix, outer, parts, index):
    rows, columns = matrix.shape
    pieces = matrix.reshape(rows, outer, parts, columns // (outer * parts))
    return lax.dynamic_index_in_dim(pieces, index, axis=2, keepdims=False).reshape(rows, -1)


def take_rows(matrix, parts, index):
    count = matrix.shape[0] // parts
    return lax.dynamic_slice_in_dim(matrix, index * count, count, axis=0)


def put_columns(gathered, outer):
    parts, rows, columns = gathered.shape
    return (
        gathered.reshape(parts, rows, outer, columns // outer)
        .transpose(1, 2, 0, 3)
        .reshape(rows, parts * columns)
    )


def gather_shards(array):
    return lax.all_gather(array, "fsdp", axis=0, tiled=True)


def scatter_shards(array, by_core=False):
    shards = lax.axis_size("fsdp")
    groups = [list(range(core, shards, 2)) for core in range(2)] if by_core else None
    return lax.psum_scatter(
        array.astype(jnp.bfloat16),
        "fsdp",
        scatter_dimension=0,
        tiled=True,
        axis_index_groups=groups,
    )


def per_device(
    tokens,
    dealing,
    first_gain,
    query_weight,
    key_weight,
    value_weight,
    output_weight,
    second_gain,
    gate_weight,
    up_weight,
    down_weight,
    cotangent,
):
    shard_count = lax.axis_size("fsdp")
    part_count = lax.axis_size("ctx")
    ctx_index = lax.axis_index("ctx")
    row_count = tokens.shape[1]
    block_rows = row_count // 2
    seq_rows = row_count * part_count
    part_width = D // part_count
    dealt_heads = D // shard_count // part_count == HEAD_DIM and part_count == 4
    kv_heads = KV_HEADS if dealt_heads else max(1, KV_HEADS // part_count)
    kv_first = 0 if dealt_heads else ctx_index * KV_HEADS // part_count
    tie = lax.optimization_barrier
    start = functools.partial(
        start_gather, part_count, shard_count, 1, tokens[0], first_gain[None], second_gain[None]
    )
    if dealt_heads:
        tokens_all, gain_first, gain_second, cosine, sine, packed, packed_hidden = start(
            query_weight, key_weight, value_weight, output_weight, gate_weight, up_weight
        )
        packed, packed_hidden = tie((packed, packed_hidden))
        gate_up_part = gather_shards(packed_hidden)
    else:
        tokens_all, gain_first, gain_second, cosine, sine = start()
        grad_out_all = lax.all_gather(cotangent[0], "ctx", axis=0, tiled=True)
        query_part = gather_shards(take_columns(query_weight, 1, part_count, ctx_index))
        output_part = take_rows(gather_shards(output_weight), part_count, ctx_index)
        key_value = gather_shards(jnp.concatenate([key_weight, value_weight], axis=1))
        key_value = key_value.reshape(D, 2, KV_HEADS, HEAD_DIM)
        key_value = lax.dynamic_slice_in_dim(key_value, kv_first, kv_heads, 2).reshape(D, -1)
        packed = jnp.concatenate([query_part, key_value], axis=1)
        gate_up_part = gather_shards(
            jnp.concatenate(
                [
                    take_columns(gate_weight, shard_count, part_count, ctx_index),
                    take_columns(up_weight, shard_count, part_count, ctx_index),
                ],
                axis=1,
            )
        )
    tables = (cosine, sine)
    down_part = gather_shards(take_rows(down_weight, part_count, ctx_index))

    forward = attend_forward(
        block_rows, part_width, kv_heads, dealing, tokens_all, gain_first, packed, tables
    )
    attended, query_rot, key_rot, value_rows, log_totals, first_across, heads_across = forward[:7]
    if dealt_heads:
        output_part = forward[7]
    residual_mid, second_all = middle_gather(
        part_count, 2, attended, output_part, tokens[0], gain_second
    )
    if dealt_heads:
        second_all, grad_out = tie((second_all, cotangent[0]))
        near = plane_near(grad_out)

    gate_up, hidden, second_across, hidden_across = hidden_forward(second_all, gate_up_part)
    if dealt_heads:
        hidden_across, *near = tie((hidden_across, *near))
        grad_out_all = place_rows(plane_far(near), jnp.bfloat16)
        down_term = core_grads(shard_count, 5, hidden_across, grad_out_all)
    else:
        down_term = column_term(hidden, grad_out_all)
    down_part, down_term = tie((down_part, down_term))
    down_piece = scatter_shards(down_term, dealt_heads)
    if dealt_heads:
        *terms, output_sum, grad_gate_up = hidden_grads(
            part_count, shard_count, 6, second_across, grad_out_all, gate_up, hidden, down_part
        )
    else:
        grad_gate_up = hidden_backward(grad_out_all, down_part, gate_up)
        gate_up_term = column_term(second_all, grad_gate_up).astype(jnp.bfloat16)
        terms = (gate_up_term[:, : FF // part_count], gate_up_term[:, FF // part_count :])
        output_partial = product(hidden, down_part).astype(jnp.bfloat16)
        output_sum = lax.psum_scatter(output_partial, "ctx", scatter_dimension=0, tiled=True)
    block_output = (residual_mid + output_sum.astype(jnp.float32)).astype(jnp.bfloat16)
    grad_gate_up, *terms = tie((grad_gate_up, *terms))
    gate_piece = scatter_shards(terms[0], dealt_heads)
    up_piece = scatter_shards(terms[1], dealt_heads)
    grad_mid, second_gain_part, branch_all = middle_back(
        part_count, 3, grad_gate_up, gate_up_part, residual_mid, gain_second, cotangent[0]
    )
    branch_all, down_piece = tie((branch_all, down_piece))
    branch_all, gate_piece = tie((branch_all, gate_piece))
    if dealt_heads:
        down_near = plane_near(down_piece)
        gate_near = plane_near(gate_piece)

    grad_packed = attend_backward(
        block_rows,
        dealing,
        branch_all,
        output_part,
        query_rot,
        key_rot,
        value_rows,
        attended,
        log_totals,
        tables,
    )
    if dealt_heads:
        packed_term, *far = attention_grads(
            shard_count,
            7,
            first_across,
            grad_packed,
            heads_across,
            branch_all,
            *down_near[1:],
            *gate_near[1:],
        )
        down_parts, gate_parts = ((*down_near, *far[:2]), (*gate_near, *far[2:]))
        grad_packed, packed_term = tie((grad_packed, packed_term))
        packed_piece = scatter_shards(packed_term, True)
    grad_norm, gain_shard, up_all = input_back(
        part_count,
        shard_count,
        4,
        grad_packed,
        packed,
        tokens[0],
        gain_first,
        second_gain_part,
        up_piece,
    )
    if dealt_heads:
        grad_norm, packed_piece = tie((grad_norm, packed_piece))
        packed_near = plane_near(packed_piece)
        gate_shard = place_hidden(shard_count, gate_parts)
        up_shard = place_sorted(shard_count, up_all)
        down_shard = place_rows(down_parts, jnp.float32)
        gate_shard, up_shard, *packed_near = tie((gate_shard, up_shard, *packed_near))
        query_shard, key_shard, value_shard, output_shard = place_attention(
            shard_count, plane_far(packed_near)
        )
    else:

        def gather_columns(piece, outer):
            return put_columns(lax.all_gather(piece, "ctx", axis=0), outer).astype(jnp.float32)

        gate_shard = gather_columns(gate_piece, shard_count)
        up_shard = put_columns(
            up_all.reshape(part_count, -1, FF // part_count), shard_count
        ).astype(jnp.float32)
        down_shard = lax.all_gather(down_piece, "ctx", axis=0, tiled=True).astype(jnp.float32)
        grad_query, grad_key_value = (grad_packed[:, :part_width], grad_packed[:, part_width:])
        query_piece = scatter_shards(product(first_across, grad_query))
        query_shard = gather_columns(query_piece, 1)
        key_value_piece = scatter_shards(product(first_across, grad_key_value))
        output_term = column_term(attended, branch_all)
        spread = jnp.zeros((D, D), jnp.float32)
        spread = lax.dynamic_update_slice_in_dim(
            spread, output_term, ctx_index * output_term.shape[0], 0
        )
        output_shard = lax.psum(scatter_shards(spread), "ctx").astype(jnp.float32)
        wide = jnp.zeros((D // shard_count, 2, KV_HEADS, HEAD_DIM), jnp.bfloat16)
        wide = lax.dynamic_update_slice_in_dim(
            wide, key_value_piece.reshape(-1, 2, kv_heads, HEAD_DIM), kv_first, 2
        )
        key_value_shard = lax.psum(wide.reshape(-1, 2 * KV_WIDTH), "ctx").astype(jnp.float32)
        key_shard, value_shard = (key_value_shard[:, :KV_WIDTH], key_value_shard[:, KV_WIDTH:])
    return (
        block_output[None],
        (grad_mid + grad_norm).astype(jnp.bfloat16)[None],
        gain_shard[0],
        query_shard,
        key_shard,
        value_shard,
        output_shard,
        gain_shard[1],
        gate_shard,
        up_shard,
        down_shard,
    )


def solution(mesh):
    in_specs = (
        P("fsdp", "ctx", None),
        P("fsdp", None),
        P("fsdp"),
        P("fsdp", None),
        P("fsdp", None),
        P("fsdp", None),
        P("fsdp", None),
        P("fsdp"),
        P("fsdp", None),
        P("fsdp", None),
        P("fsdp", None),
        P("fsdp", "ctx", None),
    )
    out_specs = (
        P("fsdp", "ctx", None),
        P("fsdp", "ctx", None),
        P("fsdp"),
        P("fsdp", None),
        P("fsdp", None),
        P("fsdp", None),
        P("fsdp", None),
        P("fsdp"),
        P("fsdp", None),
        P("fsdp", None),
        P("fsdp", None),
    )
    return jax.shard_map(
        per_device, mesh=mesh, in_specs=in_specs, out_specs=out_specs, check_vma=False
    )
```

```python
import functools
import math

import jax
import jax.numpy as jnp
from jax import lax
from jax.experimental import pallas as pl
from jax.experimental.pallas import tpu as pltpu
from jax.sharding import PartitionSpec as P

D = 2048
FF = 5632
HEADS = 32
KV_HEADS = 4
HEAD_DIM = 64
KV_WIDTH = 256


epsilon = 1e-05


MESH = pl.DeviceIdType.MESH
VMEM = pl.BlockSpec(memory_space=pltpu.VMEM)
SMEM = pl.BlockSpec(memory_space=pltpu.SMEM)
HBM = pl.BlockSpec(memory_space=pltpu.HBM)
LANES = 128
PAIR = LANES // HEAD_DIM
QUERY_ROWS = 256
VMEM_MEGABYTES = 60


def shape(dims, kind=jnp.bfloat16):
    return jax.ShapeDtypeStruct(dims, kind)


def norm_parts(values):
    inverse = lax.rsqrt(jnp.mean(values * values, axis=-1, keepdims=True) + epsilon)
    return (values * inverse, inverse)


def norm_back(gradient, normed, inverse):
    return inverse * (gradient - normed * jnp.mean(gradient * normed, axis=-1, keepdims=True))


def product(left_side, right_side):
    return jnp.dot(left_side, right_side, preferred_element_type=jnp.float32)


def times_transposed(left_side, right_side):
    return lax.dot_general(
        left_side, right_side, (((1,), (1,)), ((), ())), preferred_element_type=jnp.float32
    )


def column_term(source, gradient):
    return lax.dot_general(
        source, gradient, (((0,), (0,)), ((), ())), preferred_element_type=jnp.float32
    )


STRIP = 32
PIECES = 8
ORDER = [half * PIECES // 2 + i for i in range(PIECES // 2) for half in range(2)]


def plane_places():
    me = lax.axis_index("ctx")
    return (me, me + 1 - 2 * lax.rem(me, 2), lax.rem(me + 2, 4), 3 - me)


def signal(barrier, **place):
    pl.semaphore_signal(barrier, inc=1, device_id=place, device_id_type=MESH)


def greet(count, shards=1):
    me = lax.axis_index("ctx")
    barrier = pltpu.get_barrier_semaphore()
    for step in range(1, count):
        signal(barrier, ctx=lax.rem(me + step, count))
    for step in range(1, shards):
        signal(barrier, fsdp=lax.rem(lax.axis_index("fsdp") + step, shards))


def met(count, shards=1):
    pl.semaphore_wait(pltpu.get_barrier_semaphore(), count - 1 + shards - 1)


def meet(count, shards=1):
    greet(count, shards)
    met(count, shards)


def remote(source, target, send_sem, recv_sem, **place):
    copy = pltpu.make_async_remote_copy(
        src_ref=source,
        dst_ref=target,
        send_sem=send_sem,
        recv_sem=recv_sem,
        device_id=place,
        device_id_type=MESH,
    )
    copy.start()
    return copy


def gather_sems(count):
    sends = 3 if count == 4 else count - 1
    return [
        pltpu.SemaphoreType.DMA((PIECES,)),
        pltpu.SemaphoreType.DMA((sends, PIECES)),
        pltpu.SemaphoreType.DMA((sends, PIECES)),
    ]


class RowGather:
    def __init__(self, count, own, out, sems):
        self.count, self.own, self.out = (count, own, out)
        self.local_sem, self.send_sem, self.recv_sem = sems
        self.size = own.shape[0] // PIECES
        self.copies = [[] for _ in range(PIECES)]
        self.relays = []

    def place(self, owner, piece):
        start = owner * self.own.shape[0] + piece * self.size
        return self.out.at[pl.ds(pl.multiple_of(start, self.size), self.size)]

    def send(self, piece):
        me = lax.axis_index("ctx")
        source = self.own.at[pl.ds(piece * self.size, self.size)]
        target = self.place(me, piece)
        if self.count == 4:
            _, across, along, _ = plane_places()
            peers = (across, along)
        else:
            peers = [lax.rem(me + step, self.count) for step in range(1, self.count)]
        for index, peer in enumerate(peers):
            self.copies[piece].append(
                remote(
                    source,
                    target,
                    self.send_sem.at[index, piece],
                    self.recv_sem.at[index, piece],
                    ctx=peer,
                )
            )
        local = pltpu.make_async_copy(source, target, self.local_sem.at[piece])
        local.start()
        self.copies[piece].append(local)

    def finish(self):
        self.relay()
        self.drain()

    def relay(self, pieces=tuple(ORDER)):
        relays = self.relays
        if self.count != 4:
            return
        _, across, along, _ = plane_places()
        for piece in pieces:
            first = piece < PIECES // 2
            came, left = (0, 1) if first else (1, 0)
            owner, peer = (across, along) if first else (along, across)
            self.copies[piece][came].wait_recv()
            block = self.place(owner, piece)
            relays.append(
                remote(
                    block, block, self.send_sem.at[2, piece], self.recv_sem.at[2, piece], ctx=peer
                )
            )

    def drain(self):
        if self.count != 4:
            for copies in self.copies:
                for copy in copies:
                    copy.wait()
            return
        for piece in range(PIECES):
            to_across, to_along, local = self.copies[piece]
            (to_along if piece < PIECES // 2 else to_across).wait_recv()
            to_across.wait_send()
            to_along.wait_send()
            local.wait()
        for relay in self.relays:
            relay.wait()


CHUNKS = 2


def line_sems(shards):
    hops = shards // 2 - 1
    return [
        pltpu.SemaphoreType.DMA,
        pltpu.SemaphoreType.DMA((2 * hops, CHUNKS)),
        pltpu.SemaphoreType.DMA((2 * hops, CHUNKS)),
        pltpu.SemaphoreType.DMA((2 * hops + 1, CHUNKS)),
        pltpu.SemaphoreType.DMA((2 * hops + 1, CHUNKS)),
    ]


class LineGather:
    def __init__(self, shards, own, out, sems):
        self.own, self.out = (own, out)
        self.local_sem, self.send_sem, self.recv_sem, self.core_send, self.core_recv = sems
        self.me = lax.axis_index("fsdp")
        self.hops = shards // 2 - 1
        self.chip = self.me // 2
        self.twin = self.me + 1 - 2 * lax.rem(self.me, 2)
        self.size = own.shape[0] // CHUNKS

    def block(self, owner, chunk):
        start = owner * self.own.shape[0] + chunk * self.size
        return self.out.at[pl.ds(pl.multiple_of(start, self.size), self.size)]

    def copy(self, distance, way, chunk, sems, index, peer):
        owner = self.me - 2 * (1 - 2 * way) * distance
        target = self.block(owner, chunk)
        part = pl.ds(chunk * self.size, self.size)
        send_sem, recv_sem = sems
        return pltpu.make_async_remote_copy(
            src_ref=self.own.at[part] if distance == 0 else target,
            dst_ref=target,
            send_sem=send_sem.at[index, chunk],
            recv_sem=recv_sem.at[index, chunk],
            device_id={"fsdp": peer},
            device_id_type=MESH,
        )

    def hop(self, way, distance, chunk):
        sems = (self.send_sem, self.recv_sem)
        peer = self.me + 2 * (1 - 2 * way)
        return self.copy(distance, way, chunk, sems, way * self.hops + distance, peer)

    def cross(self, way, distance, chunk):
        index = distance if way == 0 else self.hops + distance
        sems = (self.core_send, self.core_recv)
        return self.copy(distance, way, chunk, sems, index, self.twin)

    def can_send(self, way):
        return self.chip < self.hops if way == 0 else self.chip > 0

    def behind(self, way, distance):
        return self.chip >= distance if way == 0 else self.chip + distance <= self.hops

    def local(self):
        rows = self.own.shape[0]
        target = self.out.at[pl.ds(pl.multiple_of(self.me * rows, rows), rows)]
        return pltpu.make_async_copy(self.own, target, self.local_sem)

    def start(self, chunk):
        for way in (0, 1):
            pl.when(self.can_send(way))(lambda way=way: self.hop(way, 0, chunk).start())
        self.cross(0, 0, chunk).start()
        if chunk == 0:
            self.local().start()

    def step(self, distance, chunk):
        for way in (0, 1):

            @pl.when(self.behind(way, distance))
            def _(way=way):
                self.hop(way, distance - 1, chunk).wait_recv()
                if distance < self.hops:
                    pl.when(self.can_send(way))(lambda: self.hop(way, distance, chunk).start())
                self.cross(way, distance, chunk).start()

    def drain(self):
        for chunk in range(CHUNKS):
            for way in (0, 1):
                for distance in range(self.hops):
                    here = jnp.logical_and(self.can_send(way), self.behind(way, distance))
                    pl.when(here)(
                        lambda way=way, d=distance, chunk=chunk: self.hop(way, d, chunk).wait_send()
                    )
                for distance in range(1, self.hops + 1):
                    pl.when(self.behind(way, distance))(
                        lambda way=way, d=distance, chunk=chunk: self.cross(way, d, chunk).wait()
                    )
            self.cross(0, 0, chunk).wait()
        self.local().wait()


TILE = 512


def begin(source, target, sem):
    copy = pltpu.make_async_copy(source, target, sem)
    copy.start()
    return copy


class Scatter:
    def __init__(self, count, left, right, transposed, refs):
        self.count, self.transposed = (count, transposed)
        self.left_buf, self.right_buf, self.load_sem, *refs = refs
        self.send_buf, self.recv_buf, self.kept, self.total, self.send_sem, self.recv_sem = refs
        self.rows, self.width = self.total.shape
        self.tiles = self.width // TILE
        self.loads = {}
        owners = self.owners()
        depth = self.left_buf.shape[1]
        self.load_left(left, owners[0], 0)
        for tile in range(self.tiles):
            columns = pl.ds(tile * TILE, TILE)
            if transposed:
                place = (columns, pl.ds(0, depth))
                source, target = (right.at[place], self.right_buf.at[columns])
            else:
                source, target = (right.at[:, columns], self.right_buf.at[:, columns])
            self.loads["tile", tile] = begin(source, target, self.load_sem.at[count + tile])
        for index in range(1, count):
            self.load_left(left, owners[index], index)

    def owners(self):
        me = lax.axis_index("ctx")
        if self.count != 4:
            return [lax.rem(me + step, self.count) for step in range(1, self.count)] + [me]
        _, across, along, corner = plane_places()
        return [corner, across, along, me]

    def block_rows(self, owner):
        return pl.ds(pl.multiple_of(owner * self.rows, self.rows), self.rows)

    def load_left(self, left, owner, index):
        rows = self.block_rows(owner)
        self.loads["left", index] = begin(
            left.at[rows], self.left_buf.at[rows], self.load_sem.at[index]
        )

    def tile(self, owner, columns):
        piece = self.left_buf[self.block_rows(owner), :]
        if self.transposed:
            return times_transposed(piece, self.right_buf[columns, :])
        return product(piece, self.right_buf[:, columns])

    def block(self, index, store):
        owner = self.owners()[index]
        self.loads["left", index].wait()

        def column(tile, carry):
            columns = pl.ds(pl.multiple_of(tile * TILE, TILE), TILE)
            store(columns, self.tile(owner, columns))
            return carry

        lax.fori_loop(0, self.tiles, column, 0)

    def send(self, slot, part, columns, sem, peer):
        return remote(
            self.send_buf.at[slot, part, columns],
            self.recv_buf.at[slot, part, columns],
            self.send_sem.at[sem],
            self.recv_sem.at[sem],
            ctx=peer,
        )

    def store_own(self, columns, value):
        self.total[:, columns] = value

    def run(self, shards=1, others=()):
        if self.count == 4:
            self.run_relayed(shards, list(others))
        else:
            met(self.count, shards)
            self.run_direct()
            for other in others:
                other()

    def run_direct(self):
        for tile in range(self.tiles):
            self.loads["tile", tile].wait()
        copies = []
        everything = (pl.ds(0, self.rows), pl.ds(0, self.width))
        for index, owner in enumerate(self.owners()[:-1]):

            def store_sent(columns, value, index=index):
                self.send_buf[index, :, columns] = value.astype(self.send_buf.dtype)

            self.block(index, store_sent)
            copies.append(self.send(index, *everything, index, owner))
        self.block(self.count - 1, self.store_own)
        self.relays, self.copies = ([], copies)

    def run_relayed(self, shards, others):
        corner, across, along, me = self.owners()
        send_buf, kept, tiles = (self.send_buf, self.kept, self.tiles)
        half = self.rows // 2
        low, high = (pl.ds(0, half), pl.ds(half, half))
        whole = pl.ds(0, self.width)
        relays = []
        self.loads["left", 0].wait()
        for tile in range(tiles):
            columns = pl.ds(tile * TILE, TILE)
            self.loads["tile", tile].wait()
            send_buf[0, :, columns] = self.tile(corner, columns).astype(send_buf.dtype)
            if tile == 0:
                met(self.count, shards)
            relays.append(
                (
                    self.send(0, low, columns, tile, across),
                    self.send(0, high, columns, tiles + tile, along),
                )
            )

        def store_across(columns, value):
            send_buf[1, low, columns] = value[:half].astype(send_buf.dtype)
            kept[high, columns] = value[half:]

        def store_along(columns, value):
            send_buf[1, high, columns] = value[half:].astype(send_buf.dtype)
            kept[low, columns] = value[:half]

        self.block(1, store_across)
        copies = [self.send(1, low, whole, 4 * tiles, across)]
        self.block(2, store_along)
        copies.append(self.send(1, high, whole, 4 * tiles + 1, along))
        self.block(3, self.store_own)
        for _ in range(len(others) - tiles - 1):
            others.pop(0)()
        for tile in range(tiles):
            columns = pl.ds(tile * TILE, TILE)
            for side, peer in ((0, along), (1, across)):
                if others and side == 0:
                    others.pop(0)()
                relays[tile][side].wait_recv()
                part = (low, high)[side]

                def add(where, columns=columns):
                    value = kept[where, columns] + self.recv_buf[0, where, columns].astype(
                        jnp.float32
                    )
                    send_buf[2, where, columns] = value.astype(send_buf.dtype)

                for_strips(side * half, half, add)
                sem = (2 + side) * tiles + tile
                copies.append(self.send(2, part, columns, sem, peer))
        self.relays, self.copies = (relays, copies)
        for other in others:
            other()

    def finish(self):
        for pair in self.relays:
            for copy in pair:
                copy.wait_send()
        for copy in self.copies:
            copy.wait()


def scatter_scratch(count, rows, width, left, right, transposed, depth):
    slots = 3 if count == 4 else count - 1
    sems = 4 * (width // TILE) + 2 if count == 4 else count - 1
    return [
        pltpu.VMEM(left.shape, jnp.bfloat16),
        pltpu.VMEM((width, depth) if transposed else (depth, width), jnp.bfloat16),
        pltpu.SemaphoreType.DMA((count + width // TILE,)),
        pltpu.VMEM((slots, rows, width), jnp.bfloat16),
        pltpu.VMEM((slots, rows, width), jnp.bfloat16),
        pltpu.VMEM((rows, width) if count == 4 else (8, LANES), jnp.float32),
        pltpu.VMEM((rows, width), jnp.float32),
        pltpu.SemaphoreType.DMA((sems,)),
        pltpu.SemaphoreType.DMA((sems,)),
    ]


SCATTER_REFS = 9


def side_loads(sources, refs):
    *targets, sem = refs
    return [begin(source, target, sem.at[i]) for i, (source, target) in enumerate(zip(sources, targets))]


def side_scratch(*arrays):
    return [pltpu.VMEM(a.shape, a.dtype) for a in arrays] + [
        pltpu.SemaphoreType.DMA((len(arrays),))
    ]


def received(count, recv_buf, total, rows):
    value = total[rows, :]
    for slot in (1, 2) if count == 4 else range(count - 1):
        value = value + recv_buf[slot, rows, :].astype(jnp.float32)
    return value


def for_strips(first, rows, body):
    def strip(index, carry):
        body(pl.ds(pl.multiple_of(first + index * STRIP, STRIP), STRIP))
        return carry

    lax.fori_loop(0, rows // STRIP, strip, 0)


def call_plane(body, ident, outs, out_specs, in_specs, scratch, flops, megabytes, args):
    return pl.pallas_call(
        body,
        out_shape=outs,
        in_specs=in_specs,
        out_specs=out_specs,
        scratch_shapes=scratch,
        compiler_params=pltpu.CompilerParams(
            collective_id=ident, has_side_effects=True, vmem_limit_bytes=megabytes << 20
        ),
        cost_estimate=pl.CostEstimate(
            flops=flops, bytes_accessed=flops // 300, transcendentals=0
        ),
    )(*args)


def for_part(body):
    me = lax.axis_index("ctx")
    for part in range(4):

        @pl.when(me == part)
        def _(part=part):
            body(part)


def strided_columns(values, shards, part):
    span = values.shape[1] // (4 * shards)
    starts = [(shard * 4 + part) * span for shard in range(shards)]
    wide = values.astype(jnp.float32)
    return jnp.concatenate([wide[:, i : i + span] for i in starts], axis=1).astype(values.dtype)


def pack_attention(shards, query, key, value, output, packed):
    def body(part):
        width = query.shape[1] // 4
        rows = output.shape[0] // 4
        packed[:, :width] = strided_columns(query[...], shards, part)
        packed[:, width : width + KV_WIDTH] = key[...]
        packed[:, width + KV_WIDTH : width + 2 * KV_WIDTH] = value[...]
        for index in range(4):
            packed[index * rows : (index + 1) * rows, width + 2 * KV_WIDTH :] = output[
                part * rows : (part + 1) * rows, index * width : (index + 1) * width
            ]

    for_part(body)


def pack_hidden(shards, gate, up, packed):
    def body(part):
        width = packed.shape[1] // 2

        def strip(where):
            packed[where, :width] = strided_columns(gate[where, :], shards, part)
            packed[where, width:] = strided_columns(up[where, :], shards, part)

        for_strips(0, packed.shape[0], strip)

    for_part(body)


def write_tables(cosine, sine):
    half = HEAD_DIM // 2

    def strip(where):
        dims = (STRIP, LANES)
        lane = lax.broadcasted_iota(jnp.int32, dims, 1)
        place = lax.broadcasted_iota(jnp.int32, dims, 0) + where.start
        index = lax.rem(lane, half).astype(jnp.float32)
        frequency = jnp.exp(-math.log(10000.0) * index * (2.0 / HEAD_DIM))
        angles = place.astype(jnp.float32) * frequency
        cosine[where, :] = jnp.cos(angles)
        sine[where, :] = jnp.where(low_lanes(dims, half), -jnp.sin(angles), jnp.sin(angles))

    for_strips(0, cosine.shape[0], strip)


def start_body(count, shards, tokens, first_gain, second_gain, *refs):
    if count == 4:
        weights, refs = (refs[:6], refs[6:])
    tokens_all, gain_first, gain_second, cosine, sine, *refs = refs
    if count == 4:
        weights_all, packed_hidden, *refs = refs
    gains, gains_all, gain_send, gain_recv, *refs = refs
    first = RowGather(count, tokens, tokens_all, refs[:3])
    if count == 4:
        packed, gate, up, load_sem, *line_refs = refs[3:]
        loads = [
            begin(weights[4 + i], target, load_sem.at[i]) for i, target in enumerate((gate, up))
        ]
        line = LineGather(shards, packed, weights_all, line_refs)
        pack_attention(shards, *weights[:4], packed)
    meet(count, shards)
    if count == 4:
        line.start(0)
    early, late = (ORDER[: PIECES // 2], ORDER[PIECES // 2 :])
    for piece in early:
        first.send(piece)
    me = lax.axis_index("fsdp")
    for index, gain in enumerate((first_gain, second_gain)):
        row = gain[...].astype(jnp.float32)[None, :]
        gains[index : index + 1, :] = row.astype(jnp.bfloat16)
    gains_all[me] = gains[...]
    copies = []
    for step in range(1, shards):
        copies.append(
            remote(
                gains,
                gains_all.at[me],
                gain_send.at[step - 1],
                gain_recv.at[step - 1],
                fsdp=lax.rem(me + step, shards),
            )
        )
    if count != 4:
        write_tables(cosine, sine)
        for piece in late:
            first.send(piece)
        first.finish()
    else:
        steps = [(d, c) for d in range(1, line.hops + 1) for c in range(CHUNKS)]
        write_tables(cosine, sine)
        for chunk in range(1, CHUNKS):
            line.start(chunk)
        line.step(*steps[0])
        first.relay(early)
        for piece in late:
            first.send(piece)
        for step in steps[1:3]:
            line.step(*step)
        for load in loads:
            load.wait()
        pack_hidden(shards, gate, up, packed_hidden)
        first.relay(late)
        for step in steps[3:-1]:
            line.step(*step)
        first.drain()
    for copy in copies:
        copy.wait()
    span = gains.shape[1]
    for shard in range(shards):
        lanes = slice(shard * span, (shard + 1) * span)
        gain_first[:, lanes] = gains_all[shard, 0:1, :].astype(jnp.float32)
        gain_second[:, lanes] = gains_all[shard, 1:2, :].astype(jnp.float32)
    if count == 4:
        line.step(*steps[-1])
        line.drain()


def start_gather(count, shards, ident, tokens, first_gain, second_gain, *weights):
    rows, width = tokens.shape
    span = first_gain.shape[0]
    wide = shape((1, width), jnp.float32)
    table = shape((count * rows, LANES), jnp.float32)
    outs = [shape((count * rows, width)), wide, wide, table, table]
    out_specs = [HBM] + [VMEM] * 4
    in_specs = [HBM, VMEM, VMEM]
    scratch = [
        pltpu.VMEM((2, span), jnp.bfloat16),
        pltpu.VMEM((shards, 2, span), jnp.bfloat16),
        pltpu.SemaphoreType.DMA((shards - 1,)),
        pltpu.SemaphoreType.DMA((shards - 1,)),
    ] + gather_sems(count)
    if weights:
        height = weights[0].shape[0]
        packed = width // 2 + 2 * KV_WIDTH
        outs += [shape((shards * height, packed)), shape((height, FF // 2))]
        out_specs += [HBM, VMEM]
        in_specs += [VMEM] * 4 + [HBM] * 2
        scratch += [
            pltpu.VMEM((height, packed), jnp.bfloat16),
            pltpu.VMEM((height, FF), jnp.bfloat16),
            pltpu.VMEM((height, FF), jnp.bfloat16),
            pltpu.SemaphoreType.DMA((2,)),
        ] + line_sems(shards)
    return call_plane(
        functools.partial(start_body, count, shards),
        ident,
        tuple(outs),
        tuple(out_specs),
        in_specs,
        scratch,
        5 * 10**10,
        VMEM_MEGABYTES,
        (tokens, first_gain, second_gain, *weights),
    )


def strips_and_send(gather, strip):
    size = gather.size
    for piece in ORDER:
        for_strips(piece * size, size, strip)
        gather.send(piece)
    gather.finish()


def middle_body(count, attended, weight, tokens, gain, residual, second_all, own, *refs):
    greet(count)
    scatter = Scatter(count, attended, weight, False, refs[:SCATTER_REFS])
    side = refs[SCATTER_REFS : SCATTER_REFS + 2]
    loads = side_loads([tokens], side)
    scatter.run()
    scatter.finish()
    for load in loads:
        load.wait()

    def strip(where):
        values = side[0][where, :].astype(jnp.float32) + received(
            count, scatter.recv_buf, scatter.total, where
        )
        residual[where, :] = values
        normed, _ = norm_parts(values)
        own[where, :] = (normed * gain[...]).astype(jnp.bfloat16)

    strips_and_send(RowGather(count, own, second_all, refs[SCATTER_REFS + 2 :]), strip)


def middle_gather(count, ident, attended, weight, tokens, gain):
    rows, width = tokens.shape
    return call_plane(
        functools.partial(middle_body, count),
        ident,
        (shape((rows, width), jnp.float32), shape((count * rows, width))),
        (VMEM, HBM),
        [HBM] * 3 + [VMEM],
        [pltpu.VMEM((rows, width), jnp.bfloat16)]
        + scatter_scratch(count, rows, width, attended, weight, False, attended.shape[1])
        + side_scratch(tokens)
        + gather_sems(count),
        6 * 10**10,
        VMEM_MEGABYTES,
        (attended, weight, tokens, gain),
    )


def middle_back_body(
    count, grad_gate_up, gate_up_weight, residual, grad_out, gain, grad_mid, gain_part, branch_all, own,
    *refs
):
    greet(count)
    scatter = Scatter(count, grad_gate_up, gate_up_weight, True, refs[:SCATTER_REFS])
    side = refs[SCATTER_REFS : SCATTER_REFS + 3]
    loads = side_loads([residual, grad_out], side)
    scatter.run()
    scatter.finish()
    gain_part[...] = jnp.zeros_like(gain_part)
    for load in loads:
        load.wait()

    def strip(where):
        gradient = received(count, scatter.recv_buf, scatter.total, where)
        normed, inverse = norm_parts(side[0][where, :])
        gain_part[...] += jnp.sum(gradient * normed, axis=0, keepdims=True)
        values = side[1][where, :].astype(jnp.float32) + norm_back(
            gradient * gain[...], normed, inverse
        )
        grad_mid[where, :] = values
        own[where, :] = values.astype(jnp.bfloat16)

    strips_and_send(RowGather(count, own, branch_all, refs[SCATTER_REFS + 3 :]), strip)


def column_halves(array):
    rows, width = array.shape
    if width // 2 % LANES:
        return ((array[:, : width // 2], array[:, width // 2 :]), (VMEM, VMEM))
    specs = [pl.BlockSpec((rows, width // 2), lambda *index, side=side: (0, side)) for side in (0, 1)]
    return ((array, array), specs)


def middle_back(count, ident, grad_gate_up, gate_up_weight, residual, gain, grad_out):
    rows, width = residual.shape
    return call_plane(
        functools.partial(middle_back_body, count),
        ident,
        (
            shape((rows, width), jnp.float32),
            shape((1, width), jnp.float32),
            shape((count * rows, width)),
        ),
        (VMEM, VMEM, HBM),
        [HBM] * 4 + [VMEM],
        [pltpu.VMEM((rows, width), jnp.bfloat16)]
        + scatter_scratch(
            count, rows, width, grad_gate_up, gate_up_weight, True, grad_gate_up.shape[1]
        )
        + side_scratch(residual, grad_out)
        + gather_sems(count),
        6 * 10**10,
        VMEM_MEGABYTES,
        (grad_gate_up, gate_up_weight, residual, grad_out, gain),
    )


def input_back_body(
    count, shards, grad_packed, weight, tokens, piece, gain, second_part, grad_input, gain_sums,
    piece_all, gain_part, parts, part_recv, sums, sums_recv, part_send_sem, part_recv_sem, sums_send_sem,
    sums_recv_sem, *refs
):
    greet(count, shards)
    scatter = Scatter(count, grad_packed, weight, True, refs[:SCATTER_REFS])
    side = refs[SCATTER_REFS : SCATTER_REFS + 2]
    loads = side_loads([tokens], side)
    gather = RowGather(count, piece, piece_all, refs[SCATTER_REFS + 2 :])
    scatter.run(shards)
    for part in ORDER:
        gather.send(part)
    scatter.finish()
    gain_part[...] = jnp.zeros_like(gain_part)
    for load in loads:
        load.wait()

    def strip(where):
        gradient = received(count, scatter.recv_buf, scatter.total, where)
        normed, inverse = norm_parts(side[0][where, :].astype(jnp.float32))
        gain_part[...] += jnp.sum(gradient * normed, axis=0, keepdims=True)
        grad_input[where, :] = norm_back(gradient * gain[...], normed, inverse)

    for_strips(0, grad_input.shape[0], strip)
    gather.relay()
    me = lax.axis_index("fsdp")
    span = parts.shape[2]
    for shard in range(shards):
        lanes = slice(shard * span, (shard + 1) * span)
        parts[shard, 0:1, :] = gain_part[:, lanes]
        parts[shard, 1:2, :] = second_part[:, lanes]
    copies = []
    for step in range(1, shards):
        peer = lax.rem(me + step, shards)
        copies.append(
            remote(
                parts.at[peer],
                part_recv.at[step - 1],
                part_send_sem.at[step - 1],
                part_recv_sem.at[step - 1],
                fsdp=peer,
            )
        )
    for copy in copies:
        copy.wait()
    value = parts[me]
    for step in range(1, shards):
        value = value + part_recv[step - 1]
    sums[...] = value
    copies = []
    for step in range(1, count):
        copies.append(
            remote(
                sums,
                sums_recv.at[step - 1],
                sums_send_sem.at[step - 1],
                sums_recv_sem.at[step - 1],
                ctx=lax.rem(lax.axis_index("ctx") + step, count),
            )
        )
    for copy in copies:
        copy.wait()
    for step in range(1, count):
        value = value + sums_recv[step - 1]
    gain_sums[...] = value
    gather.drain()


def input_back(
    count, shards, ident, grad_packed, weight, tokens, gain, second_part, piece
):
    rows, width = tokens.shape
    span = width // shards
    return call_plane(
        functools.partial(input_back_body, count, shards),
        ident,
        (
            shape((rows, width), jnp.float32),
            shape((2, span), jnp.float32),
            shape((count * piece.shape[0], piece.shape[1])),
        ),
        (VMEM, VMEM, HBM),
        [HBM] * 4 + [VMEM] * 2,
        [
            pltpu.VMEM((1, width), jnp.float32),
            pltpu.VMEM((shards, 2, span), jnp.float32),
            pltpu.VMEM((shards - 1, 2, span), jnp.float32),
            pltpu.VMEM((2, span), jnp.float32),
            pltpu.VMEM((count - 1, 2, span), jnp.float32),
            pltpu.SemaphoreType.DMA((shards - 1,)),
            pltpu.SemaphoreType.DMA((shards - 1,)),
            pltpu.SemaphoreType.DMA((count - 1,)),
            pltpu.SemaphoreType.DMA((count - 1,)),
        ]
        + scatter_scratch(count, rows, width, grad_packed, weight, True, grad_packed.shape[1])
        + side_scratch(tokens)
        + gather_sems(count),
        5 * 10**10,
        VMEM_MEGABYTES,
        (grad_packed, weight, tokens, piece, gain, second_part),
    )


def swap(array, along):
    pairs = [(i, (i + 2) % 4) if along else (i, i + 1 - 2 * (i % 2)) for i in range(4)]
    return lax.ppermute(array, "ctx", pairs)


def plane_near(array):
    return (array, swap(array, False), swap(array, True))


def plane_far(near):
    _, across, along = near
    half = across.shape[0] // 2
    return (*near, swap(across[:half], True), swap(along[half:], False))


def plane_gather(array):
    return plane_far(plane_near(array))


def hidden_body(rows, gate_weight, up_weight, gate_up, hidden, rows_across, hidden_across):
    width = hidden.shape[1]
    rows_across[...] = rows[...].T
    gate = product(rows[...], gate_weight[...])
    gate_up[:, :width] = gate
    upward = product(rows[...], up_weight[...])
    gate_up[:, width:] = upward
    low = (gate * jax.nn.sigmoid(gate) * upward).astype(jnp.bfloat16)
    hidden[...] = low
    hidden_across[...] = low.T


def hidden_forward(second_all, gate_up_weight):
    length, depth = second_all.shape
    width = gate_up_weight.shape[1] // 2
    (gate_weight, up_weight), specs = column_halves(gate_up_weight)
    step = QUERY_ROWS
    return pl.pallas_call(
        hidden_body,
        grid=(length // step,),
        out_shape=(
            shape((length, 2 * width), jnp.float32),
            shape((length, width)),
            shape((depth, length)),
            shape((width, length)),
        ),
        in_specs=[pl.BlockSpec((step, depth), lambda i: (i, 0))] + list(specs),
        out_specs=(
            pl.BlockSpec((step, 2 * width), lambda i: (i, 0)),
            pl.BlockSpec((step, width), lambda i: (i, 0)),
            pl.BlockSpec((depth, step), lambda i: (0, i)),
            pl.BlockSpec((width, step), lambda i: (0, i)),
        ),
        compiler_params=pltpu.CompilerParams(vmem_limit_bytes=VMEM_MEGABYTES << 20),
        cost_estimate=pl.CostEstimate(
            flops=4 * length * depth * width, bytes_accessed=3 * 10**7, transcendentals=10**6
        ),
    )(second_all, gate_weight, up_weight)


def hidden_back_body(grad_rows, down_weight, gate_up, grad_gate_up):
    width = down_weight.shape[0]
    grad_hidden = times_transposed(grad_rows[...], down_weight[...])
    gate, upward = (gate_up[:, :width], gate_up[:, width:])
    sigmoid_gate = jax.nn.sigmoid(gate)
    silu_gate = gate * sigmoid_gate
    grad_gate = grad_hidden * upward * sigmoid_gate * (1.0 + gate * (1.0 - sigmoid_gate))
    grad_gate_up[:, :width] = grad_gate.astype(jnp.bfloat16)
    grad_gate_up[:, width:] = (grad_hidden * silu_gate).astype(jnp.bfloat16)


def hidden_backward(grad_out_all, down_weight, gate_up):
    length, depth = grad_out_all.shape
    width = down_weight.shape[0]
    step = QUERY_ROWS
    return pl.pallas_call(
        hidden_back_body,
        grid=(length // step,),
        out_shape=shape((length, 2 * width)),
        in_specs=[
            pl.BlockSpec((step, depth), lambda i: (i, 0)),
            pl.BlockSpec((width, depth), lambda i: (0, 0)),
            pl.BlockSpec((step, 2 * width), lambda i: (i, 0)),
        ],
        out_specs=pl.BlockSpec((step, 2 * width), lambda i: (i, 0)),
        compiler_params=pltpu.CompilerParams(vmem_limit_bytes=VMEM_MEGABYTES << 20),
        cost_estimate=pl.CostEstimate(
            flops=4 * length * depth * width, bytes_accessed=3 * 10**7, transcendentals=10**6
        ),
    )(grad_out_all, down_weight, gate_up)


def meet_twin(neighbours=False):
    me = lax.axis_index("fsdp")
    barrier = pltpu.get_barrier_semaphore()
    signal(barrier, fsdp=me + 1 - 2 * lax.rem(me, 2))
    if neighbours:
        _, across, along, _ = plane_places()
        signal(barrier, ctx=across)
        signal(barrier, ctx=along)
    pl.semaphore_wait(barrier, 3 if neighbours else 1)


def shard_rows(array, shards, core):
    span = array.shape[0] // shards
    starts = [pl.multiple_of((2 * i + core) * span, 16) for i in range(shards // 2)]
    return jnp.concatenate([array[pl.ds(start, span), :] for start in starts], axis=0)


GRAD_TILE = 256


class CoreSum:
    def __init__(self, send_buf, recv_buf, send_sem, recv_sem):
        self.send_buf, self.recv_buf = (send_buf, recv_buf)
        self.send_sem, self.recv_sem = (send_sem, recv_sem)

    def copy(self, tile):
        me = lax.axis_index("fsdp")
        columns = pl.ds(pl.multiple_of(tile * GRAD_TILE, GRAD_TILE), GRAD_TILE)
        return pltpu.make_async_remote_copy(
            src_ref=self.send_buf.at[:, columns],
            dst_ref=self.recv_buf.at[:, columns],
            send_sem=self.send_sem.at[tile],
            recv_sem=self.recv_sem.at[tile],
            device_id={"fsdp": me + 1 - 2 * lax.rem(me, 2)},
            device_id_type=MESH,
        )


def column_tile(tile):
    return pl.ds(pl.multiple_of(tile * GRAD_TILE, GRAD_TILE), GRAD_TILE)


def core_grads_body(shards, across, gradient, out, half, send_buf, recv_buf, send_sem, recv_sem):
    core = lax.rem(lax.axis_index("fsdp"), 2)
    tiles = gradient.shape[1] // GRAD_TILE
    sums = CoreSum(send_buf, recv_buf, send_sem, recv_sem)
    half[...] = shard_rows(across, shards, 1 - core)
    meet_twin()

    def send(tile, carry):
        columns = column_tile(tile)
        send_buf[:, columns] = product(half[...], gradient[:, columns]).astype(jnp.bfloat16)
        sums.copy(tile).start()
        return carry

    lax.fori_loop(0, tiles, send, 0)
    half[...] = shard_rows(across, shards, core)

    def keep(tile, carry):
        columns = column_tile(tile)
        value = product(half[...], gradient[:, columns])
        sums.copy(tile).wait()
        out[:, columns] = (value + recv_buf[:, columns].astype(jnp.float32)).astype(jnp.bfloat16)
        return carry

    lax.fori_loop(0, tiles, keep, 0)


def core_grads(shards, ident, source, gradient):
    depth, length = source.shape
    width = gradient.shape[1]
    tiles = width // GRAD_TILE
    return call_plane(
        functools.partial(core_grads_body, shards),
        ident,
        shape((depth // 2, width)),
        VMEM,
        [VMEM] * 2,
        [
            pltpu.VMEM((depth // 2, length), jnp.bfloat16),
            pltpu.VMEM((depth // 2, width), jnp.bfloat16),
            pltpu.VMEM((depth // 2, width), jnp.bfloat16),
            pltpu.SemaphoreType.DMA((tiles,)),
            pltpu.SemaphoreType.DMA((tiles,)),
        ],
        2 * length * depth * width,
        VMEM_MEGABYTES,
        (source, gradient),
    )


def hidden_grads_body(
    count, shards, across, grad_rows, gate_up, hidden, down_weight, gate_out, up_out, output,
    gradient_out, half, gradient, rows_buf, gate_up_buf, send_buf, recv_buf, send_sem, recv_sem,
    half_sem, block_sem, store_sem, *refs
):
    core = lax.rem(lax.axis_index("fsdp"), 2)
    greet(count, shards)
    scatter = Scatter(count, hidden, down_weight, False, refs)
    width = gate_out.shape[1]
    step = rows_buf.shape[1]
    blocks = gradient.shape[0] // step
    block_loads = {}
    stores = []

    def load_block(index):
        rows = pl.ds(index * step, step)
        pairs = ((grad_rows, rows_buf), (gate_up, gate_up_buf))
        block_loads[index] = [
            begin(source.at[rows], target.at[index % 2], block_sem.at[which, index])
            for which, (source, target) in enumerate(pairs)
        ]

    load_block(0)
    load_block(1)
    span = half.shape[1] // (shards // 2)
    half_loads = []
    for which in range(2):
        owner = (1 - core, core)[which]
        for chip in range(shards // 2):
            start = pl.multiple_of((2 * chip + owner) * span, 16)
            target = half.at[which, pl.ds(chip * span, span)]
            sem = half_sem.at[which, chip]
            half_loads.append(begin(across.at[pl.ds(start, span)], target, sem))
    sums = CoreSum(send_buf, recv_buf, send_sem, recv_sem)
    tiles = gradient.shape[1] // GRAD_TILE

    def back(index):
        for load in block_loads[index]:
            load.wait()
        rows = pl.ds(index * step, step)
        grad_hidden = times_transposed(rows_buf[index % 2], scatter.right_buf[...])
        gate = gate_up_buf[index % 2, :, :width]
        upward = gate_up_buf[index % 2, :, width:]
        sigmoid_gate = jax.nn.sigmoid(gate)
        silu_gate = gate * sigmoid_gate
        grad_gate = grad_hidden * upward * sigmoid_gate * (1.0 + gate * (1.0 - sigmoid_gate))
        gradient[rows, :width] = grad_gate.astype(jnp.bfloat16)
        gradient[rows, width:] = (grad_hidden * silu_gate).astype(jnp.bfloat16)
        stores.append(begin(gradient.at[rows], gradient_out.at[rows], store_sem.at[index]))
        if index + 2 < blocks:
            load_block(index + 2)

    def send(tile, carry):
        columns = column_tile(tile)
        value = product(half[0], gradient[:, columns])
        send_buf[:, columns] = value.astype(jnp.bfloat16)
        sums.copy(tile).start()
        return carry

    def keep(tile, carry):
        columns = column_tile(tile)
        value = product(half[1], gradient[:, columns])
        sums.copy(tile).wait()
        value = (value + recv_buf[:, columns].astype(jnp.float32)).astype(jnp.bfloat16)
        send_buf[:, columns] = value
        return carry

    def last_back():
        back(blocks - 1)
        for load in half_loads:
            load.wait()

    others = [functools.partial(back, index) for index in range(blocks - 1)] + [last_back]
    bounds = [0, 3, 6, 9, tiles]
    for body in (send, keep):
        for first, last in zip(bounds, bounds[1:]):
            others.append(lambda body=body, a=first, b=last: lax.fori_loop(a, b, body, 0))
    scatter.run(shards, others)
    for index, out in enumerate((gate_out, up_out)):
        source = send_buf.at[:, pl.ds(index * width, width)]
        stores.append(begin(source, out, store_sem.at[blocks + index]))
    scatter.finish()

    def strip(where):
        output[where, :] = received(count, scatter.recv_buf, scatter.total, where)

    for_strips(0, output.shape[0], strip)
    for store in stores:
        store.wait()


def hidden_grads(count, shards, ident, across, grad_rows, gate_up, hidden, down_weight):
    depth, length = across.shape
    width = gate_up.shape[1]
    tiles = width // GRAD_TILE
    rows = length // count
    step = QUERY_ROWS
    half = shape((depth // 2, width // 2))
    return call_plane(
        functools.partial(hidden_grads_body, count, shards),
        ident,
        (half, half, shape((rows, depth), jnp.float32), shape((length, width))),
        (HBM, HBM, VMEM, HBM),
        [HBM] * 5,
        [
            pltpu.VMEM((2, depth // 2, length), jnp.bfloat16),
            pltpu.VMEM((length, width), jnp.bfloat16),
            pltpu.VMEM((2, step, depth), jnp.bfloat16),
            pltpu.VMEM((2, step, width), jnp.float32),
            pltpu.VMEM((depth // 2, width), jnp.bfloat16),
            pltpu.VMEM((depth // 2, width), jnp.bfloat16),
            pltpu.SemaphoreType.DMA((tiles,)),
            pltpu.SemaphoreType.DMA((tiles,)),
            pltpu.SemaphoreType.DMA((2, shards // 2)),
            pltpu.SemaphoreType.DMA((2, length // step)),
            pltpu.SemaphoreType.DMA((length // step + 2,)),
        ]
        + scatter_scratch(count, rows, depth, hidden, down_weight, False, hidden.shape[1]),
        8 * 10**10,
        VMEM_MEGABYTES,
        (across, grad_rows, gate_up, hidden, down_weight),
    )


def attention_grads_body(
    shards, across, gradient, heads, branch_all, *refs
):
    near, out, far, refs = (refs[:4], refs[4], refs[5:9], refs[9:])
    half, outs, send_buf, recv_buf, send_sem, recv_sem, far_send, far_recv = refs
    core = lax.rem(lax.axis_index("fsdp"), 2)
    width = gradient.shape[1]
    tiles = width // GRAD_TILE
    total = out.shape[1] // GRAD_TILE
    part = out.shape[1] - width
    span = out.shape[0] // (shards // 2)
    height = HEAD_DIM
    sums = CoreSum(send_buf, recv_buf, send_sem, recv_sem)
    meet_twin(True)
    copies = []
    _, to_across, to_along, _ = plane_places()
    for index, target in enumerate(far):
        source = near[index]
        rows = source.shape[0] // 2
        half_rows = pl.ds(rows * (index % 2), rows)
        peer = (to_along, to_across)[index % 2]
        copies.append(
            remote(source.at[half_rows], target, far_send.at[index], far_recv.at[index], ctx=peer)
        )

    def heads_product(index, carry):
        columns = pl.ds(pl.multiple_of(index * 512, 512), 512)
        outs[:, columns] = product(heads[...], branch_all[:, columns])
        return carry

    lax.fori_loop(0, branch_all.shape[1] // 512, heads_product, 0)

    def pieces(side):
        for chip in range(shards // 2):
            rows = pl.ds(pl.multiple_of((2 * chip + side) * height, height), height)
            for index in range(span // height):
                start = chip * span + index * height
                yield slice(start, start + height), outs[rows, index * part : (index + 1) * part]

    for rows, value in pieces(1 - core):
        send_buf[rows, width:] = value.astype(jnp.bfloat16)
    for tile in range(tiles, total):
        sums.copy(tile).start()
    half[...] = shard_rows(across, shards, 1 - core)

    def send(tile, carry):
        columns = column_tile(tile)
        send_buf[:, columns] = product(half[...], gradient[:, columns]).astype(jnp.bfloat16)
        sums.copy(tile).start()
        return carry

    lax.fori_loop(0, tiles, send, 0)
    half[...] = shard_rows(across, shards, core)

    def keep(tile, carry):
        columns = column_tile(tile)
        value = product(half[...], gradient[:, columns])
        sums.copy(tile).wait()
        out[:, columns] = (value + recv_buf[:, columns].astype(jnp.float32)).astype(jnp.bfloat16)
        return carry

    lax.fori_loop(0, tiles, keep, 0)
    for tile in range(tiles, total):
        sums.copy(tile).wait()
    for rows, value in pieces(core):
        value = value + recv_buf[rows, width:].astype(jnp.float32)
        out[rows, width:] = value.astype(jnp.bfloat16)
    for copy in copies:
        copy.wait()


def attention_grads(shards, ident, first_across, grad_packed, heads_across, branch_all, *near):
    depth, length = first_across.shape
    heads = heads_across.shape[0]
    width = grad_packed.shape[1] + heads
    tiles = width // GRAD_TILE
    return call_plane(
        functools.partial(attention_grads_body, shards),
        ident,
        (shape((depth // 2, width)), *[shape((n.shape[0] // 2, n.shape[1])) for n in near]),
        (VMEM,) + (HBM,) * 4,
        [VMEM] * 4 + [HBM] * 4,
        [
            pltpu.VMEM((depth // 2, length), jnp.bfloat16),
            pltpu.VMEM((heads, branch_all.shape[1]), jnp.float32),
            pltpu.VMEM((depth // 2, width), jnp.bfloat16),
            pltpu.VMEM((depth // 2, width), jnp.bfloat16),
            pltpu.SemaphoreType.DMA((tiles,)),
            pltpu.SemaphoreType.DMA((tiles,)),
            pltpu.SemaphoreType.DMA((4,)),
            pltpu.SemaphoreType.DMA((4,)),
        ],
        2 * length * depth * width,
        VMEM_MEGABYTES,
        (first_across, grad_packed, heads_across, branch_all, *near),
    )


def sort_parts(parts, sorted_parts, corner_low):
    me, across, along, corner = plane_places()
    own, from_across, from_along, low, high = parts
    sorted_parts[me] = own[...]
    sorted_parts[across] = from_across[...]
    sorted_parts[along] = from_along[...]

    @pl.when(corner_low)
    def _():
        sorted_parts[corner] = low[...]

    @pl.when(jnp.logical_not(corner_low))
    def _():
        sorted_parts[corner] = high[...]


def interleaved(values, shards):
    span = values[0].shape[1] // shards
    return jnp.concatenate(
        [v[:, shard * span : (shard + 1) * span] for shard in range(shards) for v in values], axis=1
    )


def place_sorted_body(shards, *refs):
    *parts, target = refs
    target[...] = interleaved([part[...].astype(jnp.float32) for part in parts], shards)


def place_sorted(shards, array):
    rows, width = (array.shape[0] // 4, array.shape[1])
    step = 64
    steps = rows // step
    return pl.pallas_call(
        functools.partial(place_sorted_body, shards),
        grid=(steps,),
        out_shape=shape((rows, 4 * width), jnp.float32),
        in_specs=[
            pl.BlockSpec((step, width), lambda i, part=part: (part * steps + i, 0))
            for part in range(4)
        ],
        out_specs=pl.BlockSpec((step, 4 * width), lambda i: (i, 0)),
        cost_estimate=pl.CostEstimate(flops=0, bytes_accessed=10**7, transcendentals=0),
        compiler_params=pltpu.CompilerParams(vmem_limit_bytes=24 << 20),
    )(array, array, array, array)


def place_hidden_body(shards, *refs):
    parts, (target, sorted_parts) = (refs[:5], refs[5:])
    steps = pl.num_programs(0)
    sort_parts(parts, sorted_parts, pl.program_id(0) < steps // 2)
    values = [sorted_parts[part].astype(jnp.float32) for part in range(sorted_parts.shape[0])]
    target[...] = interleaved(values, shards)


def place_hidden(shards, parts):
    rows, width = parts[0].shape
    step = 64
    half = rows // step // 2
    whole = pl.BlockSpec((step, width), lambda i: (i, 0))
    low = pl.BlockSpec((step, width), lambda i: (jnp.minimum(i, half - 1), 0))
    high = pl.BlockSpec((step, width), lambda i: (jnp.maximum(i - half, 0), 0))
    return pl.pallas_call(
        functools.partial(place_hidden_body, shards),
        grid=(rows // step,),
        out_shape=shape((rows, 4 * width), jnp.float32),
        in_specs=[whole, whole, whole, low, high],
        out_specs=pl.BlockSpec((step, 4 * width), lambda i: (i, 0)),
        scratch_shapes=[pltpu.VMEM((4, step, width), jnp.bfloat16)],
        cost_estimate=pl.CostEstimate(flops=0, bytes_accessed=10**7, transcendentals=0),
        compiler_params=pltpu.CompilerParams(vmem_limit_bytes=24 << 20),
    )(*parts)


def place_rows_body(own, from_across, from_along, low, high, out):
    me, across, along, corner = plane_places()
    rows = own.shape[0]

    def put(owner, offset, ref):
        size = ref.shape[0]
        start = pl.multiple_of(owner * rows + offset, 8)
        out[pl.ds(start, size), :] = ref[...].astype(out.dtype)

    put(me, 0, own)
    put(across, 0, from_across)
    put(along, 0, from_along)
    put(corner, 0, low)
    put(corner, rows // 2, high)


def place_rows(parts, kind):
    rows, width = parts[0].shape
    return pl.pallas_call(
        place_rows_body,
        out_shape=shape((4 * rows, width), kind),
        in_specs=[VMEM] * 5,
        out_specs=VMEM,
        cost_estimate=pl.CostEstimate(flops=0, bytes_accessed=10**7, transcendentals=0),
        compiler_params=pltpu.CompilerParams(vmem_limit_bytes=24 << 20),
    )(*parts)


def place_attention_body(shards, own, from_across, from_along, low, high, query, key, value, output, sorted_parts):
    me, across, along, corner = plane_places()
    rows = own.shape[0]
    sorted_parts[me] = own[...]
    sorted_parts[across] = from_across[...]
    sorted_parts[along] = from_along[...]
    sorted_parts[corner, : rows // 2] = low[...]
    sorted_parts[corner, rows // 2 :] = high[...]
    count = sorted_parts.shape[0]
    width = query.shape[1] // count
    span = width // shards
    values = [sorted_parts[part, :, :width].astype(jnp.float32) for part in range(count)]
    query[...] = jnp.concatenate(
        [
            values[part][:, shard * span : (shard + 1) * span]
            for shard in range(shards)
            for part in range(count)
        ],
        axis=1,
    )
    sums = None
    for part in range(count):
        term = sorted_parts[part, :, width : width + 2 * KV_WIDTH].astype(jnp.float32)
        sums = term if sums is None else sums + term
    key[...] = sums[:, :KV_WIDTH]
    value[...] = sums[:, KV_WIDTH:]
    height = rows // count
    for part in range(count):
        for index in range(count):
            tile = sorted_parts[part, index * height : (index + 1) * height, width + 2 * KV_WIDTH :]
            output[part * height : (part + 1) * height, index * width : (index + 1) * width] = (
                tile.astype(jnp.float32)
            )


def place_attention(shards, parts):
    rows, width = parts[0].shape
    wide = shape((rows, D), jnp.float32)
    narrow = shape((rows, KV_WIDTH), jnp.float32)
    return pl.pallas_call(
        functools.partial(place_attention_body, shards),
        out_shape=(wide, narrow, narrow, wide),
        in_specs=[VMEM] * 5,
        out_specs=(VMEM,) * 4,
        scratch_shapes=[pltpu.VMEM((4, rows, width), jnp.bfloat16)],
        cost_estimate=pl.CostEstimate(flops=0, bytes_accessed=10**7, transcendentals=0),
        compiler_params=pltpu.CompilerParams(vmem_limit_bytes=24 << 20),
    )(*parts)


def low_lanes(dims, size):
    return lax.rem(lax.broadcasted_iota(jnp.int32, dims, len(dims) - 1), 2 * size) < size


def turn(values, cosine, sine):
    half = HEAD_DIM // 2
    swapped = jnp.where(
        low_lanes(values.shape, half),
        pltpu.roll(values, LANES - half, 1),
        pltpu.roll(values, half, 1),
    )
    return values * cosine + swapped * sine


def two_heads(values):
    low = low_lanes(values.shape, HEAD_DIM)
    zero = jnp.zeros_like(values)
    return jnp.concatenate([jnp.where(low, values, zero), jnp.where(low, zero, values)], axis=0)


def pick_heads(values):
    rows = values.shape[1] // PAIR
    return jnp.concatenate(
        [values[:HEAD_DIM, :rows], values[HEAD_DIM:, rows:]], axis=0
    )


def later_key(dims):
    key = lax.broadcasted_iota(jnp.int32, dims, 0)
    query = lax.rem(lax.broadcasted_iota(jnp.int32, dims, 1), QUERY_ROWS)
    return key > query


def block_rows_at(order, block, rows):
    return pl.ds(pl.multiple_of(order[block] * rows, rows), rows)


def rows_in_order(order, source, index, rows):
    per = QUERY_ROWS // rows
    return jnp.concatenate(
        [source[block_rows_at(order, index * per + i, rows), :] for i in range(per)], axis=0
    )


def slots(dealing, order):
    for slot in range(dealing.shape[1]):
        order[dealing[0, slot]] = slot


def unpack_output(weight, output_part):
    width = output_part.shape[0]
    if weight.shape[1] <= width + 2 * KV_WIDTH:
        return
    parts = output_part.shape[1] // width
    shards = width // HEAD_DIM
    for shard in range(shards):
        for part in range(parts):
            start = (shard * parts + part) * HEAD_DIM
            output_part[
                shard * HEAD_DIM : (shard + 1) * HEAD_DIM, part * width : (part + 1) * width
            ] = weight[start : start + HEAD_DIM, weight.shape[1] - width :]


def attend_body(
    block_rows,
    dealing,
    tokens_all,
    gain,
    weight,
    cosine,
    sine,
    attended,
    queries,
    keys,
    values,
    log_totals,
    first_across,
    heads_across,
    output_part,
    values_across,
    order,
):
    slots(dealing, order)
    unpack_output(weight, output_part)
    length, width = queries.shape
    kv_heads = keys.shape[0]
    pairs = width // LANES
    blocks = length // QUERY_ROWS

    def project(index, carry):
        place = pl.ds(pl.multiple_of(index * QUERY_ROWS, QUERY_ROWS), QUERY_ROWS)
        normed, _ = norm_parts(
            rows_in_order(order, tokens_all, index, block_rows).astype(jnp.float32)
        )
        rows = (normed * gain[...]).astype(jnp.bfloat16)
        turned_rows = rows.T
        for i in range(QUERY_ROWS // block_rows):
            first_across[
                :, block_rows_at(order, index * (QUERY_ROWS // block_rows) + i, block_rows)
            ] = turned_rows[:, i * block_rows : (i + 1) * block_rows]
        cos_rows, sin_rows = (cosine[place, :], sine[place, :])
        projected = product(rows, weight[:, :width])
        for pair in range(pairs):
            lanes = slice(pair * LANES, (pair + 1) * LANES)
            turned = turn(projected[:, lanes], cos_rows, sin_rows).astype(jnp.bfloat16)
            queries[place, lanes] = turned * jnp.asarray(1.0 / math.sqrt(HEAD_DIM), jnp.bfloat16)
        projected = product(rows, weight[:, width : width + 2 * kv_heads * HEAD_DIM])
        for head in range(2 * kv_heads):
            tile = projected[:, head // PAIR * LANES : (head // PAIR + 1) * LANES]
            if head < kv_heads:
                tile = turn(tile, cos_rows, sin_rows)
            low = low_lanes(tile.shape, HEAD_DIM)
            moved = pltpu.roll(tile, HEAD_DIM, 1)
            both = jnp.where(low, tile, moved) if head % PAIR == 0 else jnp.where(low, moved, tile)
            if head < kv_heads:
                keys[head, place, :] = both.astype(jnp.bfloat16)
            else:
                values[head - kv_heads, place, :] = both.astype(jnp.bfloat16)
                values_across[head - kv_heads, :, place] = both.T.astype(jnp.bfloat16)
        return carry

    lax.fori_loop(0, blocks, project, 0)

    def attend(pair, carry):
        kv_head = pair // (pairs // kv_heads)
        lanes = pl.ds(pl.multiple_of(pair * LANES, LANES), LANES)
        for index in range(blocks):
            seen = (index + 1) * QUERY_ROWS
            rows = two_heads(queries[index * QUERY_ROWS : seen, lanes])
            scores = times_transposed(keys[kv_head, :seen, :], rows)
            own = scores[seen - QUERY_ROWS :]
            own = jnp.where(later_key(own.shape), -1e30, own)
            if index:
                scores = jnp.concatenate([scores[: seen - QUERY_ROWS], own], axis=0)
            else:
                scores = own
            largest = jnp.max(scores, axis=0, keepdims=True)
            exponent = jnp.exp(scores - largest)
            totals = jnp.sum(exponent, axis=0, keepdims=True)
            mixed = product(values_across[kv_head, :, :seen], exponent.astype(jnp.bfloat16))
            log_totals[pl.ds(pair * blocks + index, 1), :] = largest + jnp.log(totals)
            across = pick_heads(mixed / totals).astype(jnp.bfloat16)
            for i in range(QUERY_ROWS // block_rows):
                heads_across[
                    lanes, block_rows_at(order, index * (QUERY_ROWS // block_rows) + i, block_rows)
                ] = across[:, i * block_rows : (i + 1) * block_rows]
            mixed = across.T
            per = QUERY_ROWS // block_rows
            for i in range(per):
                attended[block_rows_at(order, index * per + i, block_rows), lanes] = mixed[
                    i * block_rows : (i + 1) * block_rows
                ]
        return carry

    lax.fori_loop(0, pairs, attend, 0)


def attend_forward(block_rows, width, kv_heads, dealing, tokens_all, gain, weight, tables):
    length, _ = tokens_all.shape
    blocks = length // QUERY_ROWS
    wide = shape((kv_heads, length, LANES))
    return pl.pallas_call(
        functools.partial(attend_body, block_rows),
        out_shape=(
            shape((length, width)),
            shape((length, width)),
            wide,
            wide,
            shape((width // LANES * blocks, PAIR * QUERY_ROWS), jnp.float32),
            shape(tokens_all.shape[::-1]),
            shape((width, length)),
            shape((width, tokens_all.shape[1])),
        ),
        in_specs=[SMEM] + [VMEM] * 5,
        out_specs=(VMEM,) * 8,
        scratch_shapes=[
            pltpu.VMEM((kv_heads, LANES, length), jnp.bfloat16),
            pltpu.SMEM((length // block_rows,), jnp.int32),
        ],
        compiler_params=pltpu.CompilerParams(vmem_limit_bytes=VMEM_MEGABYTES << 20),
        cost_estimate=pl.CostEstimate(
            flops=3 * 10**10, bytes_accessed=10**7, transcendentals=10**7
        ),
    )(dealing, tokens_all, gain, weight, *tables)


def attend_back_body(
    block_rows,
    dealing,
    branch_all,
    output_weight,
    queries,
    keys,
    values,
    attended,
    log_totals,
    cosine,
    sine,
    grad_packed,
    grads,
    row_dots,
    keys_across,
    key_sums,
    value_sums,
    order,
):
    slots(dealing, order)
    length, width = queries.shape
    kv_heads = keys.shape[0]
    pairs = width // LANES
    blocks = length // QUERY_ROWS
    per = QUERY_ROWS // block_rows

    def project(index, carry):
        place = pl.ds(pl.multiple_of(index * QUERY_ROWS, QUERY_ROWS), QUERY_ROWS)
        rows = rows_in_order(order, branch_all, index, block_rows)
        low = times_transposed(rows, output_weight[...]).astype(jnp.bfloat16)
        grads[place, :] = low
        dots = low.astype(jnp.float32) * rows_in_order(order, attended, index, block_rows).astype(
            jnp.float32
        )
        for pair in range(pairs):
            across = dots[:, pair * LANES : (pair + 1) * LANES].T
            sums = [
                jnp.sum(across[i * HEAD_DIM : (i + 1) * HEAD_DIM], axis=0, keepdims=True)
                for i in range(PAIR)
            ]
            row_dots[pl.ds(pair * blocks + index, 1), :] = jnp.concatenate(sums, axis=1)
        for head in range(kv_heads):
            keys_across[head, :, place] = keys[head, place, :].T
        return carry

    lax.fori_loop(0, blocks, project, 0)

    group = pairs // kv_heads

    def attend(kv_head, carry):
        key_sums[kv_head] = jnp.zeros(key_sums.shape[1:], jnp.float32)
        value_sums[kv_head] = jnp.zeros(value_sums.shape[1:], jnp.float32)
        for member in range(group):
            pair = kv_head * group + member
            lanes = pl.ds(pl.multiple_of(pair * LANES, LANES), LANES)
            for index in range(blocks):
                seen = (index + 1) * QUERY_ROWS
                place = slice(index * QUERY_ROWS, seen)
                rows = two_heads(queries[place, lanes])
                grad_rows = two_heads(grads[place, lanes])
                row = pl.ds(pair * blocks + index, 1)
                scores = times_transposed(keys[kv_head, :seen, :], rows)
                weights = jnp.exp(scores - log_totals[row, :])
                own = weights[seen - QUERY_ROWS :]
                own = jnp.where(later_key(own.shape), 0.0, own)
                if index:
                    weights = jnp.concatenate([weights[: seen - QUERY_ROWS], own], axis=0)
                else:
                    weights = own
                grad_probs = times_transposed(values[kv_head, :seen, :], grad_rows)
                grad_scores = (weights * (grad_probs - row_dots[row, :])).astype(jnp.bfloat16)
                value_sums[kv_head, :seen, :] += product(weights.astype(jnp.bfloat16), grad_rows)
                key_sums[kv_head, :seen, :] += product(grad_scores, rows)
                turned = product(keys_across[kv_head, :, :seen], grad_scores)
                turned = pick_heads(turned).T * (1.0 / math.sqrt(HEAD_DIM))
                turned = turn(turned, cosine[place, :], -sine[place, :]).astype(jnp.bfloat16)
                for i in range(per):
                    grad_packed[block_rows_at(order, index * per + i, block_rows), lanes] = turned[
                        i * block_rows : (i + 1) * block_rows
                    ]
        return carry

    lax.fori_loop(0, kv_heads, attend, 0)

    def finish(block, carry):
        place = pl.ds(pl.multiple_of(block * block_rows, block_rows), block_rows)
        target = block_rows_at(order, block, block_rows)

        def head_sum(head):
            if head < kv_heads:
                tile = key_sums[head, place, :]
            else:
                tile = value_sums[head - kv_heads, place, :]
            tile = tile + pltpu.roll(tile, HEAD_DIM, 1)
            if head < kv_heads:
                tile = turn(tile, cosine[place, :], -sine[place, :])
            return tile

        for tile in range(2 * kv_heads // PAIR):
            first, second = (head_sum(tile * PAIR), head_sum(tile * PAIR + 1))
            joined = jnp.where(low_lanes(first.shape, HEAD_DIM), first, second)
            start = width + tile * LANES
            grad_packed[target, start : start + LANES] = joined.astype(jnp.bfloat16)
        return carry

    lax.fori_loop(0, length // block_rows, finish, 0)


def attend_backward(
    block_rows, dealing, branch_all, output_weight, queries, keys, values, attended, log_totals, tables
):
    length, width = queries.shape
    kv_heads = keys.shape[0]
    return pl.pallas_call(
        functools.partial(attend_back_body, block_rows),
        out_shape=shape((length, width + 2 * kv_heads * HEAD_DIM)),
        in_specs=[SMEM] + [VMEM] * 9,
        out_specs=VMEM,
        scratch_shapes=[
            pltpu.VMEM((length, width), jnp.bfloat16),
            pltpu.VMEM(log_totals.shape, jnp.float32),
            pltpu.VMEM((kv_heads, LANES, length), jnp.bfloat16),
            pltpu.VMEM((kv_heads, length, LANES), jnp.float32),
            pltpu.VMEM((kv_heads, length, LANES), jnp.float32),
            pltpu.SMEM((length // block_rows,), jnp.int32),
        ],
        compiler_params=pltpu.CompilerParams(vmem_limit_bytes=VMEM_MEGABYTES << 20),
        cost_estimate=pl.CostEstimate(
            flops=6 * 10**10, bytes_accessed=10**7, transcendentals=10**7
        ),
    )(
        dealing,
        branch_all,
        output_weight,
        queries,
        keys,
        values,
        attended,
        log_totals,
        *tables,
    )


def take_columns(matrix, outer, parts, index):
    rows, columns = matrix.shape
    pieces = matrix.reshape(rows, outer, parts, columns // (outer * parts))
    return lax.dynamic_index_in_dim(pieces, index, axis=2, keepdims=False).reshape(rows, -1)


def take_rows(matrix, parts, index):
    count = matrix.shape[0] // parts
    return lax.dynamic_slice_in_dim(matrix, index * count, count, axis=0)


def put_columns(gathered, outer):
    parts, rows, columns = gathered.shape
    return (
        gathered.reshape(parts, rows, outer, columns // outer)
        .transpose(1, 2, 0, 3)
        .reshape(rows, parts * columns)
    )


def gather_shards(array):
    return lax.all_gather(array, "fsdp", axis=0, tiled=True)


def scatter_shards(array, by_core=False):
    shards = lax.axis_size("fsdp")
    groups = [list(range(core, shards, 2)) for core in range(2)] if by_core else None
    return lax.psum_scatter(
        array.astype(jnp.bfloat16),
        "fsdp",
        scatter_dimension=0,
        tiled=True,
        axis_index_groups=groups,
    )


def per_device(
    tokens,
    dealing,
    first_gain,
    query_weight,
    key_weight,
    value_weight,
    output_weight,
    second_gain,
    gate_weight,
    up_weight,
    down_weight,
    cotangent,
):
    shard_count = lax.axis_size("fsdp")
    part_count = lax.axis_size("ctx")
    ctx_index = lax.axis_index("ctx")
    row_count = tokens.shape[1]
    block_rows = row_count // 2
    seq_rows = row_count * part_count
    part_width = D // part_count
    dealt_heads = D // shard_count // part_count == HEAD_DIM and part_count == 4
    kv_heads = KV_HEADS if dealt_heads else max(1, KV_HEADS // part_count)
    kv_first = 0 if dealt_heads else ctx_index * KV_HEADS // part_count
    tie = lax.optimization_barrier
    start = functools.partial(
        start_gather, part_count, shard_count, 1, tokens[0], first_gain, second_gain
    )
    if dealt_heads:
        tokens_all, gain_first, gain_second, cosine, sine, packed, packed_hidden = start(
            query_weight, key_weight, value_weight, output_weight, gate_weight, up_weight
        )
        packed, packed_hidden = tie((packed, packed_hidden))
        gate_up_part = gather_shards(packed_hidden)
    else:
        tokens_all, gain_first, gain_second, cosine, sine = start()
        grad_out_all = lax.all_gather(cotangent[0], "ctx", axis=0, tiled=True)
        query_part = gather_shards(take_columns(query_weight, 1, part_count, ctx_index))
        output_part = take_rows(gather_shards(output_weight), part_count, ctx_index)
        key_value = gather_shards(jnp.concatenate([key_weight, value_weight], axis=1))
        key_value = key_value.reshape(D, 2, KV_HEADS, HEAD_DIM)
        key_value = lax.dynamic_slice_in_dim(key_value, kv_first, kv_heads, 2).reshape(D, -1)
        packed = jnp.concatenate([query_part, key_value], axis=1)
        gate_up_part = gather_shards(
            jnp.concatenate(
                [
                    take_columns(gate_weight, shard_count, part_count, ctx_index),
                    take_columns(up_weight, shard_count, part_count, ctx_index),
                ],
                axis=1,
            )
        )
    tables = (cosine, sine)
    down_part = gather_shards(take_rows(down_weight, part_count, ctx_index))

    forward = attend_forward(
        block_rows, part_width, kv_heads, dealing, tokens_all, gain_first, packed, tables
    )
    attended, query_rot, key_rot, value_rows, log_totals, first_across, heads_across = forward[:7]
    if dealt_heads:
        output_part = forward[7]
    residual_mid, second_all = middle_gather(
        part_count, 2, attended, output_part, tokens[0], gain_second
    )
    if dealt_heads:
        second_all, grad_out = tie((second_all, cotangent[0]))
        near = plane_near(grad_out)

    gate_up, hidden, second_across, hidden_across = hidden_forward(second_all, gate_up_part)
    if dealt_heads:
        hidden_across, *near = tie((hidden_across, *near))
        grad_out_all = place_rows(plane_far(near), jnp.bfloat16)
        down_term = core_grads(shard_count, 5, hidden_across, grad_out_all)
    else:
        down_term = column_term(hidden, grad_out_all)
    down_part, down_term = tie((down_part, down_term))
    down_piece = scatter_shards(down_term, dealt_heads)
    if dealt_heads:
        *terms, output_sum, grad_gate_up = hidden_grads(
            part_count, shard_count, 6, second_across, grad_out_all, gate_up, hidden, down_part
        )
    else:
        grad_gate_up = hidden_backward(grad_out_all, down_part, gate_up)
        gate_up_term = column_term(second_all, grad_gate_up).astype(jnp.bfloat16)
        terms = (gate_up_term[:, : FF // part_count], gate_up_term[:, FF // part_count :])
        output_partial = product(hidden, down_part).astype(jnp.bfloat16)
        output_sum = lax.psum_scatter(output_partial, "ctx", scatter_dimension=0, tiled=True)
    block_output = (residual_mid + output_sum.astype(jnp.float32)).astype(jnp.bfloat16)
    grad_gate_up, *terms = tie((grad_gate_up, *terms))
    gate_piece = scatter_shards(terms[0], dealt_heads)
    up_piece = scatter_shards(terms[1], dealt_heads)
    grad_mid, second_gain_part, branch_all = middle_back(
        part_count, 3, grad_gate_up, gate_up_part, residual_mid, gain_second, cotangent[0]
    )
    branch_all, down_piece = tie((branch_all, down_piece))
    branch_all, gate_piece = tie((branch_all, gate_piece))
    if dealt_heads:
        down_near = plane_near(down_piece)
        gate_near = plane_near(gate_piece)

    grad_packed = attend_backward(
        block_rows,
        dealing,
        branch_all,
        output_part,
        query_rot,
        key_rot,
        value_rows,
        attended,
        log_totals,
        tables,
    )
    if dealt_heads:
        packed_term, *far = attention_grads(
            shard_count,
            7,
            first_across,
            grad_packed,
            heads_across,
            branch_all,
            *down_near[1:],
            *gate_near[1:],
        )
        down_parts, gate_parts = ((*down_near, *far[:2]), (*gate_near, *far[2:]))
        grad_packed, packed_term = tie((grad_packed, packed_term))
        packed_piece = scatter_shards(packed_term, True)
    grad_norm, gain_shard, up_all = input_back(
        part_count,
        shard_count,
        4,
        grad_packed,
        packed,
        tokens[0],
        gain_first,
        second_gain_part,
        up_piece,
    )
    if dealt_heads:
        grad_norm, packed_piece = tie((grad_norm, packed_piece))
        packed_near = plane_near(packed_piece)
        gate_shard = place_hidden(shard_count, gate_parts)
        up_shard = place_sorted(shard_count, up_all)
        down_shard = place_rows(down_parts, jnp.float32)
        gate_shard, up_shard, *packed_near = tie((gate_shard, up_shard, *packed_near))
        query_shard, key_shard, value_shard, output_shard = place_attention(
            shard_count, plane_far(packed_near)
        )
    else:

        def gather_columns(piece, outer):
            return put_columns(lax.all_gather(piece, "ctx", axis=0), outer).astype(jnp.float32)

        gate_shard = gather_columns(gate_piece, shard_count)
        up_shard = put_columns(
            up_all.reshape(part_count, -1, FF // part_count), shard_count
        ).astype(jnp.float32)
        down_shard = lax.all_gather(down_piece, "ctx", axis=0, tiled=True).astype(jnp.float32)
        grad_query, grad_key_value = (grad_packed[:, :part_width], grad_packed[:, part_width:])
        query_piece = scatter_shards(product(first_across, grad_query))
        query_shard = gather_columns(query_piece, 1)
        key_value_piece = scatter_shards(product(first_across, grad_key_value))
        output_term = column_term(attended, branch_all)
        spread = jnp.zeros((D, D), jnp.float32)
        spread = lax.dynamic_update_slice_in_dim(
            spread, output_term, ctx_index * output_term.shape[0], 0
        )
        output_shard = lax.psum(scatter_shards(spread), "ctx").astype(jnp.float32)
        wide = jnp.zeros((D // shard_count, 2, KV_HEADS, HEAD_DIM), jnp.bfloat16)
        wide = lax.dynamic_update_slice_in_dim(
            wide, key_value_piece.reshape(-1, 2, kv_heads, HEAD_DIM), kv_first, 2
        )
        key_value_shard = lax.psum(wide.reshape(-1, 2 * KV_WIDTH), "ctx").astype(jnp.float32)
        key_shard, value_shard = (key_value_shard[:, :KV_WIDTH], key_value_shard[:, KV_WIDTH:])
    return (
        block_output[None],
        (grad_mid + grad_norm).astype(jnp.bfloat16)[None],
        gain_shard[0],
        query_shard,
        key_shard,
        value_shard,
        output_shard,
        gain_shard[1],
        gate_shard,
        up_shard,
        down_shard,
    )


def solution(mesh):
    in_specs = (
        P("fsdp", "ctx", None),
        P("fsdp", None),
        P("fsdp"),
        P("fsdp", None),
        P("fsdp", None),
        P("fsdp", None),
        P("fsdp", None),
        P("fsdp"),
        P("fsdp", None),
        P("fsdp", None),
        P("fsdp", None),
        P("fsdp", "ctx", None),
    )
    out_specs = (
        P("fsdp", "ctx", None),
        P("fsdp", "ctx", None),
        P("fsdp"),
        P("fsdp", None),
        P("fsdp", None),
        P("fsdp", None),
        P("fsdp", None),
        P("fsdp"),
        P("fsdp", None),
        P("fsdp", None),
        P("fsdp", None),
    )
    return jax.shard_map(
        per_device, mesh=mesh, in_specs=in_specs, out_specs=out_specs, check_vma=False
    )
```
